32 devices in a mesh: grp: 2 (over y), gx: 4 (over x, core), gy: 4 (over z).
Axes of the slice: x: 2, y: 2, z: 4, core: 2. Of those that a mesh axis runs over, the one named last changes fastest.
Arguments:
- ensemble: float32 [128, 3, 32, 1024], P('grp', None, 'gx', 'gy'), parts along dimension 0, may hold values from -16 to 16
- diffusivity: float32 [6, 32, 1024], P('grp', 'gx', 'gy'), parts along dimension 0, may hold values from 0.03 to 0.24
- mixing: float32 [3, 3], replicated, may hold values from -0.6 to 0.6
- obs_cell: int32 [4, 4, 4096], P('gx', 'gy', 'grp'), parts along dimension 2, may hold values from 0 to 2047
- obs_var: int32 [4, 4, 4096], P('gx', 'gy', 'grp'), parts along dimension 2, may hold values from 0 to 2
- obs_value: float32 [4, 4, 4096], P('gx', 'gy', 'grp'), parts along dimension 2, may hold values from -5 to 5
- obs_weight: float32 [4, 4, 4096], P('gx', 'gy', 'grp'), parts along dimension 2, may hold values from 0.5 to 6
Outputs:
- analysis: float32 [128, 3, 32, 1024], P('grp', None, 'gx', 'gy'), parts along dimension 0
The draws below stay inside these ranges and needn't reach their ends.
There are 2 independent parts, one for each index of `grp`. The reference program is written for one: setup_inputs(seed, part) draws one part's arguments, and reference() takes and returns one part's arrays. A program takes and returns all parts, laid end to end along the dimension named above; an argument that names none is the same for every part. Nothing has to cross between parts.
All inputs are finite; a program needn't handle non-finite values.
Results may differ from the reference program's by a relative error of at most 0.0001.
Values sent between devices are 32-bit elements; how exact they have to be, the bound alone decides.
No kernel may reach another device: no remote copies, remote signals or barrier semaphores. Data moves between devices by JAX's collectives and lax.ppermute only.
A program may use at most 64 MiB of HBM per device.

```python
import math
import jax
import jax.numpy as jnp
from jax import lax

K = 64
NVAR = 3
CX = 8
CY = 256
OBS_DEV = 2048
NS_ITERS = 5
TILES_X = 4
TILES_Y = 4
NX = 32
NY = 1024
OBS_ALL = 32768


def draw_ensemble(key, part):
    key_base = jax.random.fold_in(key, 11)
    key_pattern = jax.random.fold_in(key, 12)
    key_coef = jax.random.fold_in(key, 13)
    shape = (K, NVAR, NX, NY)
    base = jnp.clip(jax.random.normal(key_base, shape, jnp.float32), -4.0, 4.0)
    patterns = jnp.clip(jax.random.normal(key_pattern, (4, NVAR, NX, NY), jnp.float32), -3.0, 3.0)
    coefs = jax.random.uniform(key_coef, (4, K), jnp.float32, -1.0, 1.0)
    for mode in range(4):
        base = base + coefs[mode][:, None, None, None] * patterns[mode][None]
    return base


def draw_obs_weight(key, part):
    key_level = jax.random.fold_in(key, 21)
    tile_number = (jnp.arange(TILES_X)[:, None] * TILES_Y + jnp.arange(TILES_Y)[None, :]).astype(jnp.float32)
    rising = 1.0 + 2.0 * tile_number / float(TILES_X * TILES_Y - 1)
    shape = (TILES_X, TILES_Y, OBS_DEV)
    level = jnp.exp(jax.random.uniform(key_level, shape, jnp.float32, jnp.log(0.5), jnp.log(2.0)))
    return level * jnp.sqrt(rising)[:, :, None]


def place_ends(result, stream_key, least, largest):
    index_at = [jax.random.randint(jax.random.fold_in(stream_key, axis), (), 0, length) for axis, length in enumerate(result.shape)]
    main_axis = result.shape.index(max(result.shape))
    next_to = index_at[:main_axis] + [(index_at[main_axis] + 1) % result.shape[main_axis]] + index_at[main_axis + 1:]
    return result.at[tuple(index_at)].set(least).at[tuple(next_to)].set(largest)


def block_levels(stream_key, shape, pieces, low, largest):
    def one(position, parts):
        heights = jax.random.uniform(jax.random.fold_in(jax.random.fold_in(stream_key, 6), position), (parts,), jnp.float32, low / len(pieces), largest / len(pieces))
        return jnp.repeat(jnp.exp(heights), shape[position] // parts).reshape((-1,) + (1,) * (len(shape) - position - 1))

    factor_of = one(*pieces[0])
    for cut in pieces[1:]:
        factor_of = factor_of * one(*cut)
    return factor_of


def scatter_about(stream_key, dims, width, bound, pieces=(), kind=jnp.bfloat16):
    entries = width * jax.random.normal(stream_key, dims, jnp.float32)
    if pieces:
        entries = entries * block_levels(stream_key, dims, pieces, -0.22, 0.18)
    return jnp.clip(entries, -bound, bound).astype(kind)


def setup_inputs(seed: int = 0, part: int = 0) -> dict:
    key_list = jax.random.split(jax.random.key(seed), 8)
    part_splits = jax.random.split(jax.random.fold_in(key_list[7], part), 8)
    ensemble = draw_ensemble(jax.random.fold_in(jax.random.fold_in(key_list[7], part), 71), part)
    diffusivity = jnp.clip(jnp.exp(math.log(0.24) - 2.0794415 * jax.random.uniform(part_splits[1], (NVAR, NX, NY), jnp.float32) ** block_levels(part_splits[1], (NVAR, NX, NY), ((1, 4), (2, 4)), -0.2, 0.2)), 0.03, 0.24)
    mixing = scatter_about(key_list[2], (NVAR, NVAR), 0.15, 0.6, (), jnp.float32)
    obs_cell = place_ends(jax.random.randint(part_splits[3], (TILES_X, TILES_Y, OBS_DEV), 0, CX * CY), jax.random.fold_in(part_splits[3], 1), 0, (CX * CY) - 1).astype(jnp.int32)
    obs_var = place_ends(jax.random.randint(part_splits[4], (TILES_X, TILES_Y, OBS_DEV), 0, 3), jax.random.fold_in(part_splits[4], 1), 0, 2).astype(jnp.int32)
    obs_value = scatter_about(part_splits[5], (TILES_X, TILES_Y, OBS_DEV), 1.0, 5.0, ((0, 4), (1, 4)), jnp.float32)
    obs_weight = draw_obs_weight(jax.random.fold_in(jax.random.fold_in(key_list[7], part), 71), part)
    return dict(ensemble=ensemble, diffusivity=diffusivity, mixing=mixing, obs_cell=obs_cell, obs_var=obs_var, obs_value=obs_value, obs_weight=obs_weight)


def advance(padded, kappa_field, mixing):
    center = padded[:, :, 1:-1, 1:-1]
    beside = padded[:, :, 2:, 1:-1] + padded[:, :, :-2, 1:-1]
    beside = beside + padded[:, :, 1:-1, 2:] + padded[:, :, 1:-1, :-2]
    coupled = jnp.zeros_like(center)
    for source in range(3):
        coupled = coupled + mixing[:, source][None, :, None, None] * center[:, source][:, None]
    return center + kappa_field[None] * (beside - 4.0 * center) + coupled

def pad_zero(state):
    return jnp.pad(state, ((0, 0), (0, 0), (1, 1), (1, 1)))

def transform(gram, pull):
    identity = jnp.eye(gram.shape[0], dtype=jnp.float32)
    matrix = identity + gram
    frob_norm = jnp.sqrt(jnp.sum(matrix * matrix))

    def ns_step(step, carry):
        sqrt_iter, inv_iter = carry
        correction = 1.5 * identity - 0.5 * jnp.dot(inv_iter, sqrt_iter, precision=lax.Precision.HIGHEST)
        return (jnp.dot(sqrt_iter, correction, precision=lax.Precision.HIGHEST), jnp.dot(correction, inv_iter, precision=lax.Precision.HIGHEST))
    sqrt_iter, inv_iter = lax.fori_loop(0, NS_ITERS, ns_step, (matrix / frob_norm, identity))
    root_inv = inv_iter / jnp.sqrt(frob_norm)
    inverse = jnp.dot(root_inv, root_inv, precision=lax.Precision.HIGHEST)
    mean_shift = jnp.dot(inverse, pull, precision=lax.Precision.HIGHEST)
    return mean_shift[:, None] + root_inv

def reference(ensemble, diffusivity, mixing, obs_cell, obs_var, obs_value, obs_weight):
    members = ensemble.shape[0]
    first_state = advance(pad_zero(ensemble), diffusivity, mixing)
    second_state = advance(pad_zero(first_state), diffusivity, mixing)
    row_index = (jnp.arange(TILES_X, dtype=jnp.int32)[:, None, None] * CX + obs_cell // CY).astype(jnp.int32)
    col_index = (jnp.arange(TILES_Y, dtype=jnp.int32)[None, :, None] * CY + obs_cell % CY).astype(jnp.int32)
    observed = second_state[:, obs_var, row_index, col_index].reshape(members, -1)
    obs_mean = lax.optimization_barrier(jnp.mean(observed, axis=0))
    factor = 1.0 / math.sqrt((members - 1) * OBS_ALL)
    weight = obs_weight.reshape(-1)
    spread = (observed - obs_mean) * (weight * factor)
    departure = weight * (obs_value.reshape(-1) - obs_mean)
    gram = jnp.dot(spread, spread.T, precision=lax.Precision.HIGHEST)
    pull = jnp.dot(spread, departure, precision=lax.Precision.HIGHEST)
    weights = transform(gram, pull)
    state_mean = lax.optimization_barrier(jnp.mean(second_state, axis=0))
    anomalies = (second_state - state_mean).reshape(members, -1)
    moved = jnp.dot(weights.T, anomalies, precision=lax.Precision.HIGHEST)
    return state_mean + moved.reshape(second_state.shape)
```

```python
import functools
import math

import jax
import jax.numpy as jnp
from jax import lax
from jax.experimental import pallas as pl
from jax.experimental.pallas import tpu as pltpu
from jax.sharding import PartitionSpec as P

NS_ITERS = 5
LANES = 128
HIGHEST = lax.Precision.HIGHEST
F32 = jnp.float32
BF16 = jnp.bfloat16


def vmem():
    return pl.BlockSpec(memory_space=pltpu.VMEM)


def smem():
    return pl.BlockSpec(memory_space=pltpu.SMEM)


def nt(a, b):
    return lax.dot_general(a, b, (((1,), (1,)), ((), ())), preferred_element_type=F32)


def split_2(x):
    high = x.astype(BF16)
    return high, (x - high.astype(F32)).astype(BF16)


def split_3(x):
    high = x.astype(BF16)
    rest = x - high.astype(F32)
    middle = rest.astype(BF16)
    return high, middle, (rest - middle.astype(F32)).astype(BF16)


def pair_swap(partner, sizes):
    grp, nx, ny = sizes
    pairs = []
    for g in range(grp):
        for x in range(nx):
            for y in range(ny):
                there = partner(g, x, y)
                if there is not None:
                    tg, tx, ty = there
                    pairs.append(((g * nx + x) * ny + y, (tg * nx + tx) * ny + ty))
    return lambda value: lax.ppermute(value, ("grp", "gx", "gy"), pairs)


def along(place, count, phase):
    first = place - (place - phase) % 2
    if first < 0 or first + 1 >= count:
        return None
    return first + 1 if place == first else first


def x_swap(phase, sizes):
    def partner(g, x, y):
        there = along(x, sizes[1], phase)
        if there is not None:
            return g, there, y
        return (g ^ 1, x, y) if sizes[0] % 2 == 0 else None

    return pair_swap(partner, sizes)


def y_swap(phase, sizes):
    def partner(g, x, y):
        there = along(y, sizes[2], phase)
        if there is not None:
            return g, x, there
        return (g, x ^ 1, y) if sizes[1] % 2 == 0 else None

    return pair_swap(partner, sizes)


def all_sum(value, sizes):
    grp, nx, ny = sizes
    if nx & (nx - 1) or ny & (ny - 1) or nx < 2:
        return lax.psum(value, ("gx", "gy"))

    def chip_swap(mask_0, mask_1):
        def partner(g, x, y):
            chip = ((x >> 1) * ny + y) ^ (mask_1 if x & 1 else mask_0)
            return g, ((chip // ny) << 1) | (x & 1), chip % ny

        return pair_swap(partner, sizes)

    core_swap = pair_swap(lambda g, x, y: (g, x ^ 1, y), sizes)
    chips = nx // 2 * ny
    value = value + core_swap(value)
    if chips == 8:
        parts = [chip_swap(a, b)(value) for a, b in ((4, 4), (1, 5), (2, 6), (3, 7))]
        core_1 = lax.axis_index("gx") % 2 == 1
        own = jnp.where(core_1, 0.0, value + parts[0])
        value = own + parts[1] + parts[2] + parts[3]
        return value + core_swap(value)
    step = 1
    while step < chips:
        value = value + chip_swap(step, step)(value)
        step *= 2
    return value


def load_kernel(dims, ens, kappa, state, send_a, send_b, sides, buf, sems):
    k, nv, cx, cy = dims
    rows = nv * cx
    chunks = 4
    part = k // chunks
    copies = []
    half = cy // LANES
    for c in range(chunks):
        span = pl.ds(c * part * rows, part * rows)
        for h in range(half):
            lanes = slice(h * LANES, (h + 1) * LANES)
            copies.append(pltpu.make_async_copy(ens.at[span, lanes], buf.at[h, span], sems.at[c, h]))
            copies[-1].start()
    for c in range(chunks):
        for h in range(half):
            copies[c * half + h].wait()
            for r in range(cx):
                for v in range(nv):
                    value = buf[h, pl.ds(c * part * rows + v * cx + r, part, stride=rows), :]
                    at = pl.ds(((r + 2) * nv + v) * k + c * part, part)
                    state[at, h * LANES : (h + 1) * LANES] = value
    block = nv * k
    even_x = lax.axis_index("gx") % 2 == 0
    top = 2 * block
    bottom = (cx + 1) * block
    for ref, near_top in ((send_a, jnp.logical_not(even_x)), (send_b, even_x)):
        near = jnp.where(near_top, top, bottom)
        second = jnp.where(near_top, top + block, bottom - block)
        for j in range(0, block, 64):
            ref[pl.ds(j, 64), :] = state[pl.ds(pl.multiple_of(near + j, 64), 64), :]
            ref[pl.ds(block + j, 64), :] = state[pl.ds(pl.multiple_of(second + j, 64), 64), :]
        for v in range(nv):
            edge = jnp.where(near_top, kappa[v, 0:1, :], kappa[v, cx - 1 : cx, :])
            ref[pl.ds(2 * block + v, 1), :] = edge
        ref[pl.ds(2 * block + nv, 8 - nv), :] = jnp.zeros((8 - nv, cy), F32)

    lane = lax.broadcasted_iota(jnp.int32, (1, LANES), 1)
    total = jnp.zeros((k, LANES), F32)
    total_k = jnp.zeros((8, LANES), F32)
    for r in range(cx):
        for v in range(nv):
            place = 2 * (nv * (r + 1) + v)
            base = ((r + 2) * nv + v) * k
            low = (lane >= place) & (lane < place + 2)
            high = (lane >= 64 + place) & (lane < 64 + place + 2)

            def add(acc, right, left):
                acc = jnp.where(low, pltpu.roll(right, (place + 2) % LANES, 1), acc)
                return jnp.where(high, pltpu.roll(left, 64 + place, 1), acc)

            total = add(total, state[pl.ds(base, k), cy - LANES :], state[pl.ds(base, k), :LANES])
            row = kappa[v, r : r + 1, :]
            total_k = add(
                total_k,
                jnp.broadcast_to(row[:, cy - LANES :], (8, LANES)),
                jnp.broadcast_to(row[:, :LANES], (8, LANES)),
            )
    sides[0:k, :] = total
    sides[k : k + 8, :] = total_k


def scatter_kernel(dims, cell, var, value, weight, out):
    k, nv, cx, cy = dims
    count = cell.shape[1]
    row = cell[...] // cy * nv + var[...]
    column = cell[...] % cy
    square = weight[...] * weight[...]
    rows = 32
    hit = lax.broadcasted_iota(jnp.int32, (rows, count), 0) == row
    parts = split_3(square) + split_3(square * value[...])
    left = [jnp.where(hit, p.astype(F32), 0.0).astype(BF16) for p in parts]
    one = (lax.broadcasted_iota(jnp.int32, (cy, count), 0) == column).astype(F32).astype(BF16)
    got = nt(jnp.concatenate(left, axis=0), one)
    piece = [got[i * rows : (i + 1) * rows] for i in range(6)]
    out[0:rows, :] = piece[0] + piece[1] + piece[2]
    out[rows : 2 * rows, :] = piece[3] + piece[4] + piece[5]


def forecast_kernel(
    dims, factor, mixing, state_in, recv_a, recv_b, sides, halo, corner_a, corner_b, kappa, cells,
    state, anomalies, means, gram, first, kext, spread, moved,
):
    k, nv, cx, cy = dims
    block = nv * k
    gx = lax.axis_index("gx")
    nx = lax.axis_size("gx")
    even_x = gx % 2 == 0
    has_up = gx > 0
    has_down = gx < nx - 1
    up_is_a = jnp.logical_not(even_x)

    def pick(ref_is_a, has, a, b):
        return jnp.where(has, jnp.where(ref_is_a, a, b), 0.0)

    for j in range(0, 2 * block, 64):
        a = recv_a[pl.ds(j, 64), :]
        b = recv_b[pl.ds(j, 64), :]
        up_at = (block if j < block else -block) + j
        state[pl.ds(up_at, 64), :] = pick(up_is_a, has_up, a, b)
        state[pl.ds((cx + 2) * block + j, 64), :] = pick(even_x, has_down, a, b)
    for v in range(nv):
        a = recv_a[pl.ds(2 * block + v, 1), :]
        b = recv_b[pl.ds(2 * block + v, 1), :]
        kext[pl.ds(v, 1), :] = pick(up_is_a, has_up, a, b)
        kext[pl.ds((cx + 1) * 8 + v, 1), :] = pick(even_x, has_down, a, b)
        for r in range(cx):
            kext[pl.ds((r + 1) * 8 + v, 1), :] = kappa[v, r : r + 1, :]
            spread[pl.ds(r * 8 + v, 1), :] = cells[pl.ds(r * nv + v, 1), :]
            spread[pl.ds(r * 8 + nv + v, 1), :] = cells[pl.ds(32 + r * nv + v, 1), :]

    lane = lax.broadcasted_iota(jnp.int32, (1, LANES), 1)
    slot = lane % 64
    inside = (slot >= 2 * nv) & (slot < 2 * nv * (cx + 1))
    up_corner = pick(up_is_a, has_up, corner_a[...], corner_b[...])
    down_corner = pick(even_x, has_down, corner_a[...], corner_b[...])
    far = 2 * nv * cx
    columns = jnp.where(slot < 2 * nv, pltpu.roll(up_corner, LANES - far, 1), halo[...])
    columns = jnp.where(
        (slot >= 2 * nv * (cx + 1)) & (slot < 2 * nv * (cx + 2)), pltpu.roll(down_corner, far, 1), columns
    )
    kcol = columns[k : k + 1, :]
    columns = columns[0:k, :]

    own = sides[0:k, :]
    beside = jnp.where(
        lane < 64,
        pltpu.roll(columns, 1, 1) + pltpu.roll(own, 65, 1),
        pltpu.roll(columns, LANES - 1, 1) + pltpu.roll(own, 63, 1),
    )
    step = 2 * nv
    beside = beside + pltpu.roll(columns, step, 1) + pltpu.roll(columns, LANES - step, 1)
    which = slot // 2 % nv
    mixed = jnp.zeros((k, LANES), F32)
    for shift in range(1 - nv, nv):
        coef = jnp.zeros((1, LANES), F32)
        for v in range(nv):
            if 0 <= v + shift < nv:
                coef = jnp.where(which == v, mixing[v, v + shift], coef)
        source = pltpu.roll(columns, (-2 * shift) % LANES, 1) if shift else columns
        mixed = mixed + coef * source
    first_columns = jnp.where(inside, columns + kcol * (beside - 4.0 * columns) + mixed, 0.0)

    half = cy // LANES

    def advance(source, side, r, store):
        eight = pl.ds(pl.multiple_of(r * 8, 8), 8)
        kappas = [kext[eight, h * LANES : (h + 1) * LANES] for h in range(half)]
        for v in range(nv):
            at = 2 * (nv * r + v)
            left_edge = pltpu.roll(side, (LANES - 1 - at) & (LANES - 1), 1)
            right_edge = pltpu.roll(side, (2 * LANES - 1 - 64 - at) & (LANES - 1), 1)
            base = (r + 1) * block

            def load(row, w, h):
                return source[pl.ds(pl.multiple_of(base + row * block + w * k, k), k), h * LANES : (h + 1) * LANES]

            center = [load(0, v, h) for h in range(half)]
            ahead = [pltpu.roll(c, 1, 1) for c in center]
            behind = [pltpu.roll(c, LANES - 1, 1) for c in center]
            for h in range(half):
                kap = kappas[h][v : v + 1]
                left = jnp.where(lane == 0, left_edge if h == 0 else ahead[h - 1], ahead[h])
                right = jnp.where(lane == LANES - 1, right_edge if h == half - 1 else behind[h + 1], behind[h])
                around = (load(-1, v, h) + load(1, v, h)) + (left + right)
                out = (1.0 - 4.0 * kap + mixing[v, v]) * center[h] + kap * around
                for w in range(nv):
                    if w != v:
                        out = out + mixing[v, w] * load(0, w, h)
                store(v, h, out)

    def step_1(r, carry):
        def store(v, h, out):
            first[pl.ds(pl.multiple_of(r * block + v * k, k), k), h * LANES : (h + 1) * LANES] = out

        advance(state, columns, r, store)
        return carry

    lax.fori_loop(0, cx + 2, step_1, 0)

    sub = lax.broadcasted_iota(jnp.int32, (8, 1), 0)

    def step_2(r, carry):
        eight = pl.ds(pl.multiple_of((r - 1) * 8, 8), 8)
        spreads = [spread[eight, h * LANES : (h + 1) * LANES] for h in range(half)]
        found = [jnp.zeros((8, LANES), F32) for h in range(half)]

        def store(v, h, out):
            q = (r - 1) * nv + v
            mean = jnp.sum(out, axis=0, keepdims=True) * (1.0 / k)
            found[h] = jnp.where(sub == v, mean, found[h])
            part = out - mean
            s2 = spreads[h][v : v + 1]
            s1 = spreads[h][nv + v : nv + v + 1]
            at = pl.ds(pl.multiple_of(q * cy + h * LANES, LANES), LANES)
            high, low = split_2(part)
            anomalies[0:k, at] = high
            anomalies[k : 2 * k, at] = low
            high, low = split_2(part * (s2 * (factor * factor)))
            moved[0:k, at] = high
            moved[k : 2 * k, at] = low
            pull = jnp.broadcast_to((s1 - mean * s2) * factor, (16, LANES))
            high, low = split_2(pull)
            moved[2 * k : 2 * k + 16, at] = high
            moved[2 * k + 16 : 2 * k + 32, at] = low

        advance(first_view(), first_columns, r, store)
        for h in range(half):
            means[eight, h * LANES : (h + 1) * LANES] = found[h]
        return carry

    class first_view:
        def __getitem__(self, index):
            return first[pl.ds(pl.multiple_of(index[0].start - block, k), k), index[1]]

    lax.fori_loop(1, cx + 1, step_2, 0)

    got = nt(moved[...], anomalies[...])
    whole = got[:, 0:k] + got[:, k : 2 * k]
    matrix = whole[0:k] + whole[k : 2 * k]
    pull = whole[2 * k : 2 * k + 8] + whole[2 * k + 16 : 2 * k + 24]
    gram[0 : k // 2, :] = jnp.concatenate([matrix[0 : k // 2], matrix[k // 2 :]], axis=1)
    gram[k // 2 : k // 2 + 8, :] = jnp.concatenate([pull, pull], axis=1)


def apply_kernel(dims, gram, anomalies, means, out, buf, sems):
    k, nv, cx, cy = dims
    rows = nv * cx
    row = lax.broadcasted_iota(jnp.int32, (k, k), 0)
    col = lax.broadcasted_iota(jnp.int32, (k, k), 1)
    eye = (row == col).astype(F32)
    both = gram[...]
    matrix = jnp.concatenate([both[0 : k // 2, 0:k], both[0 : k // 2, k : 2 * k]], axis=0) + eye
    pull = both[k // 2 : k // 2 + 8, 0:k]
    norm = jnp.sqrt(jnp.sum(jnp.sum(matrix * matrix, axis=1, keepdims=True), axis=0, keepdims=True))

    def dot(a, b):
        return jnp.dot(a, b, precision=HIGHEST, preferred_element_type=F32)

    root = matrix / norm
    correction = 1.5 * eye - 0.5 * root
    carried = jnp.concatenate([correction, dot(pull, correction)], axis=0)
    root = dot(root, correction)
    for i in range(1, NS_ITERS):
        correction = 1.5 * eye - 0.5 * dot(carried[0:k], root)
        if i < NS_ITERS - 1:
            root = dot(root, correction)
        carried = dot(carried, correction)
    shift = dot(carried[k:], carried[0:k]) / norm
    weights = carried[0:k] / jnp.sqrt(norm) + shift[0:1, :]
    high, low = split_2(weights)
    high_2 = jnp.concatenate([high, high], axis=1)
    for v in range(nv):
        for r in range(cx):
            q = r * nv + v
            at = slice(q * cy, (q + 1) * cy)
            value = jnp.dot(high_2, anomalies[:, at], preferred_element_type=F32)
            value = value + jnp.dot(low, anomalies[0:k, at], preferred_element_type=F32)
            value = value + means[r * 8 + v : r * 8 + v + 1, :]
            for h in range(cy // LANES):
                buf[h, pl.ds(v * cx + r, k, stride=rows), :] = value[:, h * LANES : (h + 1) * LANES]
    copies = []
    for h in range(cy // LANES):
        copies.append(pltpu.make_async_copy(buf.at[h], out.at[:, h * LANES : (h + 1) * LANES], sems.at[h]))
        copies[-1].start()
    for copy in copies:
        copy.wait()


def local(sizes, ensemble, diffusivity, mixing, obs_cell, obs_var, obs_value, obs_weight):
    k, nv, cx, cy = ensemble.shape
    dims = (k, nv, cx, cy)
    assert k == 64 and nv == 3 and cx == 8 and cy % LANES == 0
    block = nv * k
    rows = nv * cx
    grp, nx, ny = sizes
    count = obs_cell.shape[2]
    factor = 1.0 / math.sqrt((k - 1) * count * nx * ny)
    limits = pltpu.CompilerParams(vmem_limit_bytes=48 << 20)

    def shape(*dims, dtype=F32):
        return jax.ShapeDtypeStruct(dims, dtype)

    state, send_a, send_b, sides = pl.pallas_call(
        functools.partial(load_kernel, dims),
        name="load",
        in_specs=[pl.BlockSpec(memory_space=pl.ANY), vmem()],
        out_specs=[vmem()] * 4,
        out_shape=[
            shape((cx + 4) * block, cy),
            shape(2 * block + 8, cy),
            shape(2 * block + 8, cy),
            shape(k + 8, LANES),
        ],
        scratch_shapes=[pltpu.VMEM((cy // LANES, k * rows, LANES), F32), pltpu.SemaphoreType.DMA((4, cy // LANES))],
        compiler_params=limits,
    )(ensemble.reshape(k * rows, cy), diffusivity)

    recv_b = x_swap(1, sizes)(send_b)
    recv_a = x_swap(0, sizes)(send_a)
    side_a = y_swap(0, sizes)(sides)
    side_b = y_swap(1, sizes)(sides)

    cells = pl.pallas_call(
        functools.partial(scatter_kernel, dims),
        name="scatter",
        in_specs=[vmem()] * 4,
        out_specs=vmem(),
        out_shape=shape(64, cy),
        compiler_params=limits,
    )(*(a.reshape(1, count) for a in (obs_cell, obs_var, obs_value, obs_weight)))

    gy = lax.axis_index("gy")
    lane = lax.broadcasted_iota(jnp.int32, (1, LANES), 1)
    from_a = (gy % 2 == 1) == (lane < 64)
    there = jnp.where(lane < 64, gy > 0, gy < ny - 1)
    halo = jnp.where(there, jnp.where(from_a, side_a, side_b), 0.0)
    corner_b = x_swap(1, sizes)(halo)
    corner_a = x_swap(0, sizes)(halo)

    _, anomalies, means, gram = pl.pallas_call(
        functools.partial(forecast_kernel, dims, factor),
        name="forecast",
        in_specs=[smem()] + [vmem()] * 9,
        out_specs=[vmem()] * 4,
        out_shape=[
            shape((cx + 4) * block, cy),
            shape(2 * k, rows * cy, dtype=BF16),
            shape(cx * 8, cy),
            shape(k // 2 + 8, 2 * k),
        ],
        scratch_shapes=[
            pltpu.VMEM(((cx + 2) * block, cy), F32),
            pltpu.VMEM(((cx + 2) * 8, cy), F32),
            pltpu.VMEM((cx * 8, cy), F32),
            pltpu.VMEM((2 * k + 32, rows * cy), BF16),
        ],
        input_output_aliases={1: 0},
        compiler_params=limits,
    )(mixing, state, recv_a, recv_b, sides, halo, corner_a, corner_b, diffusivity, cells)

    gram = all_sum(gram, sizes)

    out = pl.pallas_call(
        functools.partial(apply_kernel, dims),
        name="apply",
        in_specs=[vmem()] * 3,
        out_specs=pl.BlockSpec(memory_space=pl.ANY),
        out_shape=shape(k * rows, cy),
        scratch_shapes=[pltpu.VMEM((cy // LANES, k * rows, LANES), F32), pltpu.SemaphoreType.DMA((cy // LANES,))],
        compiler_params=limits,
    )(gram, anomalies, means)
    return out.reshape(k, nv, cx, cy)


def solution(mesh):
    sizes = tuple(mesh.shape[a] for a in ("grp", "gx", "gy"))
    return jax.shard_map(
        functools.partial(local, sizes),
        mesh=mesh,
        in_specs=(
            P("grp", None, "gx", "gy"),
            P("grp", "gx", "gy"),
            P(),
            P("gx", "gy", "grp"),
            P("gx", "gy", "grp"),
            P("gx", "gy", "grp"),
            P("gx", "gy", "grp"),
        ),
        out_specs=P("grp", None, "gx", "gy"),
        check_vma=False,
    )
```

```python
import functools
import math

import jax
import jax.numpy as jnp
from jax import lax
from jax.experimental import pallas as pl
from jax.experimental.pallas import tpu as pltpu
from jax.sharding import PartitionSpec as P

NS_ITERS = 5
LANES = 128
HIGHEST = lax.Precision.HIGHEST
F32 = jnp.float32
BF16 = jnp.bfloat16


def vmem():
    return pl.BlockSpec(memory_space=pltpu.VMEM)


def smem():
    return pl.BlockSpec(memory_space=pltpu.SMEM)


def nt(a, b):
    return lax.dot_general(a, b, (((1,), (1,)), ((), ())), preferred_element_type=F32)


def split_2(x):
    high = x.astype(BF16)
    return high, (x - high.astype(F32)).astype(BF16)


def split_3(x):
    high = x.astype(BF16)
    rest = x - high.astype(F32)
    middle = rest.astype(BF16)
    return high, middle, (rest - middle.astype(F32)).astype(BF16)


def pair_swap(partner, sizes):
    grp, nx, ny = sizes
    pairs = []
    for g in range(grp):
        for x in range(nx):
            for y in range(ny):
                there = partner(g, x, y)
                if there is not None:
                    tg, tx, ty = there
                    pairs.append(((g * nx + x) * ny + y, (tg * nx + tx) * ny + ty))
    return lambda value: lax.ppermute(value, ("grp", "gx", "gy"), pairs)


def along(place, count, phase):
    first = place - (place - phase) % 2
    if first < 0 or first + 1 >= count:
        return None
    return first + 1 if place == first else first


def x_swap(phase, sizes):
    def partner(g, x, y):
        there = along(x, sizes[1], phase)
        if there is not None:
            return g, there, y
        return (g ^ 1, x, y) if sizes[0] % 2 == 0 else None

    return pair_swap(partner, sizes)


def y_swap(phase, sizes):
    def partner(g, x, y):
        there = along(y, sizes[2], phase)
        if there is not None:
            return g, x, there
        return (g, x ^ 1, y) if sizes[1] % 2 == 0 else None

    return pair_swap(partner, sizes)


def all_sum(value, sizes):
    grp, nx, ny = sizes
    if nx & (nx - 1) or ny & (ny - 1) or nx < 2:
        return lax.psum(value, ("gx", "gy"))

    def chip_swap(mask_0, mask_1):
        def partner(g, x, y):
            chip = ((x >> 1) * ny + y) ^ (mask_1 if x & 1 else mask_0)
            return g, ((chip // ny) << 1) | (x & 1), chip % ny

        return pair_swap(partner, sizes)

    core_swap = pair_swap(lambda g, x, y: (g, x ^ 1, y), sizes)
    chips = nx // 2 * ny
    value = value + core_swap(value)
    if chips == 8:
        parts = [chip_swap(a, b)(value) for a, b in ((4, 4), (1, 5), (2, 6), (3, 7))]
        value = 0.5 * (value + parts[0]) + parts[1] + parts[2] + parts[3]
        return value + core_swap(value)
    step = 1
    while step < chips:
        value = value + chip_swap(step, step)(value)
        step *= 2
    return value


def load_kernel(dims, ens, *refs):
    small_in, (state, send_a, send_b, sides, side_a, side_b) = refs[:6], refs[6:12]
    small, (buf, sems, small_sems) = refs[12:18], refs[18:]
    kappa = small[0]
    k, nv, cx, cy = dims
    rows = nv * cx
    chunks = 4
    part = k // chunks
    copies = []
    half = cy // LANES
    for c in range(chunks):
        span = pl.ds(c * part * rows, part * rows)
        for h in range(half):
            lanes = slice(h * LANES, (h + 1) * LANES)
            copies.append(pltpu.make_async_copy(ens.at[span, lanes], buf.at[h, span], sems.at[c, h]))
            copies[-1].start()
    small_copies = [pltpu.make_async_copy(a, b, small_sems.at[i]) for i, (a, b) in enumerate(zip(small_in, small))]
    for copy in small_copies:
        copy.start()
    for c in range(chunks):
        for h in range(half):
            copies[c * half + h].wait()
            for r in range(cx):
                for v in range(nv):
                    value = buf[h, pl.ds(c * part * rows + v * cx + r, part, stride=rows), :]
                    at = pl.ds(((r + 2) * nv + v) * k + c * part, part)
                    state[at, h * LANES : (h + 1) * LANES] = value
    for copy in small_copies:
        copy.wait()
    block = nv * k
    even_x = lax.axis_index("gx") % 2 == 0
    top = 2 * block
    bottom = (cx + 1) * block
    for ref, near_top in ((send_a, jnp.logical_not(even_x)), (send_b, even_x)):
        near = jnp.where(near_top, top, bottom)
        second = jnp.where(near_top, top + block, bottom - block)
        for j in range(0, block, 64):
            ref[pl.ds(j, 64), :] = state[pl.ds(pl.multiple_of(near + j, 64), 64), :]
            ref[pl.ds(block + j, 64), :] = state[pl.ds(pl.multiple_of(second + j, 64), 64), :]
        for v in range(nv):
            edge = jnp.where(near_top, kappa[v, 0:1, :], kappa[v, cx - 1 : cx, :])
            ref[pl.ds(2 * block + v, 1), :] = edge
        ref[pl.ds(2 * block + nv, 8 - nv), :] = jnp.zeros((8 - nv, cy), F32)

    lane = lax.broadcasted_iota(jnp.int32, (1, LANES), 1)
    total = jnp.zeros((k, LANES), F32)
    total_k = jnp.zeros((8, LANES), F32)
    for r in range(cx):
        for v in range(nv):
            place = 2 * (nv * (r + 1) + v)
            base = ((r + 2) * nv + v) * k
            low = (lane >= place) & (lane < place + 2)
            high = (lane >= 64 + place) & (lane < 64 + place + 2)

            def add(acc, right, left):
                acc = jnp.where(low, pltpu.roll(right, (place + 2) % LANES, 1), acc)
                return jnp.where(high, pltpu.roll(left, 64 + place, 1), acc)

            total = add(total, state[pl.ds(base, k), cy - LANES :], state[pl.ds(base, k), :LANES])
            row = kappa[v, r : r + 1, :]
            total_k = add(
                total_k,
                jnp.broadcast_to(row[:, cy - LANES :], (8, LANES)),
                jnp.broadcast_to(row[:, :LANES], (8, LANES)),
            )
    sides[0:k, :] = total
    sides[k : k + 8, :] = total_k
    gy = lax.axis_index("gy")
    even_y = gy % 2 == 0
    has_left = gy > 0
    has_right = gy < lax.axis_size("gy") - 1
    for ref, to_right in ((side_a, even_y), (side_b, jnp.logical_not(even_y))):
        start = jnp.where(jnp.where(to_right, has_right, has_left), jnp.where(to_right, 0, 64), LANES)
        wanted = (lane >= start) & (lane < start + 64)
        ref[0:k, :] = jnp.where(wanted, total, 0.0)
        ref[k : k + 8, :] = jnp.where(wanted, total_k, 0.0)


def scatter_kernel(dims, cell, var, value, weight, out):
    k, nv, cx, cy = dims
    count = cell.shape[1]
    row = cell[...] // cy * nv + var[...]
    column = cell[...] % cy
    square = weight[...] * weight[...]
    rows = 32
    hit = lax.broadcasted_iota(jnp.int32, (rows, count), 0) == row
    parts = split_3(square) + split_3(square * value[...])
    left = [jnp.where(hit, p.astype(F32), 0.0).astype(BF16) for p in parts]
    one = (lax.broadcasted_iota(jnp.int32, (cy, count), 0) == column).astype(F32).astype(BF16)
    got = nt(jnp.concatenate(left, axis=0), one)
    piece = [got[i * rows : (i + 1) * rows] for i in range(6)]
    out[0:rows, :] = piece[0] + piece[1] + piece[2]
    out[rows : 2 * rows, :] = piece[3] + piece[4] + piece[5]


def first_columns_of(dims, mixing, columns, kcol, own, lane):
    k, nv, cx, cy = dims
    slot = lane % 64
    inside = (slot >= 2 * nv) & (slot < 2 * nv * (cx + 1))
    beside = jnp.where(
        lane < 64,
        pltpu.roll(columns, 1, 1) + pltpu.roll(own, 65, 1),
        pltpu.roll(columns, LANES - 1, 1) + pltpu.roll(own, 63, 1),
    )
    step = 2 * nv
    beside = beside + pltpu.roll(columns, step, 1) + pltpu.roll(columns, LANES - step, 1)
    which = slot // 2 % nv
    mixed = jnp.zeros((k, LANES), F32)
    for shift in range(1 - nv, nv):
        coef = jnp.zeros((1, LANES), F32)
        for v in range(nv):
            if 0 <= v + shift < nv:
                coef = jnp.where(which == v, mixing[v, v + shift], coef)
        source = pltpu.roll(columns, (-2 * shift) % LANES, 1) if shift else columns
        mixed = mixed + coef * source
    return jnp.where(inside, columns + kcol * (beside - 4.0 * columns) + mixed, 0.0)


def advance(dims, mixing, kext, load, side, e, lane, store):
    k, nv, cx, cy = dims
    half = cy // LANES
    eight = pl.ds(pl.multiple_of(e * 8, 8), 8)
    kappas = [kext[eight, h * LANES : (h + 1) * LANES] for h in range(half)]
    first_lane = lane == 0
    last_lane = lane == LANES - 1
    for v in range(nv):
        at = 2 * (nv * e + v)
        to_left = (LANES - 1 - at) & (LANES - 1)
        to_right = (2 * LANES - 1 - 64 - at) & (LANES - 1)
        kap = [jnp.broadcast_to(kappas[h][v : v + 1], (8, LANES)) for h in range(half)]
        own = [1.0 - 4.0 * kap[h] + mixing[v, v] for h in range(half)]
        others = [(w, mixing[v, w]) for w in range(nv) if w != v]
        for j in range(0, k, 8):
            edge = side[pl.ds(j, 8), :]
            left_edge = pltpu.roll(edge, to_left, 1)
            right_edge = pltpu.roll(edge, to_right, 1)
            center = [load(0, v, j, h) for h in range(half)]
            ahead = [pltpu.roll(c, 1, 1) for c in center]
            behind = [pltpu.roll(c, LANES - 1, 1) for c in center]
            for h in range(half):
                left = jnp.where(first_lane, left_edge if h == 0 else ahead[h - 1], ahead[h])
                right = jnp.where(last_lane, right_edge if h == half - 1 else behind[h + 1], behind[h])
                around = (load(-1, v, j, h) + load(1, v, j, h)) + (left + right)
                out = own[h] * center[h] + kap[h] * around
                for w, factor in others:
                    out = out + factor * load(0, w, j, h)
                store(v, j, h, out)


def rows_forecast(
    dims, factor, mixing, kext, spread, state, first, side, first_side, rows_1, rows_2, outs, lane
):
    k, nv, cx, cy = dims
    block = nv * k
    half = cy // LANES
    anomalies, means, moved, kept = outs

    def loader(ref, base):
        def load(row, w, j, h):
            at = pl.multiple_of(base + row * block + w * k + j, 8)
            return ref[pl.ds(at, 8), h * LANES : (h + 1) * LANES]

        return load

    def step_1(i, carry):
        e = rows_1[1](i)

        def store(v, j, h, out):
            first[pl.ds(pl.multiple_of(e * block + v * k + j, 8), 8), h * LANES : (h + 1) * LANES] = out

        advance(dims, mixing, kext, loader(state, (e + 1) * block), side, e, lane, store)
        return carry

    lax.fori_loop(0, rows_1[0], step_1, 0)
    sub = lax.broadcasted_iota(jnp.int32, (8, 1), 0)

    def step_2(i, carry):
        e = rows_2[1](i)
        eight = pl.ds(pl.multiple_of((e - 1) * 8, 8), 8)
        spreads = [spread[eight, h * LANES : (h + 1) * LANES] for h in range(half)]

        def store(v, j, h, out):
            kept[pl.ds(v * k + j, 8), h * LANES : (h + 1) * LANES] = out

        advance(dims, mixing, kext, loader(first, e * block), first_side, e, lane, store)
        for h in range(half):
            found = jnp.zeros((8, LANES), F32)
            for v in range(nv):
                lanes = slice(h * LANES, (h + 1) * LANES)
                out = kept[v * k : (v + 1) * k, lanes]
                mean = jnp.sum(out, axis=0, keepdims=True) * (1.0 / k)
                found = jnp.where(sub == v, mean, found)
                s2 = spreads[h][v : v + 1]
                s1 = spreads[h][nv + v : nv + v + 1]
                at = pl.ds(pl.multiple_of((i * nv + v) * cy + h * LANES, LANES), LANES)
                scale = s2 * (factor * factor)
                for j in range(0, k, 16):
                    part = out[j : j + 16] - mean
                    high, low = split_2(part)
                    anomalies[j : j + 16, at] = high
                    anomalies[k + j : k + j + 16, at] = low
                    high, low = split_2(part * scale)
                    moved[j : j + 16, at] = high
                    moved[k + j : k + j + 16, at] = low
                pull = jnp.broadcast_to((s1 - mean * s2) * factor, (16, LANES))
                high, low = split_2(pull)
                moved[2 * k : 2 * k + 16, at] = high
                moved[2 * k + 16 : 2 * k + 32, at] = low
            means[pl.ds(pl.multiple_of(i * 8, 8), 8), h * LANES : (h + 1) * LANES] = found
        return carry

    lax.fori_loop(0, rows_2[0], step_2, 0)
    return nt(moved[...], anomalies[...])


def set_rows(dims, kappa, cells, kext, spread):
    k, nv, cx, cy = dims
    for v in range(nv):
        for r in range(cx):
            kext[pl.ds((r + 1) * 8 + v, 1), :] = kappa[v, r : r + 1, :]
            spread[pl.ds(r * 8 + v, 1), :] = cells[pl.ds(r * nv + v, 1), :]
            spread[pl.ds(r * 8 + nv + v, 1), :] = cells[pl.ds(32 + r * nv + v, 1), :]


def inner_kernel(
    dims, factor, mixing, state, sides, halo, kappa, cells,
    first, anomalies, means, partial, kext, spread, first_side, moved, kept,
):
    k, nv, cx, cy = dims
    set_rows(dims, kappa, cells, kext, spread)
    lane = lax.broadcasted_iota(jnp.int32, (1, LANES), 1)
    first_side[...] = first_columns_of(
        dims, mixing, halo[0:k, :], halo[k : k + 1, :], sides[0:k, :], lane
    )
    partial[...] = rows_forecast(
        dims, factor, mixing, kext, spread, state, first, halo, first_side,
        (cx - 2, lambda i: i + 2), (cx - 4, lambda i: i + 3),
        (anomalies, means, moved, kept), lane,
    )


def edge_kernel(
    dims, factor, mixing, state_in, first_in, partial, recv_a, recv_b, sides, halo, corner_a, corner_b, kappa, cells,
    state, first, anomalies, means, gram, kext, spread, side, first_side, moved, kept,
):
    k, nv, cx, cy = dims
    block = nv * k
    gx = lax.axis_index("gx")
    nx = lax.axis_size("gx")
    even_x = gx % 2 == 0
    has_up = gx > 0
    has_down = gx < nx - 1
    up_is_a = jnp.logical_not(even_x)

    def pick(ref_is_a, has, a, b):
        return jnp.where(has, jnp.where(ref_is_a, a, b), 0.0)

    for j in range(0, 2 * block, 32):
        a = recv_a[pl.ds(j, 32), :]
        b = recv_b[pl.ds(j, 32), :]
        up_at = (block if j < block else -block) + j
        state[pl.ds(up_at, 32), :] = pick(up_is_a, has_up, a, b)
        state[pl.ds((cx + 2) * block + j, 32), :] = pick(even_x, has_down, a, b)
    set_rows(dims, kappa, cells, kext, spread)
    for v in range(nv):
        a = recv_a[pl.ds(2 * block + v, 1), :]
        b = recv_b[pl.ds(2 * block + v, 1), :]
        kext[pl.ds(v, 1), :] = pick(up_is_a, has_up, a, b)
        kext[pl.ds((cx + 1) * 8 + v, 1), :] = pick(even_x, has_down, a, b)

    lane = lax.broadcasted_iota(jnp.int32, (1, LANES), 1)
    slot = lane % 64
    up_corner = pick(up_is_a, has_up, corner_a[...], corner_b[...])
    down_corner = pick(even_x, has_down, corner_a[...], corner_b[...])
    far = 2 * nv * cx
    columns = jnp.where(slot < 2 * nv, pltpu.roll(up_corner, LANES - far, 1), halo[...])
    columns = jnp.where(
        (slot >= 2 * nv * (cx + 1)) & (slot < 2 * nv * (cx + 2)), pltpu.roll(down_corner, far, 1), columns
    )
    side[...] = columns[0:k, :]
    first_side[...] = first_columns_of(dims, mixing, columns[0:k, :], columns[k : k + 1, :], sides[0:k, :], lane)
    got = partial[...] + rows_forecast(
        dims, factor, mixing, kext, spread, state, first, side, first_side,
        (4, lambda i: jnp.where(i < 2, i, i + cx - 2)), (4, lambda i: jnp.where(i < 2, i + 1, i + cx - 3)),
        (anomalies, means, moved, kept), lane,
    )
    whole = got[:, 0:k] + got[:, k : 2 * k]
    matrix = whole[0:k] + whole[k : 2 * k]
    pull = whole[2 * k : 2 * k + 8] + whole[2 * k + 16 : 2 * k + 24]
    gram[0 : k // 2, :] = jnp.concatenate([matrix[0 : k // 2], matrix[k // 2 :]], axis=1)
    gram[k // 2 : k // 2 + 8, :] = jnp.concatenate([pull, pull], axis=1)


def apply_kernel(dims, gram, inner, inner_means, edge, edge_means, out, buf, sems):
    k, nv, cx, cy = dims
    rows = nv * cx
    row = lax.broadcasted_iota(jnp.int32, (k, k), 0)
    col = lax.broadcasted_iota(jnp.int32, (k, k), 1)
    eye = (row == col).astype(F32)
    both = gram[...]
    matrix = jnp.concatenate([both[0 : k // 2, 0:k], both[0 : k // 2, k : 2 * k]], axis=0) + eye
    pull = both[k // 2 : k // 2 + 8, 0:k]
    norm = jnp.sqrt(jnp.sum(jnp.sum(matrix * matrix, axis=1, keepdims=True), axis=0, keepdims=True))

    def dot(a, b):
        return jnp.dot(a, b, precision=HIGHEST, preferred_element_type=F32)

    root = matrix / norm
    correction = 1.5 * eye - 0.5 * root
    carried = jnp.concatenate([correction, dot(pull, correction)], axis=0)
    root = dot(root, correction)
    for i in range(1, NS_ITERS):
        correction = 1.5 * eye - 0.5 * dot(carried[0:k], root)
        if i < NS_ITERS - 1:
            root = dot(root, correction)
        carried = dot(carried, correction)
    shift = dot(carried[k:], carried[0:k]) / norm
    weights = carried[0:k] / jnp.sqrt(norm) + shift[0:1, :]
    high, low = split_2(weights)
    high_2 = jnp.concatenate([high, high], axis=1)
    for v in range(nv):
        for r in range(cx):
            deep = 2 <= r < cx - 2
            i = r - 2 if deep else (r if r < 2 else r - cx + 4)
            anomalies = inner if deep else edge
            means = inner_means if deep else edge_means
            at = slice((i * nv + v) * cy, (i * nv + v + 1) * cy)
            value = jnp.dot(high_2, anomalies[:, at], preferred_element_type=F32)
            value = value + jnp.dot(low, anomalies[0:k, at], preferred_element_type=F32)
            value = value + means[i * 8 + v : i * 8 + v + 1, :]
            for h in range(cy // LANES):
                buf[h, pl.ds(v * cx + r, k, stride=rows), :] = value[:, h * LANES : (h + 1) * LANES]
    copies = []
    for h in range(cy // LANES):
        copies.append(pltpu.make_async_copy(buf.at[h], out.at[:, h * LANES : (h + 1) * LANES], sems.at[h]))
        copies[-1].start()
    for copy in copies:
        copy.wait()


def local(sizes, ensemble, diffusivity, mixing, obs_cell, obs_var, obs_value, obs_weight):
    k, nv, cx, cy = ensemble.shape
    dims = (k, nv, cx, cy)
    assert k == 64 and nv == 3 and cx == 8 and cy % LANES == 0
    block = nv * k
    rows = nv * cx
    grp, nx, ny = sizes
    count = obs_cell.shape[2]
    factor = 1.0 / math.sqrt((k - 1) * count * nx * ny)
    limits = pltpu.CompilerParams(vmem_limit_bytes=16 << 20)

    def shape(*dims, dtype=F32):
        return jax.ShapeDtypeStruct(dims, dtype)

    small = (diffusivity, mixing) + tuple(a.reshape(1, count) for a in (obs_cell, obs_var, obs_value, obs_weight))
    state, send_a, send_b, sides, side_a, side_b, kappa, mixing, *obs = pl.pallas_call(
        functools.partial(load_kernel, dims),
        name="load",
        in_specs=[pl.BlockSpec(memory_space=pltpu.HBM)] * 7,
        out_specs=[vmem()] * 12,
        out_shape=[
            shape((cx + 4) * block, cy),
            shape(2 * block + 8, cy),
            shape(2 * block + 8, cy),
            shape(k + 8, LANES),
            shape(k + 8, LANES),
            shape(k + 8, LANES),
        ]
        + [shape(*a.shape, dtype=a.dtype) for a in small],
        scratch_shapes=[pltpu.VMEM((cy // LANES, k * rows, LANES), F32), pltpu.SemaphoreType.DMA((4, cy // LANES)), pltpu.SemaphoreType.DMA((6,))],
        compiler_params=limits,
    )(
        *(pltpu.with_memory_space_constraint(a, pltpu.HBM) for a in (ensemble.reshape(k * rows, cy),) + small)
    )

    recv_b = x_swap(1, sizes)(send_b)
    side_a = y_swap(0, sizes)(side_a)
    side_b = y_swap(1, sizes)(side_b)
    recv_a = x_swap(0, sizes)(send_a)

    cells = pl.pallas_call(
        functools.partial(scatter_kernel, dims),
        name="scatter",
        in_specs=[vmem()] * 4,
        out_specs=vmem(),
        out_shape=shape(64, cy),
        compiler_params=limits,
    )(*obs)

    side_a, side_b, cells = lax.optimization_barrier((side_a, side_b, cells))
    halo = side_a + side_b
    corner_b = x_swap(1, sizes)(halo)
    corner_a = x_swap(0, sizes)(halo)

    inner_rows = cx - 4
    first, inner_anomalies, inner_means, partial = pl.pallas_call(
        functools.partial(inner_kernel, dims, factor),
        name="inner",
        in_specs=[smem()] + [vmem()] * 5,
        out_specs=[vmem()] * 4,
        out_shape=[
            shape((cx + 2) * block, cy),
            shape(2 * k, inner_rows * nv * cy, dtype=BF16),
            shape(inner_rows * 8, cy),
            shape(2 * k + 32, 2 * k),
        ],
        scratch_shapes=[
            pltpu.VMEM(((cx + 2) * 8, cy), F32),
            pltpu.VMEM((cx * 8, cy), F32),
            pltpu.VMEM((k, LANES), F32),
            pltpu.VMEM((2 * k + 32, inner_rows * nv * cy), BF16),
            pltpu.VMEM((block, cy), F32),
        ],
        compiler_params=limits,
    )(mixing, state, sides, halo, kappa, cells)

    _, _, edge_anomalies, edge_means, gram = pl.pallas_call(
        functools.partial(edge_kernel, dims, factor),
        name="edge",
        in_specs=[smem()] + [vmem()] * 11,
        out_specs=[vmem()] * 5,
        out_shape=[
            shape((cx + 4) * block, cy),
            shape((cx + 2) * block, cy),
            shape(2 * k, 4 * nv * cy, dtype=BF16),
            shape(4 * 8, cy),
            shape(k // 2 + 8, 2 * k),
        ],
        scratch_shapes=[
            pltpu.VMEM(((cx + 2) * 8, cy), F32),
            pltpu.VMEM((cx * 8, cy), F32),
            pltpu.VMEM((k, LANES), F32),
            pltpu.VMEM((k, LANES), F32),
            pltpu.VMEM((2 * k + 32, 4 * nv * cy), BF16),
            pltpu.VMEM((block, cy), F32),
        ],
        input_output_aliases={1: 0, 2: 1},
        compiler_params=limits,
    )(
        mixing, state, first, partial, recv_a, recv_b, sides, halo, corner_a, corner_b, kappa, cells
    )

    gram = all_sum(gram, sizes)

    out = pl.pallas_call(
        functools.partial(apply_kernel, dims),
        name="apply",
        in_specs=[vmem()] * 5,
        out_specs=pl.BlockSpec(memory_space=pltpu.HBM),
        out_shape=shape(k * rows, cy),
        scratch_shapes=[pltpu.VMEM((cy // LANES, k * rows, LANES), F32), pltpu.SemaphoreType.DMA((cy // LANES,))],
        compiler_params=limits,
    )(gram, inner_anomalies, inner_means, edge_anomalies, edge_means)
    return out.reshape(k, nv, cx, cy)


def solution(mesh):
    sizes = tuple(mesh.shape[a] for a in ("grp", "gx", "gy"))
    return jax.shard_map(
        functools.partial(local, sizes),
        mesh=mesh,
        in_specs=(
            P("grp", None, "gx", "gy"),
            P("grp", "gx", "gy"),
            P(),
            P("gx", "gy", "grp"),
            P("gx", "gy", "grp"),
            P("gx", "gy", "grp"),
            P("gx", "gy", "grp"),
        ),
        out_specs=P("grp", None, "gx", "gy"),
        check_vma=False,
    )
```

```python
import functools
import math

import jax
import jax.numpy as jnp
from jax import lax
from jax.experimental import pallas as pl
from jax.experimental.pallas import tpu as pltpu
from jax.sharding import PartitionSpec as P

NS_ITERS = 5
LANES = 128
F32 = jnp.float32
BF16 = jnp.bfloat16


def vmem():
    return pl.BlockSpec(memory_space=pltpu.VMEM)


def smem():
    return pl.BlockSpec(memory_space=pltpu.SMEM)


def nt(a, b):
    return lax.dot_general(a, b, (((1,), (1,)), ((), ())), preferred_element_type=F32)


def split_2(x):
    high = x.astype(BF16)
    return high, (x - high.astype(F32)).astype(BF16)


def split_3(x):
    high = x.astype(BF16)
    rest = x - high.astype(F32)
    middle = rest.astype(BF16)
    return high, middle, (rest - middle.astype(F32)).astype(BF16)


def pair_swap(partner, sizes):
    grp, nx, ny = sizes
    pairs = []
    for g in range(grp):
        for x in range(nx):
            for y in range(ny):
                there = partner(g, x, y)
                if there is not None:
                    tg, tx, ty = there
                    pairs.append(((g * nx + x) * ny + y, (tg * nx + tx) * ny + ty))
    return lambda value: lax.ppermute(value, ("grp", "gx", "gy"), pairs)


def along(place, count, phase):
    first = place - (place - phase) % 2
    if first < 0 or first + 1 >= count:
        return None
    return first + 1 if place == first else first


def x_swap(phase, sizes):
    def partner(g, x, y):
        there = along(x, sizes[1], phase)
        if there is not None:
            return g, there, y
        return (g ^ 1, x, y) if sizes[0] % 2 == 0 else None

    return pair_swap(partner, sizes)


def y_swap(phase, sizes):
    def partner(g, x, y):
        there = along(y, sizes[2], phase)
        if there is not None:
            return g, x, there
        return (g, x ^ 1, y) if sizes[1] % 2 == 0 else None

    return pair_swap(partner, sizes)


def all_sum(value, sizes):
    grp, nx, ny = sizes
    if nx & (nx - 1) or ny & (ny - 1) or nx < 2:
        return lax.psum(value, ("gx", "gy"))

    def chip_swap(mask_0, mask_1):
        def partner(g, x, y):
            chip = ((x >> 1) * ny + y) ^ (mask_1 if x & 1 else mask_0)
            return g, ((chip // ny) << 1) | (x & 1), chip % ny

        return pair_swap(partner, sizes)

    core_swap = pair_swap(lambda g, x, y: (g, x ^ 1, y), sizes)
    chips = nx // 2 * ny
    value = value + core_swap(value)
    if chips == 8:
        parts = [chip_swap(a, b)(value) for a, b in ((4, 4), (1, 5), (2, 6), (3, 7))]
        value = 0.5 * (value + parts[0]) + parts[1] + parts[2] + parts[3]
        return value + core_swap(value)
    step = 1
    while step < chips:
        value = value + chip_swap(step, step)(value)
        step *= 2
    return value


def load_kernel(dims, ens, *refs):
    small_in, (state, send_a, send_b, sides, side_a, side_b) = refs[:6], refs[6:12]
    small, (buf, sems, small_sems) = refs[12:18], refs[18:]
    kappa = small[0]
    k, nv, cx, cy = dims
    rows = nv * cx
    chunks = 4
    part = k // chunks
    copies = []
    half = cy // LANES
    for c in range(chunks):
        span = pl.ds(c * part * rows, part * rows)
        for h in range(half):
            lanes = slice(h * LANES, (h + 1) * LANES)
            copies.append(pltpu.make_async_copy(ens.at[span, lanes], buf.at[h, span], sems.at[c, h]))
            copies[-1].start()
    small_copies = [pltpu.make_async_copy(a, b, small_sems.at[i]) for i, (a, b) in enumerate(zip(small_in, small))]
    for copy in small_copies:
        copy.start()
    lane = lax.broadcasted_iota(jnp.int32, (1, LANES), 1)

    def add(acc, place, right, left):
        low = (lane >= place) & (lane < place + 2)
        high = (lane >= 64 + place) & (lane < 64 + place + 2)
        acc = jnp.where(low, pltpu.roll(right, (place + 2) % LANES, 1), acc)
        return jnp.where(high, pltpu.roll(left, 64 + place, 1), acc)

    gy = lax.axis_index("gy")
    even_y = gy % 2 == 0
    has_left = gy > 0
    has_right = gy < lax.axis_size("gy") - 1
    wanted = []
    for to_right in (even_y, jnp.logical_not(even_y)):
        start = jnp.where(jnp.where(to_right, has_right, has_left), jnp.where(to_right, 0, 64), LANES)
        wanted.append((lane >= start) & (lane < start + 64))

    def put_sides(at, total):
        sides[at, :] = total
        side_a[at, :] = jnp.where(wanted[0], total, 0.0)
        side_b[at, :] = jnp.where(wanted[1], total, 0.0)

    for c in range(chunks):
        for h in range(half):
            copies[c * half + h].wait()
        total = jnp.zeros((part, LANES), F32)
        for r in range(cx):
            for v in range(nv):
                at = pl.ds(((r + 2) * nv + v) * k + c * part, part)
                values = [buf[h, pl.ds(c * part * rows + v * cx + r, part, stride=rows), :] for h in range(half)]
                for h in range(half):
                    state[at, h * LANES : (h + 1) * LANES] = values[h]
                total = add(total, 2 * (nv * (r + 1) + v), values[-1], values[0])
        put_sides(pl.ds(c * part, part), total)
    for copy in small_copies:
        copy.wait()
    block = nv * k
    even_x = lax.axis_index("gx") % 2 == 0
    top = 2 * block
    bottom = (cx + 1) * block
    gx = lax.axis_index("gx")
    has_up = gx > 0
    has_down = gx < lax.axis_size("gx") - 1
    for ref, near_top in ((send_a, jnp.logical_not(even_x)), (send_b, even_x)):
        has = jnp.where(near_top, has_up, has_down)
        near = jnp.where(near_top, top, bottom)
        second = jnp.where(near_top, top + block, bottom - block)
        for j in range(0, block, 64):
            ref[pl.ds(j, 64), :] = jnp.where(has, state[pl.ds(pl.multiple_of(near + j, 64), 64), :], 0.0)
            ref[pl.ds(block + j, 64), :] = jnp.where(has, state[pl.ds(pl.multiple_of(second + j, 64), 64), :], 0.0)
        for v in range(nv):
            edge = jnp.where(near_top, kappa[v, 0:1, :], kappa[v, cx - 1 : cx, :])
            ref[pl.ds(2 * block + v, 1), :] = jnp.where(has, edge, 0.0)
        ref[pl.ds(2 * block + nv, 8 - nv), :] = jnp.zeros((8 - nv, cy), F32)

    total = jnp.zeros((8, LANES), F32)
    for r in range(cx):
        for v in range(nv):
            row = kappa[v, r : r + 1, :]
            total = add(
                total,
                2 * (nv * (r + 1) + v),
                jnp.broadcast_to(row[:, cy - LANES :], (8, LANES)),
                jnp.broadcast_to(row[:, :LANES], (8, LANES)),
            )
    put_sides(pl.ds(k, 8), total)


def scatter_kernel(dims, cell, var, value, weight, out):
    k, nv, cx, cy = dims
    count = cell.shape[1]
    row = cell[...] // cy * nv + var[...]
    column = cell[...] % cy
    square = weight[...] * weight[...]
    rows = 32
    hit = lax.broadcasted_iota(jnp.int32, (rows, count), 0) == row
    parts = split_3(square) + split_3(square * value[...])
    left = [jnp.where(hit, p.astype(F32), 0.0).astype(BF16) for p in parts]
    one = (lax.broadcasted_iota(jnp.int32, (cy, count), 0) == column).astype(F32).astype(BF16)
    got = nt(jnp.concatenate(left, axis=0), one)
    piece = [got[i * rows : (i + 1) * rows] for i in range(6)]
    out[0:rows, :] = piece[0] + piece[1] + piece[2]
    out[rows : 2 * rows, :] = piece[3] + piece[4] + piece[5]


def first_columns_of(dims, mixing, columns, kcol, own, lane):
    k, nv, cx, cy = dims
    slot = lane % 64
    inside = (slot >= 2 * nv) & (slot < 2 * nv * (cx + 1))
    beside = jnp.where(
        lane < 64,
        pltpu.roll(columns, 1, 1) + pltpu.roll(own, 65, 1),
        pltpu.roll(columns, LANES - 1, 1) + pltpu.roll(own, 63, 1),
    )
    step = 2 * nv
    beside = beside + pltpu.roll(columns, step, 1) + pltpu.roll(columns, LANES - step, 1)
    which = slot // 2 % nv
    mixed = jnp.zeros((k, LANES), F32)
    for shift in range(1 - nv, nv):
        coef = jnp.zeros((1, LANES), F32)
        for v in range(nv):
            if 0 <= v + shift < nv:
                coef = jnp.where(which == v, mixing[v, v + shift], coef)
        source = pltpu.roll(columns, (-2 * shift) % LANES, 1) if shift else columns
        mixed = mixed + coef * source
    return jnp.where(inside, columns + kcol * (beside - 4.0 * columns) + mixed, 0.0)


def advance(dims, mixing, kext, load, side, e, lane, store):
    k, nv, cx, cy = dims
    half = cy // LANES
    eight = pl.ds(pl.multiple_of(e * 8, 8), 8)
    kappas = [kext[eight, h * LANES : (h + 1) * LANES] for h in range(half)]
    first_lane = lane == 0
    last_lane = lane == LANES - 1
    for v in range(nv):
        shift = (LANES - 1 - 2 * (nv * e + v)) & (LANES - 1)
        kap = [jnp.broadcast_to(kappas[h][v : v + 1], (8, LANES)) for h in range(half)]
        own = [1.0 - 4.0 * kap[h] + mixing[v, v] for h in range(half)]
        others = [(w, mixing[v, w]) for w in range(nv) if w != v]
        for j in range(0, k, 8):
            edge = 0.0 if side is None else pltpu.roll(side[pl.ds(j, 8), :], shift, 1)
            center = [load(0, v, j, h) for h in range(half)]
            ahead = [pltpu.roll(c, 1, 1) for c in center]
            behind = [pltpu.roll(c, LANES - 1, 1) for c in center]
            for h in range(half):
                left = jnp.where(first_lane, edge if h == 0 else ahead[h - 1], ahead[h])
                right = jnp.where(last_lane, edge if h == half - 1 else behind[h + 1], behind[h])
                around = (load(-1, v, j, h) + load(1, v, j, h)) + (left + right)
                out = own[h] * center[h] + kap[h] * around
                for w, factor in others:
                    out = out + factor * load(0, w, j, h)
                store(v, j, h, out)


def edges_of(columns, lane):
    return jnp.where(lane % 2 == 0, pltpu.roll(columns, 64, 1), columns)


def loader(ref, base, k, row_size):
    def load(row, w, j, h):
        at = pl.multiple_of(base + row * row_size + w * k + j, 8)
        return ref[pl.ds(at, 8), h * LANES : (h + 1) * LANES]

    return load


def first_step(dims, mixing, kext, state, first, side, count, row_of, lane):
    k, nv, cx, cy = dims
    block = nv * k

    def step(i, carry):
        e = row_of(i)

        def store(v, j, h, out):
            first[pl.ds(pl.multiple_of(e * block + v * k + j, 8), 8), h * LANES : (h + 1) * LANES] = out

        advance(dims, mixing, kext, loader(state, (e + 1) * block, k, block), side, e, lane, store)
        return carry

    lax.fori_loop(0, count, step, 0)


def add_sides(dims, kext, first, side, count, row_of, lane):
    k, nv, cx, cy = dims
    block = nv * k
    ends = ((0, lane == 0), (cy - LANES, lane == LANES - 1))

    def step(i, carry):
        e = row_of(i)
        eight = pl.ds(pl.multiple_of(e * 8, 8), 8)
        for v in range(nv):
            shift = (LANES - 1 - 2 * (nv * e + v)) & (LANES - 1)
            kap = []
            for at, here in ends:
                row = jnp.where(here, kext[eight, at : at + LANES][v : v + 1], 0.0)
                kap.append(jnp.broadcast_to(row, (8, LANES)))
            for j in range(0, k, 8):
                edge = pltpu.roll(side[pl.ds(j, 8), :], shift, 1)
                rows = pl.ds(pl.multiple_of(e * block + v * k + j, 8), 8)
                for (at, here), factor in zip(ends, kap):
                    first[rows, at : at + LANES] += factor * edge
        return carry

    lax.fori_loop(0, count, step, 0)


def second_step(dims, factor, mixing, kext, spread, first, first_side, count, row_of, outs, lane):
    k, nv, cx, cy = dims
    block = nv * k
    half = cy // LANES
    anomalies, means, moved, kept = outs
    sub = lax.broadcasted_iota(jnp.int32, (8, 1), 0)

    def step_2(i, carry):
        e = row_of(i)
        eight = pl.ds(pl.multiple_of((e - 1) * 8, 8), 8)
        spreads = [spread[eight, h * LANES : (h + 1) * LANES] for h in range(half)]

        def store(v, j, h, out):
            kept[pl.ds(v * k + j, 8), h * LANES : (h + 1) * LANES] = out

        advance(dims, mixing, kext, loader(first, e * block, k, block), first_side, e, lane, store)
        for h in range(half):
            found = jnp.zeros((8, LANES), F32)
            for v in range(nv):
                lanes = slice(h * LANES, (h + 1) * LANES)
                out = kept[v * k : (v + 1) * k, lanes]
                mean = jnp.sum(out, axis=0, keepdims=True) * (1.0 / k)
                found = jnp.where(sub == v, mean, found)
                s2 = spreads[h][v : v + 1]
                s1 = spreads[h][nv + v : nv + v + 1]
                at = pl.ds(pl.multiple_of((i * nv + v) * cy + h * LANES, LANES), LANES)
                scale = s2 * (factor * factor)
                for j in range(0, k, 16):
                    part = out[j : j + 16] - mean
                    high, low = split_2(part)
                    anomalies[j : j + 16, at] = high
                    anomalies[k + j : k + j + 16, at] = low
                    high, low = split_2(part * scale)
                    moved[j : j + 16, at] = high
                    moved[k + j : k + j + 16, at] = low
                pull = jnp.broadcast_to((s1 - mean * s2) * factor, (16, LANES))
                high, low = split_2(pull)
                moved[2 * k : 2 * k + 16, at] = high
                moved[2 * k + 16 : 2 * k + 32, at] = low
            means[pl.ds(pl.multiple_of(i * 8, 8), 8), h * LANES : (h + 1) * LANES] = found
        return carry

    lax.fori_loop(0, count, step_2, 0)
    return nt(moved[...], anomalies[...])


def set_kappa(dims, kappa, kext):
    k, nv, cx, cy = dims
    for v in range(nv):
        for r in range(cx):
            kext[pl.ds((r + 1) * 8 + v, 1), :] = kappa[v, r : r + 1, :]


def middle_kernel(dims, mixing, state, kappa, cell, var, value, weight, first, kext, spread, cells):
    k, nv, cx, cy = dims
    scatter_kernel(dims, cell, var, value, weight, cells)
    for v in range(nv):
        for r in range(cx):
            spread[pl.ds(r * 8 + v, 1), :] = cells[pl.ds(r * nv + v, 1), :]
            spread[pl.ds(r * 8 + nv + v, 1), :] = cells[pl.ds(32 + r * nv + v, 1), :]
    set_kappa(dims, kappa, kext)
    lane = lax.broadcasted_iota(jnp.int32, (1, LANES), 1)
    first_step(dims, mixing, kext, state, first, None, cx - 2, lambda i: i + 2, lane)


def inner_kernel(
    dims, factor, mixing, first_in, sides, halo, kext, spread,
    first, anomalies, means, partial, side, first_side, moved, kept,
):
    k, nv, cx, cy = dims
    lane = lax.broadcasted_iota(jnp.int32, (1, LANES), 1)
    columns = first_columns_of(dims, mixing, halo[0:k, :], halo[k : k + 1, :], sides[0:k, :], lane)
    side[...] = edges_of(halo[0:k, :], lane)
    first_side[...] = edges_of(columns, lane)
    add_sides(dims, kext, first, side, cx - 2, lambda i: i + 2, lane)
    outs = (anomalies, means, moved, kept)
    partial[...] = second_step(
        dims, factor, mixing, kext, spread, first, first_side, cx - 4, lambda i: i + 3, outs, lane
    )


def edge_kernel(
    dims, factor, mixing, state_in, first_in, partial, recv_a, recv_b, sides, halo, corner_a, corner_b, kext_in, spread,
    state, first, anomalies, means, gram, kext, side, first_side, moved, kept,
):
    k, nv, cx, cy = dims
    block = nv * k
    gx = lax.axis_index("gx")
    nx = lax.axis_size("gx")
    down_is_a = gx % 2 == 0

    def both(a, b):
        return jnp.where(down_is_a, b, a), jnp.where(down_is_a, a, b)

    for j in range(0, 2 * block, 32):
        up, down = both(recv_a[pl.ds(j, 32), :], recv_b[pl.ds(j, 32), :])
        state[pl.ds((block if j < block else -block) + j, 32), :] = up
        state[pl.ds((cx + 2) * block + j, 32), :] = down
    up, down = both(recv_a[2 * block : 2 * block + 8, :], recv_b[2 * block : 2 * block + 8, :])
    kext[8 : 8 * (cx + 1), :] = kext_in[8 : 8 * (cx + 1), :]
    kext[0:8, :] = up
    kext[8 * (cx + 1) : 8 * (cx + 2), :] = down

    lane = lax.broadcasted_iota(jnp.int32, (1, LANES), 1)
    slot = lane % 64
    up, down = both(corner_a[...], corner_b[...])
    up = jnp.where(gx > 0, up, 0.0)
    down = jnp.where(gx < nx - 1, down, 0.0)
    far = 2 * nv * cx
    columns = jnp.where(slot < 2 * nv, pltpu.roll(up, LANES - far, 1), halo[...])
    columns = jnp.where((slot >= 2 * nv * (cx + 1)) & (slot < 2 * nv * (cx + 2)), pltpu.roll(down, far, 1), columns)
    side[...] = edges_of(columns[0:k, :], lane)
    columns = first_columns_of(dims, mixing, columns[0:k, :], columns[k : k + 1, :], sides[0:k, :], lane)
    first_side[...] = edges_of(columns, lane)
    first_step(
        dims, mixing, kext, state, first, side, 4, lambda i: jnp.where(i < 2, i, i + cx - 2), lane
    )
    got = partial[...] + second_step(
        dims, factor, mixing, kext, spread, first, first_side, 4, lambda i: jnp.where(i < 2, i + 1, i + cx - 3),
        (anomalies, means, moved, kept), lane,
    )
    whole = got[:, 0:k] + got[:, k : 2 * k]
    matrix = whole[0:k] + whole[k : 2 * k]
    pull = whole[2 * k : 2 * k + 8] + whole[2 * k + 16 : 2 * k + 24]
    gram[0 : k // 2, :] = jnp.concatenate([matrix[0 : k // 2], matrix[k // 2 :]], axis=1)
    gram[k // 2 : k // 2 + 8, :] = jnp.concatenate([pull, pull], axis=1)


def apply_kernel(dims, gram, inner, inner_means, edge, edge_means, out, buf, sems):
    k, nv, cx, cy = dims
    half = cy // LANES
    row = lax.broadcasted_iota(jnp.int32, (k, k), 0)
    col = lax.broadcasted_iota(jnp.int32, (k, k), 1)
    eye = (row == col).astype(F32)
    both = gram[...]
    matrix = jnp.concatenate([both[0 : k // 2, 0:k], both[0 : k // 2, k : 2 * k]], axis=0) + eye
    pull = both[k // 2 : k // 2 + 8, 0:k]
    norm = jnp.sqrt(jnp.sum(jnp.sum(matrix * matrix, axis=1, keepdims=True), axis=0, keepdims=True))

    def dot(a, b):
        a_high, a_low = split_2(a)
        b_high, b_low = split_2(b)

        def one(x, y):
            return jnp.dot(x, y, preferred_element_type=F32)

        return one(a_high, b_high) + (one(a_high, b_low) + one(a_low, b_high))

    root = matrix / norm
    correction = 1.5 * eye - 0.5 * root
    carried = jnp.concatenate([correction, dot(pull, correction)], axis=0)
    root = dot(root, correction)
    for i in range(1, NS_ITERS):
        correction = 1.5 * eye - 0.5 * dot(carried[0:k], root)
        if i < NS_ITERS - 1:
            root = dot(root, correction)
        carried = dot(carried, correction)
    shift = dot(carried[k:], carried[0:k]) / norm
    weights = carried[0:k] / jnp.sqrt(norm) + shift[0:1, :]
    high, low = split_2(weights)
    high_2 = jnp.concatenate([high, high], axis=1)
    copies = []
    for v in range(nv):
        for r in range(cx):
            deep = 2 <= r < cx - 2
            i = r - 2 if deep else (r if r < 2 else r - cx + 4)
            anomalies = inner if deep else edge
            means = inner_means if deep else edge_means
            at = slice((i * nv + v) * cy, (i * nv + v + 1) * cy)
            value = jnp.dot(high_2, anomalies[:, at], preferred_element_type=F32)
            value = value + jnp.dot(low, anomalies[0:k, at], preferred_element_type=F32)
            value = value + means[i * 8 + v : i * 8 + v + 1, :]
            for h in range(half):
                buf[v * half + h, pl.ds(r, k, stride=cx), :] = value[:, h * LANES : (h + 1) * LANES]
        for h in range(half):
            source = buf.at[v * half + h].reshape(k, cx, LANES)
            target = out.at[:, v, :, h * LANES : (h + 1) * LANES]
            copies.append(pltpu.make_async_copy(source, target, sems.at[v, h]))
            copies[-1].start()
    for copy in copies:
        copy.wait()


def local(sizes, ensemble, diffusivity, mixing, obs_cell, obs_var, obs_value, obs_weight):
    k, nv, cx, cy = ensemble.shape
    dims = (k, nv, cx, cy)
    assert k == 64 and nv == 3 and cx == 8 and cy % LANES == 0
    block = nv * k
    rows = nv * cx
    grp, nx, ny = sizes
    count = obs_cell.shape[2]
    factor = 1.0 / math.sqrt((k - 1) * count * nx * ny)
    limits = pltpu.CompilerParams(vmem_limit_bytes=16 << 20)

    def shape(*dims, dtype=F32):
        return jax.ShapeDtypeStruct(dims, dtype)

    small = (diffusivity, mixing) + tuple(a.reshape(1, count) for a in (obs_cell, obs_var, obs_value, obs_weight))
    state, send_a, send_b, sides, side_a, side_b, kappa, mixing, *obs = pl.pallas_call(
        functools.partial(load_kernel, dims),
        name="load",
        in_specs=[pl.BlockSpec(memory_space=pltpu.HBM)] * 7,
        out_specs=[vmem()] * 12,
        out_shape=[
            shape((cx + 4) * block, cy),
            shape(2 * block + 8, cy),
            shape(2 * block + 8, cy),
            shape(k + 8, LANES),
            shape(k + 8, LANES),
            shape(k + 8, LANES),
        ]
        + [shape(*a.shape, dtype=a.dtype) for a in small],
        scratch_shapes=[pltpu.VMEM((cy // LANES, k * rows, LANES), F32), pltpu.SemaphoreType.DMA((4, cy // LANES)), pltpu.SemaphoreType.DMA((6,))],
        compiler_params=limits,
    )(
        *(pltpu.with_memory_space_constraint(a, pltpu.HBM) for a in (ensemble.reshape(k * rows, cy),) + small)
    )

    recv_b = x_swap(1, sizes)(send_b)
    side_a = y_swap(0, sizes)(side_a)
    side_b = y_swap(1, sizes)(side_b)
    recv_a = x_swap(0, sizes)(send_a)

    first, kext, spread = pl.pallas_call(
        functools.partial(middle_kernel, dims),
        name="middle",
        in_specs=[smem()] + [vmem()] * 6,
        out_specs=[vmem()] * 3,
        out_shape=[shape((cx + 2) * block, cy), shape((cx + 2) * 8, cy), shape(cx * 8, cy)],
        scratch_shapes=[pltpu.VMEM((64, cy), F32)],
        compiler_params=limits,
    )(mixing, state, kappa, *obs)
    side_a, side_b, first = lax.optimization_barrier((side_a, side_b, first))
    halo = side_a + side_b
    corner_b = x_swap(1, sizes)(halo)
    corner_a = x_swap(0, sizes)(halo)

    inner_rows = cx - 4
    first, inner_anomalies, inner_means, partial = pl.pallas_call(
        functools.partial(inner_kernel, dims, factor),
        name="inner",
        in_specs=[smem()] + [vmem()] * 5,
        out_specs=[vmem()] * 4,
        input_output_aliases={1: 0},
        out_shape=[
            shape((cx + 2) * block, cy),
            shape(2 * k, inner_rows * nv * cy, dtype=BF16),
            shape(inner_rows * 8, cy),
            shape(2 * k + 32, 2 * k),
        ],
        scratch_shapes=[
            pltpu.VMEM((k, LANES), F32),
            pltpu.VMEM((k, LANES), F32),
            pltpu.VMEM((2 * k + 32, inner_rows * nv * cy), BF16),
            pltpu.VMEM((block, cy), F32),
        ],
        compiler_params=limits,
    )(mixing, first, sides, halo, kext, spread)

    _, _, edge_anomalies, edge_means, gram = pl.pallas_call(
        functools.partial(edge_kernel, dims, factor),
        name="edge",
        in_specs=[smem()] + [vmem()] * 11,
        out_specs=[vmem()] * 5,
        out_shape=[
            shape((cx + 4) * block, cy),
            shape((cx + 2) * block, cy),
            shape(2 * k, 4 * nv * cy, dtype=BF16),
            shape(4 * 8, cy),
            shape(k // 2 + 8, 2 * k),
        ],
        scratch_shapes=[
            pltpu.VMEM(((cx + 2) * 8, cy), F32),
            pltpu.VMEM((k, LANES), F32),
            pltpu.VMEM((k, LANES), F32),
            pltpu.VMEM((2 * k + 32, 4 * nv * cy), BF16),
            pltpu.VMEM((block, cy), F32),
        ],
        input_output_aliases={1: 0, 2: 1},
        compiler_params=limits,
    )(
        mixing, state, first, partial, recv_a, recv_b, sides, halo, corner_a, corner_b, kext, spread
    )

    gram = all_sum(gram, sizes)

    return pl.pallas_call(
        functools.partial(apply_kernel, dims),
        name="apply",
        in_specs=[vmem()] * 5,
        out_specs=pl.BlockSpec(memory_space=pltpu.HBM),
        out_shape=shape(k, nv, cx, cy),
        scratch_shapes=[
            pltpu.VMEM((nv * (cy // LANES), k * cx, LANES), F32),
            pltpu.SemaphoreType.DMA((nv, cy // LANES)),
        ],
        compiler_params=limits,
    )(gram, inner_anomalies, inner_means, edge_anomalies, edge_means)


def solution(mesh):
    sizes = tuple(mesh.shape[a] for a in ("grp", "gx", "gy"))
    return jax.shard_map(
        functools.partial(local, sizes),
        mesh=mesh,
        in_specs=(
            P("grp", None, "gx", "gy"),
            P("grp", "gx", "gy"),
            P(),
            P("gx", "gy", "grp"),
            P("gx", "gy", "grp"),
            P("gx", "gy", "grp"),
            P("gx", "gy", "grp"),
        ),
        out_specs=P("grp", None, "gx", "gy"),
        check_vma=False,
    )
```

```python
import functools
import math

import jax
import jax.numpy as jnp
from jax import lax
from jax.experimental import pallas as pl
from jax.experimental.pallas import tpu as pltpu
from jax.sharding import PartitionSpec as P

NS_ITERS = 5
LANES = 128
F32 = jnp.float32
BF16 = jnp.bfloat16


def vmem():
    return pl.BlockSpec(memory_space=pltpu.VMEM)


def smem():
    return pl.BlockSpec(memory_space=pltpu.SMEM)


def nt(a, b):
    return lax.dot_general(a, b, (((1,), (1,)), ((), ())), preferred_element_type=F32)


def split_2(x):
    high = x.astype(BF16)
    return high, (x - high.astype(F32)).astype(BF16)


def split_3(x):
    high = x.astype(BF16)
    rest = x - high.astype(F32)
    middle = rest.astype(BF16)
    return high, middle, (rest - middle.astype(F32)).astype(BF16)


def pair_swap(partner, sizes):
    grp, nx, ny = sizes
    pairs = []
    for g in range(grp):
        for x in range(nx):
            for y in range(ny):
                there = partner(g, x, y)
                if there is not None:
                    tg, tx, ty = there
                    pairs.append(((g * nx + x) * ny + y, (tg * nx + tx) * ny + ty))
    return lambda value: lax.ppermute(value, ("grp", "gx", "gy"), pairs)


def along(place, count, phase):
    first = place - (place - phase) % 2
    if first < 0 or first + 1 >= count:
        return None
    return first + 1 if place == first else first


def x_swap(phase, sizes):
    def partner(g, x, y):
        there = along(x, sizes[1], phase)
        if there is not None:
            return g, there, y
        return (g ^ 1, x, y) if sizes[0] % 2 == 0 else None

    return pair_swap(partner, sizes)


def y_swap(phase, sizes):
    def partner(g, x, y):
        there = along(y, sizes[2], phase)
        if there is not None:
            return g, x, there
        return (g, x ^ 1, y) if sizes[1] % 2 == 0 else None

    return pair_swap(partner, sizes)


def all_sum(value, sizes):
    grp, nx, ny = sizes
    if nx & (nx - 1) or ny & (ny - 1) or nx < 2:
        return lax.psum(value, ("gx", "gy"))

    def chip_swap(mask_0, mask_1):
        def partner(g, x, y):
            chip = ((x >> 1) * ny + y) ^ (mask_1 if x & 1 else mask_0)
            return g, ((chip // ny) << 1) | (x & 1), chip % ny

        return pair_swap(partner, sizes)

    core_swap = pair_swap(lambda g, x, y: (g, x ^ 1, y), sizes)
    chips = nx // 2 * ny
    value = value + core_swap(value)
    if chips == 8:
        parts = [chip_swap(a, b)(value) for a, b in ((4, 4), (1, 5), (2, 6), (3, 7))]
        value = 0.5 * (value + parts[0]) + parts[1] + parts[2] + parts[3]
        return value + core_swap(value)
    step = 1
    while step < chips:
        value = value + chip_swap(step, step)(value)
        step *= 2
    return value


def send_rows(dims, state, kappa, ref, near_top):
    k, nv, cx, cy = dims
    block = nv * k
    gx = lax.axis_index("gx")
    has = jnp.where(near_top, gx > 0, gx < lax.axis_size("gx") - 1)
    near = jnp.where(near_top, 2, cx + 1) * block
    second = jnp.where(near_top, 3, cx) * block
    for j in range(0, block, 64):
        ref[pl.ds(j, 64), :] = jnp.where(has, state[pl.ds(pl.multiple_of(near + j, 64), 64), :], 0.0)
        ref[pl.ds(block + j, 64), :] = jnp.where(has, state[pl.ds(pl.multiple_of(second + j, 64), 64), :], 0.0)
    for v in range(nv):
        edge = jnp.where(near_top, kappa[v, 0:1, :], kappa[v, cx - 1 : cx, :])
        ref[pl.ds(2 * block + v, 1), :] = jnp.where(has, edge, 0.0)
    ref[pl.ds(2 * block + nv, 8 - nv), :] = jnp.zeros((8 - nv, cy), F32)


def load_kernel(dims, ens, *refs):
    small_in, (state, send_b, sides, side_a, side_b) = refs[:6], refs[6:11]
    small, (buf, sems, small_sems) = refs[11:17], refs[17:]
    kappa = small[0]
    k, nv, cx, cy = dims
    rows = nv * cx
    chunks = 4
    part = k // chunks
    copies = []
    half = cy // LANES
    for c in range(chunks):
        span = pl.ds(c * part * rows, part * rows)
        for h in range(half):
            lanes = slice(h * LANES, (h + 1) * LANES)
            copies.append(pltpu.make_async_copy(ens.at[span, lanes], buf.at[h, span], sems.at[c, h]))
            copies[-1].start()
    small_copies = [pltpu.make_async_copy(a, b, small_sems.at[i]) for i, (a, b) in enumerate(zip(small_in, small))]
    for copy in small_copies:
        copy.start()
    lane = lax.broadcasted_iota(jnp.int32, (1, LANES), 1)

    def add(acc, place, right, left):
        low = (lane >= place) & (lane < place + 2)
        high = (lane >= 64 + place) & (lane < 64 + place + 2)
        acc = jnp.where(low, pltpu.roll(right, (place + 2) % LANES, 1), acc)
        return jnp.where(high, pltpu.roll(left, 64 + place, 1), acc)

    gy = lax.axis_index("gy")
    even_y = gy % 2 == 0
    has_left = gy > 0
    has_right = gy < lax.axis_size("gy") - 1
    wanted = []
    for to_right in (even_y, jnp.logical_not(even_y)):
        start = jnp.where(jnp.where(to_right, has_right, has_left), jnp.where(to_right, 0, 64), LANES)
        wanted.append((lane >= start) & (lane < start + 64))

    def put_sides(at, total):
        sides[at, :] = total
        side_a[at, :] = jnp.where(wanted[0], total, 0.0)
        side_b[at, :] = jnp.where(wanted[1], total, 0.0)

    for c in range(chunks):
        for h in range(half):
            copies[c * half + h].wait()
        total = jnp.zeros((part, LANES), F32)
        for r in range(cx):
            for v in range(nv):
                at = pl.ds(((r + 2) * nv + v) * k + c * part, part)
                values = [buf[h, pl.ds(c * part * rows + v * cx + r, part, stride=rows), :] for h in range(half)]
                for h in range(half):
                    state[at, h * LANES : (h + 1) * LANES] = values[h]
                total = add(total, 2 * (nv * (r + 1) + v), values[-1], values[0])
        put_sides(pl.ds(c * part, part), total)
    for copy in small_copies:
        copy.wait()
    send_rows(dims, state, kappa, send_b, lax.axis_index("gx") % 2 == 0)
    total = jnp.zeros((8, LANES), F32)
    for r in range(cx):
        for v in range(nv):
            row = kappa[v, r : r + 1, :]
            total = add(
                total,
                2 * (nv * (r + 1) + v),
                jnp.broadcast_to(row[:, cy - LANES :], (8, LANES)),
                jnp.broadcast_to(row[:, :LANES], (8, LANES)),
            )
    put_sides(pl.ds(k, 8), total)


def scatter_kernel(dims, cell, var, value, weight, out):
    k, nv, cx, cy = dims
    count = cell.shape[1]
    row = cell[...] // cy * nv + var[...]
    column = cell[...] % cy
    square = weight[...] * weight[...]
    rows = 32
    hit = lax.broadcasted_iota(jnp.int32, (rows, count), 0) == row
    parts = split_3(square) + split_3(square * value[...])
    left = [jnp.where(hit, p.astype(F32), 0.0).astype(BF16) for p in parts]
    one = (lax.broadcasted_iota(jnp.int32, (cy, count), 0) == column).astype(F32).astype(BF16)
    got = nt(jnp.concatenate(left, axis=0), one)
    piece = [got[i * rows : (i + 1) * rows] for i in range(6)]
    out[0:rows, :] = piece[0] + piece[1] + piece[2]
    out[rows : 2 * rows, :] = piece[3] + piece[4] + piece[5]


def first_columns_of(dims, mixing, columns, kcol, own, lane):
    k, nv, cx, cy = dims
    slot = lane % 64
    inside = (slot >= 2 * nv) & (slot < 2 * nv * (cx + 1))
    beside = jnp.where(
        lane < 64,
        pltpu.roll(columns, 1, 1) + pltpu.roll(own, 65, 1),
        pltpu.roll(columns, LANES - 1, 1) + pltpu.roll(own, 63, 1),
    )
    step = 2 * nv
    beside = beside + pltpu.roll(columns, step, 1) + pltpu.roll(columns, LANES - step, 1)
    which = slot // 2 % nv
    mixed = jnp.zeros((k, LANES), F32)
    for shift in range(1 - nv, nv):
        coef = jnp.zeros((1, LANES), F32)
        for v in range(nv):
            if 0 <= v + shift < nv:
                coef = jnp.where(which == v, mixing[v, v + shift], coef)
        source = pltpu.roll(columns, (-2 * shift) % LANES, 1) if shift else columns
        mixed = mixed + coef * source
    return jnp.where(inside, columns + kcol * (beside - 4.0 * columns) + mixed, 0.0)


def advance(dims, mixing, kext, load, side, e, lane, store):
    k, nv, cx, cy = dims
    half = cy // LANES
    eight = pl.ds(e * 8, 8)
    kappas = [kext[eight, h * LANES : (h + 1) * LANES] for h in range(half)]
    first_lane = lane == 0
    last_lane = lane == LANES - 1
    kap = [[jnp.broadcast_to(kappas[h][v : v + 1], (8, LANES)) for h in range(half)] for v in range(nv)]
    own = [[1.0 - 4.0 * kap[v][h] + mixing[v, v] for h in range(half)] for v in range(nv)]
    for j in range(0, k, 8):
        centers = [[load(0, v, j, h) for h in range(half)] for v in range(nv)]
        for v in range(nv):
            center = centers[v]
            shift = (LANES - 1 - 2 * (nv * e + v)) & (LANES - 1)
            edge = 0.0 if side is None else pltpu.roll(side[pl.ds(j, 8), :], shift, 1)
            ahead = [pltpu.roll(c, 1, 1) for c in center]
            behind = [pltpu.roll(c, LANES - 1, 1) for c in center]
            for h in range(half):
                left = jnp.where(first_lane, edge if h == 0 else ahead[h - 1], ahead[h])
                right = jnp.where(last_lane, edge if h == half - 1 else behind[h + 1], behind[h])
                around = (load(-1, v, j, h) + load(1, v, j, h)) + (left + right)
                out = own[v][h] * center[h] + kap[v][h] * around
                for w in range(nv):
                    if w != v:
                        out = out + mixing[v, w] * centers[w][h]
                store(v, j, h, out)


def edges_of(columns, lane):
    return jnp.where(lane % 2 == 0, pltpu.roll(columns, 64, 1), columns)


def loader(ref, base, k, row_size):
    def load(row, w, j, h):
        at = base + row * row_size + w * k + j
        return ref[pl.ds(at, 8), h * LANES : (h + 1) * LANES]

    return load


def first_step(dims, mixing, kext, state, first, side, rows, lane, inside=False):
    k, nv, cx, cy = dims
    block = nv * k
    for e in rows:

        def store(v, j, h, out):
            first[pl.ds(e * block + v * k + j, 8), h * LANES : (h + 1) * LANES] = out

        plain = loader(state, (e + 1) * block, k, block)

        def load(row, w, j, h):
            return 0.0 if inside and not 1 <= e + row <= cx else plain(row, w, j, h)

        advance(dims, mixing, kext, load, side, e, lane, store)


def add_sides(dims, kext, first, side, rows, lane):
    k, nv, cx, cy = dims
    block = nv * k
    ends = ((0, lane == 0), (cy - LANES, lane == LANES - 1))
    for e in rows:
        for v in range(nv):
            shift = (LANES - 1 - 2 * (nv * e + v)) & (LANES - 1)
            kap = []
            for at, here in ends:
                row = jnp.where(here, kext[e * 8 + v : e * 8 + v + 1, at : at + LANES], 0.0)
                kap.append(jnp.broadcast_to(row, (8, LANES)))
            for j in range(0, k, 8):
                edge = pltpu.roll(side[pl.ds(j, 8), :], shift, 1)
                place = pl.ds(e * block + v * k + j, 8)
                for (at, here), factor in zip(ends, kap):
                    first[place, at : at + LANES] += factor * edge


def second_step(dims, mixing, kext, first, first_side, e, ref, slot, lane):
    k, nv, cx, cy = dims
    block = nv * k
    sums = {}

    def store(v, j, h, out):
        ref[pl.ds(slot * block + v * k + j, 8), h * LANES : (h + 1) * LANES] = out
        sums[v, h] = out if j == 0 else sums[v, h] + out

    advance(dims, mixing, kext, loader(first, e * block, k, block), first_side, e, lane, store)
    return sums


def anomalies_of(dims, factor, spread, e, i, sums, kept, outs):
    k, nv, cx, cy = dims
    block = nv * k
    half = cy // LANES
    anomalies, means, moved = outs
    sub = lax.broadcasted_iota(jnp.int32, (8, 1), 0)
    for h in range(half):
        lanes = slice(h * LANES, (h + 1) * LANES)
        spreads = spread[pl.ds((e - 1) * 8, 8), lanes]
        found = jnp.zeros((8, LANES), F32)
        for v in range(nv):
            mean = jnp.sum(sums[v, h], axis=0, keepdims=True) * (1.0 / k)
            found = jnp.where(sub == v, mean, found)
            s2 = spreads[v : v + 1]
            s1 = spreads[nv + v : nv + v + 1]
            at = pl.ds((i * nv + v) * cy + h * LANES, LANES)
            scale = s2 * (factor * factor)
            for j in range(0, k, 16):
                part = kept[pl.ds(i * block + v * k + j, 16), lanes] - mean
                high, low = split_2(part)
                anomalies[j : j + 16, at] = high
                anomalies[k + j : k + j + 16, at] = low
                high, low = split_2(part * scale)
                moved[j : j + 16, at] = high
                moved[k + j : k + j + 16, at] = low
            pull = jnp.broadcast_to((s1 - mean * s2) * factor, (16, LANES))
            high, low = split_2(pull)
            moved[2 * k : 2 * k + 16, at] = high
            moved[2 * k + 16 : 2 * k + 32, at] = low
        means[i * 8 : i * 8 + 8, lanes] = found


def set_kappa(dims, kappa, kext):
    k, nv, cx, cy = dims
    for v in range(nv):
        for r in range(cx):
            kext[pl.ds((r + 1) * 8 + v, 1), :] = kappa[v, r : r + 1, :]


def middle_kernel(dims, mixing, state, kappa, cell, var, value, weight, first, kext, spread, send_a, cells):
    k, nv, cx, cy = dims
    send_rows(dims, state, kappa, send_a, lax.axis_index("gx") % 2 == 1)
    scatter_kernel(dims, cell, var, value, weight, cells)
    for v in range(nv):
        for r in range(cx):
            spread[pl.ds(r * 8 + v, 1), :] = cells[pl.ds(r * nv + v, 1), :]
            spread[pl.ds(r * 8 + nv + v, 1), :] = cells[pl.ds(32 + r * nv + v, 1), :]
    set_kappa(dims, kappa, kext)
    lane = lax.broadcasted_iota(jnp.int32, (1, LANES), 1)
    first_step(dims, mixing, kext, state, first, None, range(1, cx + 1), lane, inside=True)


def inner_kernel(
    dims, factor, mixing, first_in, sides, halo, kext, spread,
    first, anomalies, means, partial, early, side, first_side, moved, kept,
):
    k, nv, cx, cy = dims
    lane = lax.broadcasted_iota(jnp.int32, (1, LANES), 1)
    columns = first_columns_of(dims, mixing, halo[0:k, :], halo[k : k + 1, :], sides[0:k, :], lane)
    side[...] = edges_of(halo[0:k, :], lane)
    first_side[...] = edges_of(columns, lane)
    add_sides(dims, kext, first, side, range(1, cx + 1), lane)
    outs = (anomalies, means, moved)
    for i, e in enumerate(range(3, cx - 1)):
        sums = second_step(dims, mixing, kext, first, first_side, e, kept, i, lane)
        anomalies_of(dims, factor, spread, e, i, sums, kept, outs)
    partial[...] = nt(moved[...], anomalies[...])
    second_step(dims, mixing, kext, first, first_side, 2, early, 0, lane)
    second_step(dims, mixing, kext, first, first_side, cx - 1, early, 1, lane)


def edge_kernel(
    dims, factor, mixing, state_in, first_in, partial, early, recv_a, recv_b, sides, halo, corner_a, corner_b, kext_in, spread,
    state, first, anomalies, means, gram, kext, side, first_side, moved, kept,
):
    k, nv, cx, cy = dims
    block = nv * k
    gx = lax.axis_index("gx")
    nx = lax.axis_size("gx")
    down_is_a = gx % 2 == 0

    def both(a, b):
        return jnp.where(down_is_a, b, a), jnp.where(down_is_a, a, b)

    for j in range(0, 2 * block, 32):
        up, down = both(recv_a[pl.ds(j, 32), :], recv_b[pl.ds(j, 32), :])
        state[pl.ds((block if j < block else -block) + j, 32), :] = up
        state[pl.ds((cx + 2) * block + j, 32), :] = down
    up, down = both(recv_a[2 * block : 2 * block + 8, :], recv_b[2 * block : 2 * block + 8, :])
    kext[8 : 8 * (cx + 1), :] = kext_in[8 : 8 * (cx + 1), :]
    kext[0:8, :] = up
    kext[8 * (cx + 1) : 8 * (cx + 2), :] = down

    lane = lax.broadcasted_iota(jnp.int32, (1, LANES), 1)
    slot = lane % 64
    up, down = both(corner_a[...], corner_b[...])
    up = jnp.where(gx > 0, up, 0.0)
    down = jnp.where(gx < nx - 1, down, 0.0)
    far = 2 * nv * cx
    columns = jnp.where(slot < 2 * nv, pltpu.roll(up, LANES - far, 1), halo[...])
    columns = jnp.where((slot >= 2 * nv * (cx + 1)) & (slot < 2 * nv * (cx + 2)), pltpu.roll(down, far, 1), columns)
    side[...] = edges_of(columns[0:k, :], lane)
    columns = first_columns_of(dims, mixing, columns[0:k, :], columns[k : k + 1, :], sides[0:k, :], lane)
    first_side[...] = edges_of(columns, lane)
    first_step(dims, mixing, kext, state, first, side, (0, cx + 1), lane)
    half = cy // LANES
    outs = (anomalies, means, moved)

    def late(e, beyond, near, read, write):
        sums = {}
        for v in range(nv):
            for h in range(half):
                lanes = slice(h * LANES, (h + 1) * LANES)
                row = kext[e * 8 + v : e * 8 + v + 1, lanes]
                if near != e:
                    row = row * kext[near * 8 + v : near * 8 + v + 1, lanes]
                row = jnp.broadcast_to(row, (8, LANES))
                for j in range(0, k, 8):
                    out = read[0][pl.ds(read[1] + v * k + j, 8), lanes]
                    out = out + row * state[pl.ds(beyond * block + v * k + j, 8), lanes]
                    write[0][pl.ds(write[1] + v * k + j, 8), lanes] = out
                    sums[v, h] = out if j == 0 else sums[v, h] + out
        return sums

    for e, beyond in ((1, 1), (cx, cx + 2)):
        late(e, beyond, e, (first, e * block), (first, e * block))
    for i, e in enumerate((1, 2, cx - 1, cx)):
        if i in (0, 3):
            sums = second_step(dims, mixing, kext, first, first_side, e, kept, i, lane)
        elif i == 1:
            sums = late(e, 1, 1, (early, 0), (kept, i * block))
        else:
            sums = late(e, cx + 2, cx, (early, block), (kept, i * block))
        anomalies_of(dims, factor, spread, e, i, sums, kept, outs)
    got = partial[...] + nt(moved[...], anomalies[...])
    whole = got[:, 0:k] + got[:, k : 2 * k]
    matrix = whole[0:k] + whole[k : 2 * k]
    pull = whole[2 * k : 2 * k + 8] + whole[2 * k + 16 : 2 * k + 24]
    gram[0 : k // 2, :] = jnp.concatenate([matrix[0 : k // 2], matrix[k // 2 :]], axis=1)
    gram[k // 2 : k // 2 + 8, :] = jnp.concatenate([pull, pull], axis=1)


def apply_kernel(dims, gram, inner, inner_means, edge, edge_means, out, buf, sems):
    k, nv, cx, cy = dims
    half = cy // LANES
    row = lax.broadcasted_iota(jnp.int32, (k, k), 0)
    col = lax.broadcasted_iota(jnp.int32, (k, k), 1)
    eye = (row == col).astype(F32)
    both = gram[...]
    matrix = jnp.concatenate([both[0 : k // 2, 0:k], both[0 : k // 2, k : 2 * k]], axis=0) + eye
    pull = both[k // 2 : k // 2 + 8, 0:k]
    pull = jnp.concatenate([pull, pull], axis=0)
    norm = jnp.sqrt(jnp.sum(jnp.sum(matrix * matrix, axis=1, keepdims=True), axis=0, keepdims=True))

    def one(x, y):
        return jnp.dot(x, y, preferred_element_type=F32)

    def dot(a, b):
        a_high, a_low = split_2(a)
        b_high, b_low = split_2(b)
        rows = a.shape[0]
        both = one(jnp.concatenate([a_high, a_low], axis=0), b_high)
        return both[0:rows] + (both[rows:] + one(a_high, b_low))

    root = matrix / norm
    correction = 1.5 * eye - 0.5 * root
    stacked = dot(jnp.concatenate([root, pull], axis=0), correction)
    root = dot(stacked[0:k], correction)
    carried = jnp.concatenate([correction, stacked[k:]], axis=0)
    for i in range(1, NS_ITERS):
        correction = 1.5 * eye - 0.5 * root
        if i < NS_ITERS - 1:
            root = dot(dot(root, correction), correction)
        carried = dot(carried, correction)
    shift = dot(carried[k:], carried[0:k]) / norm
    weights = carried[0:k] / jnp.sqrt(norm) + shift[0:1, :]
    high, low = split_2(weights)
    high_2 = jnp.concatenate([high, high], axis=1)
    copies = []
    for v in range(nv):
        for r in range(cx):
            deep = 2 <= r < cx - 2
            i = r - 2 if deep else (r if r < 2 else r - cx + 4)
            anomalies = inner if deep else edge
            means = inner_means if deep else edge_means
            at = slice((i * nv + v) * cy, (i * nv + v + 1) * cy)
            value = jnp.dot(high_2, anomalies[:, at], preferred_element_type=F32)
            value = value + jnp.dot(low, anomalies[0:k, at], preferred_element_type=F32)
            value = value + means[i * 8 + v : i * 8 + v + 1, :]
            for h in range(half):
                buf[v * half + h, pl.ds(r, k, stride=cx), :] = value[:, h * LANES : (h + 1) * LANES]
        for h in range(half):
            source = buf.at[v * half + h].reshape(k, cx, LANES)
            target = out.at[:, v, :, h * LANES : (h + 1) * LANES]
            copies.append(pltpu.make_async_copy(source, target, sems.at[v, h]))
            copies[-1].start()
    for copy in copies:
        copy.wait()


def local(sizes, ensemble, diffusivity, mixing, obs_cell, obs_var, obs_value, obs_weight):
    k, nv, cx, cy = ensemble.shape
    dims = (k, nv, cx, cy)
    assert k == 64 and nv == 3 and cx == 8 and cy % LANES == 0
    block = nv * k
    rows = nv * cx
    grp, nx, ny = sizes
    count = obs_cell.shape[2]
    factor = 1.0 / math.sqrt((k - 1) * count * nx * ny)
    limits = pltpu.CompilerParams(vmem_limit_bytes=16 << 20)

    def shape(*dims, dtype=F32):
        return jax.ShapeDtypeStruct(dims, dtype)

    small = (diffusivity, mixing) + tuple(a.reshape(1, count) for a in (obs_cell, obs_var, obs_value, obs_weight))
    state, send_b, sides, side_a, side_b, kappa, mixing, *obs = pl.pallas_call(
        functools.partial(load_kernel, dims),
        name="load",
        in_specs=[pl.BlockSpec(memory_space=pltpu.HBM)] * 7,
        out_specs=[vmem()] * 11,
        out_shape=[
            shape((cx + 4) * block, cy),
            shape(2 * block + 8, cy),
            shape(k + 8, LANES),
            shape(k + 8, LANES),
            shape(k + 8, LANES),
        ]
        + [shape(*a.shape, dtype=a.dtype) for a in small],
        scratch_shapes=[pltpu.VMEM((cy // LANES, k * rows, LANES), F32), pltpu.SemaphoreType.DMA((4, cy // LANES)), pltpu.SemaphoreType.DMA((6,))],
        compiler_params=limits,
    )(
        *(pltpu.with_memory_space_constraint(a, pltpu.HBM) for a in (ensemble.reshape(k * rows, cy),) + small)
    )

    recv_b = x_swap(1, sizes)(send_b)
    side_a = y_swap(0, sizes)(side_a)
    side_b = y_swap(1, sizes)(side_b)

    first, kext, spread, send_a = pl.pallas_call(
        functools.partial(middle_kernel, dims),
        name="middle",
        in_specs=[smem()] + [vmem()] * 6,
        out_specs=[vmem()] * 4,
        out_shape=[
            shape((cx + 2) * block, cy),
            shape((cx + 2) * 8, cy),
            shape(cx * 8, cy),
            shape(2 * block + 8, cy),
        ],
        scratch_shapes=[pltpu.VMEM((64, cy), F32)],
        compiler_params=limits,
    )(mixing, state, kappa, *obs)
    side_a, side_b, first, send_a = lax.optimization_barrier((side_a, side_b, first, send_a))
    recv_a = x_swap(0, sizes)(send_a)
    halo = side_a + side_b
    corner_b = x_swap(1, sizes)(halo)
    corner_a = x_swap(0, sizes)(halo)

    inner_rows = cx - 4
    first, inner_anomalies, inner_means, partial, early = pl.pallas_call(
        functools.partial(inner_kernel, dims, factor),
        name="inner",
        in_specs=[smem()] + [vmem()] * 5,
        out_specs=[vmem()] * 5,
        input_output_aliases={1: 0},
        out_shape=[
            shape((cx + 2) * block, cy),
            shape(2 * k, inner_rows * nv * cy, dtype=BF16),
            shape(inner_rows * 8, cy),
            shape(2 * k + 32, 2 * k),
            shape(2 * block, cy),
        ],
        scratch_shapes=[
            pltpu.VMEM((k, LANES), F32),
            pltpu.VMEM((k, LANES), F32),
            pltpu.VMEM((2 * k + 32, inner_rows * nv * cy), BF16),
            pltpu.VMEM((4 * block, cy), F32),
        ],
        compiler_params=limits,
    )(mixing, first, sides, halo, kext, spread)

    _, _, edge_anomalies, edge_means, gram = pl.pallas_call(
        functools.partial(edge_kernel, dims, factor),
        name="edge",
        in_specs=[smem()] + [vmem()] * 12,
        out_specs=[vmem()] * 5,
        out_shape=[
            shape((cx + 4) * block, cy),
            shape((cx + 2) * block, cy),
            shape(2 * k, 4 * nv * cy, dtype=BF16),
            shape(4 * 8, cy),
            shape(k // 2 + 8, 2 * k),
        ],
        scratch_shapes=[
            pltpu.VMEM(((cx + 2) * 8, cy), F32),
            pltpu.VMEM((k, LANES), F32),
            pltpu.VMEM((k, LANES), F32),
            pltpu.VMEM((2 * k + 32, 4 * nv * cy), BF16),
            pltpu.VMEM((4 * block, cy), F32),
        ],
        input_output_aliases={1: 0, 2: 1},
        compiler_params=limits,
    )(
        mixing, state, first, partial, early, recv_a, recv_b, sides, halo, corner_a, corner_b, kext, spread
    )

    gram = all_sum(gram, sizes)

    return pl.pallas_call(
        functools.partial(apply_kernel, dims),
        name="apply",
        in_specs=[vmem()] * 5,
        out_specs=pl.BlockSpec(memory_space=pltpu.HBM),
        out_shape=shape(k, nv, cx, cy),
        scratch_shapes=[
            pltpu.VMEM((nv * (cy // LANES), k * cx, LANES), F32),
            pltpu.SemaphoreType.DMA((nv, cy // LANES)),
        ],
        compiler_params=limits,
    )(gram, inner_anomalies, inner_means, edge_anomalies, edge_means)


def solution(mesh):
    sizes = tuple(mesh.shape[a] for a in ("grp", "gx", "gy"))
    return jax.shard_map(
        functools.partial(local, sizes),
        mesh=mesh,
        in_specs=(
            P("grp", None, "gx", "gy"),
            P("grp", "gx", "gy"),
            P(),
            P("gx", "gy", "grp"),
            P("gx", "gy", "grp"),
            P("gx", "gy", "grp"),
            P("gx", "gy", "grp"),
        ),
        out_specs=P("grp", None, "gx", "gy"),
        check_vma=False,
    )
```

```python
import functools
import math

import jax
import jax.numpy as jnp
from jax import lax
from jax.experimental import pallas as pl
from jax.experimental.pallas import tpu as pltpu
from jax.sharding import PartitionSpec as P

NS_ITERS = 5
LANES = 128
F32 = jnp.float32
BF16 = jnp.bfloat16


def vmem():
    return pl.BlockSpec(memory_space=pltpu.VMEM)


def smem():
    return pl.BlockSpec(memory_space=pltpu.SMEM)


def nt(a, b):
    return lax.dot_general(a, b, (((1,), (1,)), ((), ())), preferred_element_type=F32)


def split_2(x):
    high = x.astype(BF16)
    return high, (x - high.astype(F32)).astype(BF16)


def split_3(x):
    high = x.astype(BF16)
    rest = x - high.astype(F32)
    middle = rest.astype(BF16)
    return high, middle, (rest - middle.astype(F32)).astype(BF16)


def pair_swap(partner, sizes):
    grp, nx, ny = sizes
    pairs = []
    for g in range(grp):
        for x in range(nx):
            for y in range(ny):
                there = partner(g, x, y)
                if there is not None:
                    tg, tx, ty = there
                    pairs.append(((g * nx + x) * ny + y, (tg * nx + tx) * ny + ty))
    return lambda value: lax.ppermute(value, ("grp", "gx", "gy"), pairs)


def along(place, count, phase):
    first = place - (place - phase) % 2
    if first < 0 or first + 1 >= count:
        return None
    return first + 1 if place == first else first


def x_swap(phase, sizes):
    def partner(g, x, y):
        there = along(x, sizes[1], phase)
        if there is not None:
            return g, there, y
        return (g ^ 1, x, y) if sizes[0] % 2 == 0 else None

    return pair_swap(partner, sizes)


def y_swap(phase, sizes):
    def partner(g, x, y):
        there = along(y, sizes[2], phase)
        if there is not None:
            return g, x, there
        return (g, x ^ 1, y) if sizes[1] % 2 == 0 else None

    return pair_swap(partner, sizes)


def all_sum(value, sizes):
    grp, nx, ny = sizes
    if nx & (nx - 1) or ny & (ny - 1) or nx < 2:
        return lax.psum(value, ("gx", "gy"))

    def chip_swap(mask_0, mask_1):
        def partner(g, x, y):
            chip = ((x >> 1) * ny + y) ^ (mask_1 if x & 1 else mask_0)
            return g, ((chip // ny) << 1) | (x & 1), chip % ny

        return pair_swap(partner, sizes)

    core_swap = pair_swap(lambda g, x, y: (g, x ^ 1, y), sizes)
    chips = nx // 2 * ny
    value = value + core_swap(value)
    if chips == 8:
        parts = [chip_swap(a, b)(value) for a, b in ((4, 4), (1, 5), (2, 6), (3, 7))]
        value = 0.5 * (value + parts[0]) + parts[1] + parts[2] + parts[3]
        return value + core_swap(value)
    step = 1
    while step < chips:
        value = value + chip_swap(step, step)(value)
        step *= 2
    return value


def send_rows(dims, state, kappa, ref, near_top):
    k, nv, cx, cy = dims
    block = nv * k
    gx = lax.axis_index("gx")
    has = jnp.where(near_top, gx > 0, gx < lax.axis_size("gx") - 1)
    near = jnp.where(near_top, 2, cx + 1) * block
    second = jnp.where(near_top, 3, cx) * block
    for j in range(0, block, 64):
        ref[pl.ds(j, 64), :] = jnp.where(has, state[pl.ds(pl.multiple_of(near + j, 64), 64), :], 0.0)
        ref[pl.ds(block + j, 64), :] = jnp.where(has, state[pl.ds(pl.multiple_of(second + j, 64), 64), :], 0.0)
    for v in range(nv):
        edge = jnp.where(near_top, kappa[v, 0:1, :], kappa[v, cx - 1 : cx, :])
        ref[pl.ds(2 * block + v, 1), :] = jnp.where(has, edge, 0.0)
    ref[pl.ds(2 * block + nv, 8 - nv), :] = jnp.zeros((8 - nv, cy), F32)


def load_kernel(dims, ens, *refs):
    small_in, (state, send_a, send_b, sides, side_a, side_b) = refs[:6], refs[6:12]
    small, (buf, sems, small_sems) = refs[12:18], refs[18:]
    kappa = small[0]
    k, nv, cx, cy = dims
    rows = nv * cx
    chunks = 4
    part = k // chunks
    copies = []
    half = cy // LANES
    for c in range(chunks):
        span = pl.ds(c * part * rows, part * rows)
        for h in range(half):
            lanes = slice(h * LANES, (h + 1) * LANES)
            copies.append(pltpu.make_async_copy(ens.at[span, lanes], buf.at[h, span], sems.at[c, h]))
            copies[-1].start()
    small_copies = [pltpu.make_async_copy(a, b, small_sems.at[i]) for i, (a, b) in enumerate(zip(small_in, small))]
    for copy in small_copies:
        copy.start()
    lane = lax.broadcasted_iota(jnp.int32, (1, LANES), 1)

    def add(acc, place, right, left):
        low = (lane >= place) & (lane < place + 2)
        high = (lane >= 64 + place) & (lane < 64 + place + 2)
        acc = jnp.where(low, pltpu.roll(right, (place + 2) % LANES, 1), acc)
        return jnp.where(high, pltpu.roll(left, 64 + place, 1), acc)

    gy = lax.axis_index("gy")
    even_y = gy % 2 == 0
    has_left = gy > 0
    has_right = gy < lax.axis_size("gy") - 1
    wanted = []
    for to_right in (even_y, jnp.logical_not(even_y)):
        start = jnp.where(jnp.where(to_right, has_right, has_left), jnp.where(to_right, 0, 64), LANES)
        wanted.append((lane >= start) & (lane < start + 64))

    def put_sides(at, total):
        sides[at, :] = total
        side_a[at, :] = jnp.where(wanted[0], total, 0.0)
        side_b[at, :] = jnp.where(wanted[1], total, 0.0)

    for c in range(chunks):
        for h in range(half):
            copies[c * half + h].wait()
        total = jnp.zeros((part, LANES), F32)
        for r in range(cx):
            for v in range(nv):
                at = pl.ds(((r + 2) * nv + v) * k + c * part, part)
                values = [buf[h, pl.ds(c * part * rows + v * cx + r, part, stride=rows), :] for h in range(half)]
                for h in range(half):
                    state[at, h * LANES : (h + 1) * LANES] = values[h]
                total = add(total, 2 * (nv * (r + 1) + v), values[-1], values[0])
        put_sides(pl.ds(c * part, part), total)
    for copy in small_copies:
        copy.wait()
    even_x = lax.axis_index("gx") % 2 == 0
    send_rows(dims, state, kappa, send_a, jnp.logical_not(even_x))
    send_rows(dims, state, kappa, send_b, even_x)
    total = jnp.zeros((8, LANES), F32)
    for r in range(cx):
        for v in range(nv):
            row = kappa[v, r : r + 1, :]
            total = add(
                total,
                2 * (nv * (r + 1) + v),
                jnp.broadcast_to(row[:, cy - LANES :], (8, LANES)),
                jnp.broadcast_to(row[:, :LANES], (8, LANES)),
            )
    put_sides(pl.ds(k, 8), total)


def scatter_kernel(dims, cell, var, value, weight, out):
    k, nv, cx, cy = dims
    count = cell.shape[1]
    row = cell[...] // cy * nv + var[...]
    column = cell[...] % cy
    square = weight[...] * weight[...]
    rows = 32
    hit = lax.broadcasted_iota(jnp.int32, (rows, count), 0) == row
    parts = split_3(square) + split_3(square * value[...])
    left = [jnp.where(hit, p.astype(F32), 0.0).astype(BF16) for p in parts]
    one = (lax.broadcasted_iota(jnp.int32, (cy, count), 0) == column).astype(F32).astype(BF16)
    got = nt(jnp.concatenate(left, axis=0), one)
    piece = [got[i * rows : (i + 1) * rows] for i in range(6)]
    out[0:rows, :] = piece[0] + piece[1] + piece[2]
    out[rows : 2 * rows, :] = piece[3] + piece[4] + piece[5]


def first_columns_of(dims, mixing, columns, kcol, own, lane):
    k, nv, cx, cy = dims
    slot = lane % 64
    inside = (slot >= 2 * nv) & (slot < 2 * nv * (cx + 1))
    beside = jnp.where(
        lane < 64,
        pltpu.roll(columns, 1, 1) + pltpu.roll(own, 65, 1),
        pltpu.roll(columns, LANES - 1, 1) + pltpu.roll(own, 63, 1),
    )
    step = 2 * nv
    beside = beside + pltpu.roll(columns, step, 1) + pltpu.roll(columns, LANES - step, 1)
    which = slot // 2 % nv
    mixed = jnp.zeros((k, LANES), F32)
    for shift in range(1 - nv, nv):
        coef = jnp.zeros((1, LANES), F32)
        for v in range(nv):
            if 0 <= v + shift < nv:
                coef = jnp.where(which == v, mixing[v, v + shift], coef)
        source = pltpu.roll(columns, (-2 * shift) % LANES, 1) if shift else columns
        mixed = mixed + coef * source
    return jnp.where(inside, columns + kcol * (beside - 4.0 * columns) + mixed, 0.0)


def advance(dims, mixing, kext, load, side, e, lane, store):
    k, nv, cx, cy = dims
    half = cy // LANES
    eight = pl.ds(e * 8, 8)
    kappas = [kext[eight, h * LANES : (h + 1) * LANES] for h in range(half)]
    first_lane = lane == 0
    last_lane = lane == LANES - 1
    kap = [[jnp.broadcast_to(kappas[h][v : v + 1], (8, LANES)) for h in range(half)] for v in range(nv)]
    own = [[1.0 - 4.0 * kap[v][h] + mixing[v, v] for h in range(half)] for v in range(nv)]
    for j in range(0, k, 8):
        centers = [[load(0, v, j, h) for h in range(half)] for v in range(nv)]
        for v in range(nv):
            center = centers[v]
            shift = (LANES - 1 - 2 * (nv * e + v)) & (LANES - 1)
            edge = 0.0 if side is None else pltpu.roll(side[pl.ds(j, 8), :], shift, 1)
            ahead = [pltpu.roll(c, 1, 1) for c in center]
            behind = [pltpu.roll(c, LANES - 1, 1) for c in center]
            for h in range(half):
                left = jnp.where(first_lane, edge if h == 0 else ahead[h - 1], ahead[h])
                right = jnp.where(last_lane, edge if h == half - 1 else behind[h + 1], behind[h])
                around = (load(-1, v, j, h) + load(1, v, j, h)) + (left + right)
                out = own[v][h] * center[h] + kap[v][h] * around
                for w in range(nv):
                    if w != v:
                        out = out + mixing[v, w] * centers[w][h]
                store(v, j, h, out)


def edges_of(columns, lane):
    return jnp.where(lane % 2 == 0, pltpu.roll(columns, 64, 1), columns)


def loader(ref, base, k, row_size):
    def load(row, w, j, h):
        at = base + row * row_size + w * k + j
        return ref[pl.ds(at, 8), h * LANES : (h + 1) * LANES]

    return load


def first_step(dims, mixing, kext, state, first, side, rows, lane, inside=False):
    k, nv, cx, cy = dims
    block = nv * k
    for e in rows:

        def store(v, j, h, out):
            first[pl.ds(e * block + v * k + j, 8), h * LANES : (h + 1) * LANES] = out

        plain = loader(state, (e + 1) * block, k, block)

        def load(row, w, j, h):
            return 0.0 if inside and not 1 <= e + row <= cx else plain(row, w, j, h)

        advance(dims, mixing, kext, load, side, e, lane, store)


def add_sides(dims, kext, first, side, rows, lane):
    k, nv, cx, cy = dims
    block = nv * k
    ends = ((0, lane == 0), (cy - LANES, lane == LANES - 1))
    for e in rows:
        for v in range(nv):
            shift = (LANES - 1 - 2 * (nv * e + v)) & (LANES - 1)
            kap = []
            for at, here in ends:
                row = jnp.where(here, kext[e * 8 + v : e * 8 + v + 1, at : at + LANES], 0.0)
                kap.append(jnp.broadcast_to(row, (8, LANES)))
            for j in range(0, k, 8):
                edge = pltpu.roll(side[pl.ds(j, 8), :], shift, 1)
                place = pl.ds(e * block + v * k + j, 8)
                for (at, here), factor in zip(ends, kap):
                    first[place, at : at + LANES] += factor * edge


def second_step(dims, mixing, kext, first, first_side, e, ref, slot, lane):
    k, nv, cx, cy = dims
    block = nv * k
    sums = {}

    def store(v, j, h, out):
        ref[pl.ds(slot * block + v * k + j, 8), h * LANES : (h + 1) * LANES] = out
        sums[v, h] = out if j == 0 else sums[v, h] + out

    advance(dims, mixing, kext, loader(first, e * block, k, block), first_side, e, lane, store)
    return sums


def anomalies_of(dims, factor, spread, e, i, sums, kept, outs):
    k, nv, cx, cy = dims
    block = nv * k
    half = cy // LANES
    anomalies, means, moved = outs
    sub = lax.broadcasted_iota(jnp.int32, (8, 1), 0)
    for h in range(half):
        lanes = slice(h * LANES, (h + 1) * LANES)
        spreads = spread[pl.ds((e - 1) * 8, 8), lanes]
        found = jnp.zeros((8, LANES), F32)
        for v in range(nv):
            mean = jnp.sum(sums[v, h], axis=0, keepdims=True) * (1.0 / k)
            found = jnp.where(sub == v, mean, found)
            s2 = spreads[v : v + 1]
            s1 = spreads[nv + v : nv + v + 1]
            at = pl.ds((i * nv + v) * cy + h * LANES, LANES)
            scale = s2 * (factor * factor)
            for j in range(0, k, 16):
                part = kept[pl.ds(i * block + v * k + j, 16), lanes] - mean
                high, low = split_2(part)
                anomalies[j : j + 16, at] = high
                anomalies[k + j : k + j + 16, at] = low
                high, low = split_2(part * scale)
                moved[j : j + 16, at] = high
                moved[k + j : k + j + 16, at] = low
            pull = jnp.broadcast_to((s1 - mean * s2) * factor, (16, LANES))
            high, low = split_2(pull)
            moved[2 * k : 2 * k + 16, at] = high
            moved[2 * k + 16 : 2 * k + 32, at] = low
        means[i * 8 : i * 8 + 8, lanes] = found


def set_kappa(dims, kappa, kext):
    k, nv, cx, cy = dims
    for v in range(nv):
        for r in range(cx):
            kext[pl.ds((r + 1) * 8 + v, 1), :] = kappa[v, r : r + 1, :]


def middle_kernel(dims, mixing, state, kappa, cell, var, value, weight, first, kext, spread, cells):
    k, nv, cx, cy = dims
    scatter_kernel(dims, cell, var, value, weight, cells)
    for v in range(nv):
        for r in range(cx):
            spread[pl.ds(r * 8 + v, 1), :] = cells[pl.ds(r * nv + v, 1), :]
            spread[pl.ds(r * 8 + nv + v, 1), :] = cells[pl.ds(32 + r * nv + v, 1), :]
    set_kappa(dims, kappa, kext)
    lane = lax.broadcasted_iota(jnp.int32, (1, LANES), 1)
    first_step(dims, mixing, kext, state, first, None, range(1, cx + 1), lane, inside=True)


def inner_kernel(
    dims, factor, mixing, first_in, sides, halo, kext, spread,
    first, anomalies, means, partial, early, side, first_side, moved, kept,
):
    k, nv, cx, cy = dims
    lane = lax.broadcasted_iota(jnp.int32, (1, LANES), 1)
    columns = first_columns_of(dims, mixing, halo[0:k, :], halo[k : k + 1, :], sides[0:k, :], lane)
    side[...] = edges_of(halo[0:k, :], lane)
    first_side[...] = edges_of(columns, lane)
    add_sides(dims, kext, first, side, range(1, cx + 1), lane)
    outs = (anomalies, means, moved)
    for i, e in enumerate(range(3, cx - 1)):
        sums = second_step(dims, mixing, kext, first, first_side, e, kept, i, lane)
        anomalies_of(dims, factor, spread, e, i, sums, kept, outs)
    partial[...] = nt(moved[...], anomalies[...])
    second_step(dims, mixing, kext, first, first_side, 2, early, 0, lane)
    second_step(dims, mixing, kext, first, first_side, cx - 1, early, 1, lane)


def edge_kernel(
    dims, factor, mixing, state_in, first_in, partial, early, recv_a, recv_b, sides, halo, corner_a, corner_b, kext_in, spread,
    state, first, anomalies, means, gram, kext, side, first_side, moved, kept,
):
    k, nv, cx, cy = dims
    block = nv * k
    gx = lax.axis_index("gx")
    nx = lax.axis_size("gx")
    down_is_a = gx % 2 == 0

    def both(a, b):
        return jnp.where(down_is_a, b, a), jnp.where(down_is_a, a, b)

    for j in range(0, 2 * block, 32):
        up, down = both(recv_a[pl.ds(j, 32), :], recv_b[pl.ds(j, 32), :])
        state[pl.ds((block if j < block else -block) + j, 32), :] = up
        state[pl.ds((cx + 2) * block + j, 32), :] = down
    up, down = both(recv_a[2 * block : 2 * block + 8, :], recv_b[2 * block : 2 * block + 8, :])
    kext[8 : 8 * (cx + 1), :] = kext_in[8 : 8 * (cx + 1), :]
    kext[0:8, :] = up
    kext[8 * (cx + 1) : 8 * (cx + 2), :] = down

    lane = lax.broadcasted_iota(jnp.int32, (1, LANES), 1)
    slot = lane % 64
    up, down = both(corner_a[...], corner_b[...])
    up = jnp.where(gx > 0, up, 0.0)
    down = jnp.where(gx < nx - 1, down, 0.0)
    far = 2 * nv * cx
    columns = jnp.where(slot < 2 * nv, pltpu.roll(up, LANES - far, 1), halo[...])
    columns = jnp.where((slot >= 2 * nv * (cx + 1)) & (slot < 2 * nv * (cx + 2)), pltpu.roll(down, far, 1), columns)
    side[...] = edges_of(columns[0:k, :], lane)
    columns = first_columns_of(dims, mixing, columns[0:k, :], columns[k : k + 1, :], sides[0:k, :], lane)
    first_side[...] = edges_of(columns, lane)
    first_step(dims, mixing, kext, state, first, side, (0, cx + 1), lane)
    half = cy // LANES
    outs = (anomalies, means, moved)

    def late(e, beyond, near, read, write):
        sums = {}
        for v in range(nv):
            for h in range(half):
                lanes = slice(h * LANES, (h + 1) * LANES)
                row = kext[e * 8 + v : e * 8 + v + 1, lanes]
                if near != e:
                    row = row * kext[near * 8 + v : near * 8 + v + 1, lanes]
                row = jnp.broadcast_to(row, (8, LANES))
                for j in range(0, k, 8):
                    out = read[0][pl.ds(read[1] + v * k + j, 8), lanes]
                    out = out + row * state[pl.ds(beyond * block + v * k + j, 8), lanes]
                    write[0][pl.ds(write[1] + v * k + j, 8), lanes] = out
                    sums[v, h] = out if j == 0 else sums[v, h] + out
        return sums

    for e, beyond in ((1, 1), (cx, cx + 2)):
        late(e, beyond, e, (first, e * block), (first, e * block))
    for i, e in enumerate((1, 2, cx - 1, cx)):
        if i in (0, 3):
            sums = second_step(dims, mixing, kext, first, first_side, e, kept, i, lane)
        elif i == 1:
            sums = late(e, 1, 1, (early, 0), (kept, i * block))
        else:
            sums = late(e, cx + 2, cx, (early, block), (kept, i * block))
        anomalies_of(dims, factor, spread, e, i, sums, kept, outs)
    got = partial[...] + nt(moved[...], anomalies[...])
    whole = got[:, 0:k] + got[:, k : 2 * k]
    matrix = whole[0:k] + whole[k : 2 * k]
    pull = whole[2 * k : 2 * k + 8] + whole[2 * k + 16 : 2 * k + 24]
    gram[0 : k // 2, :] = jnp.concatenate([matrix[0 : k // 2], matrix[k // 2 :]], axis=1)
    gram[k // 2 : k // 2 + 8, :] = jnp.concatenate([pull, pull], axis=1)


def apply_kernel(dims, gram, inner, inner_means, edge, edge_means, out, buf, sems):
    k, nv, cx, cy = dims
    half = cy // LANES
    row = lax.broadcasted_iota(jnp.int32, (k, k), 0)
    col = lax.broadcasted_iota(jnp.int32, (k, k), 1)
    eye = (row == col).astype(F32)
    both = gram[...]
    matrix = jnp.concatenate([both[0 : k // 2, 0:k], both[0 : k // 2, k : 2 * k]], axis=0) + eye
    pull = both[k // 2 : k // 2 + 8, 0:k]
    pull = jnp.concatenate([pull, pull], axis=0)
    norm = jnp.sqrt(jnp.sum(jnp.sum(matrix * matrix, axis=1, keepdims=True), axis=0, keepdims=True))

    def one(x, y):
        return jnp.dot(x, y, preferred_element_type=F32)

    def dot(a, b):
        a_high, a_low = split_2(a)
        b_high, b_low = split_2(b)
        rows = a.shape[0]
        both = one(jnp.concatenate([a_high, a_low], axis=0), b_high)
        return both[0:rows] + (both[rows:] + one(a_high, b_low))

    root = matrix / norm
    correction = 1.5 * eye - 0.5 * root
    stacked = dot(jnp.concatenate([root, pull], axis=0), correction)
    root = dot(stacked[0:k], correction)
    carried = jnp.concatenate([correction, stacked[k:]], axis=0)
    for i in range(1, NS_ITERS):
        correction = 1.5 * eye - 0.5 * root
        if i < NS_ITERS - 1:
            root = dot(dot(root, correction), correction)
        carried = dot(carried, correction)
    shift = dot(carried[k:], carried[0:k]) / norm
    weights = carried[0:k] / jnp.sqrt(norm) + shift[0:1, :]
    high, low = split_2(weights)
    high_2 = jnp.concatenate([high, high], axis=1)
    copies = []
    for v in range(nv):
        for r in range(cx):
            deep = 2 <= r < cx - 2
            i = r - 2 if deep else (r if r < 2 else r - cx + 4)
            anomalies = inner if deep else edge
            means = inner_means if deep else edge_means
            at = slice((i * nv + v) * cy, (i * nv + v + 1) * cy)
            value = jnp.dot(high_2, anomalies[:, at], preferred_element_type=F32)
            value = value + jnp.dot(low, anomalies[0:k, at], preferred_element_type=F32)
            value = value + means[i * 8 + v : i * 8 + v + 1, :]
            for h in range(half):
                buf[v * half + h, pl.ds(r, k, stride=cx), :] = value[:, h * LANES : (h + 1) * LANES]
        for h in range(half):
            source = buf.at[v * half + h].reshape(k, cx, LANES)
            target = out.at[:, v, :, h * LANES : (h + 1) * LANES]
            copies.append(pltpu.make_async_copy(source, target, sems.at[v, h]))
            copies[-1].start()
    for copy in copies:
        copy.wait()


def local(sizes, ensemble, diffusivity, mixing, obs_cell, obs_var, obs_value, obs_weight):
    k, nv, cx, cy = ensemble.shape
    dims = (k, nv, cx, cy)
    assert k == 64 and nv == 3 and cx == 8 and cy % LANES == 0
    block = nv * k
    rows = nv * cx
    grp, nx, ny = sizes
    count = obs_cell.shape[2]
    factor = 1.0 / math.sqrt((k - 1) * count * nx * ny)
    limits = pltpu.CompilerParams(vmem_limit_bytes=16 << 20)

    def shape(*dims, dtype=F32):
        return jax.ShapeDtypeStruct(dims, dtype)

    small = (diffusivity, mixing) + tuple(a.reshape(1, count) for a in (obs_cell, obs_var, obs_value, obs_weight))
    state, send_a, send_b, sides, side_a, side_b, kappa, mixing, *obs = pl.pallas_call(
        functools.partial(load_kernel, dims),
        name="load",
        in_specs=[pl.BlockSpec(memory_space=pltpu.HBM)] * 7,
        out_specs=[vmem()] * 12,
        out_shape=[
            shape((cx + 4) * block, cy),
            shape(2 * block + 8, cy),
            shape(2 * block + 8, cy),
            shape(k + 8, LANES),
            shape(k + 8, LANES),
            shape(k + 8, LANES),
        ]
        + [shape(*a.shape, dtype=a.dtype) for a in small],
        scratch_shapes=[pltpu.VMEM((cy // LANES, k * rows, LANES), F32), pltpu.SemaphoreType.DMA((4, cy // LANES)), pltpu.SemaphoreType.DMA((6,))],
        compiler_params=limits,
    )(
        *(pltpu.with_memory_space_constraint(a, pltpu.HBM) for a in (ensemble.reshape(k * rows, cy),) + small)
    )

    recv_b = x_swap(1, sizes)(send_b)
    side_a = y_swap(0, sizes)(side_a)
    side_b = y_swap(1, sizes)(side_b)
    recv_a = x_swap(0, sizes)(send_a)

    first, kext, spread = pl.pallas_call(
        functools.partial(middle_kernel, dims),
        name="middle",
        in_specs=[smem()] + [vmem()] * 6,
        out_specs=[vmem()] * 3,
        out_shape=[shape((cx + 2) * block, cy), shape((cx + 2) * 8, cy), shape(cx * 8, cy)],
        scratch_shapes=[pltpu.VMEM((64, cy), F32)],
        compiler_params=limits,
    )(mixing, state, kappa, *obs)
    side_a, side_b, first = lax.optimization_barrier((side_a, side_b, first))
    halo = side_a + side_b
    corner_b = x_swap(1, sizes)(halo)
    corner_a = x_swap(0, sizes)(halo)

    inner_rows = cx - 4
    first, inner_anomalies, inner_means, partial, early = pl.pallas_call(
        functools.partial(inner_kernel, dims, factor),
        name="inner",
        in_specs=[smem()] + [vmem()] * 5,
        out_specs=[vmem()] * 5,
        input_output_aliases={1: 0},
        out_shape=[
            shape((cx + 2) * block, cy),
            shape(2 * k, inner_rows * nv * cy, dtype=BF16),
            shape(inner_rows * 8, cy),
            shape(2 * k + 32, 2 * k),
            shape(2 * block, cy),
        ],
        scratch_shapes=[
            pltpu.VMEM((k, LANES), F32),
            pltpu.VMEM((k, LANES), F32),
            pltpu.VMEM((2 * k + 32, inner_rows * nv * cy), BF16),
            pltpu.VMEM((4 * block, cy), F32),
        ],
        compiler_params=limits,
    )(mixing, first, sides, halo, kext, spread)

    _, _, edge_anomalies, edge_means, gram = pl.pallas_call(
        functools.partial(edge_kernel, dims, factor),
        name="edge",
        in_specs=[smem()] + [vmem()] * 12,
        out_specs=[vmem()] * 5,
        out_shape=[
            shape((cx + 4) * block, cy),
            shape((cx + 2) * block, cy),
            shape(2 * k, 4 * nv * cy, dtype=BF16),
            shape(4 * 8, cy),
            shape(k // 2 + 8, 2 * k),
        ],
        scratch_shapes=[
            pltpu.VMEM(((cx + 2) * 8, cy), F32),
            pltpu.VMEM((k, LANES), F32),
            pltpu.VMEM((k, LANES), F32),
            pltpu.VMEM((2 * k + 32, 4 * nv * cy), BF16),
            pltpu.VMEM((4 * block, cy), F32),
        ],
        input_output_aliases={1: 0, 2: 1},
        compiler_params=limits,
    )(
        mixing, state, first, partial, early, recv_a, recv_b, sides, halo, corner_a, corner_b, kext, spread
    )

    gram = all_sum(gram, sizes)

    return pl.pallas_call(
        functools.partial(apply_kernel, dims),
        name="apply",
        in_specs=[vmem()] * 5,
        out_specs=pl.BlockSpec(memory_space=pltpu.HBM),
        out_shape=shape(k, nv, cx, cy),
        scratch_shapes=[
            pltpu.VMEM((nv * (cy // LANES), k * cx, LANES), F32),
            pltpu.SemaphoreType.DMA((nv, cy // LANES)),
        ],
        compiler_params=limits,
    )(gram, inner_anomalies, inner_means, edge_anomalies, edge_means)


def solution(mesh):
    sizes = tuple(mesh.shape[a] for a in ("grp", "gx", "gy"))
    return jax.shard_map(
        functools.partial(local, sizes),
        mesh=mesh,
        in_specs=(
            P("grp", None, "gx", "gy"),
            P("grp", "gx", "gy"),
            P(),
            P("gx", "gy", "grp"),
            P("gx", "gy", "grp"),
            P("gx", "gy", "grp"),
            P("gx", "gy", "grp"),
        ),
        out_specs=P("grp", None, "gx", "gy"),
        check_vma=False,
    )
```

```python
import functools
import math

import jax
import jax.numpy as jnp
from jax import lax
from jax.experimental import pallas as pl
from jax.experimental.pallas import tpu as pltpu
from jax.sharding import PartitionSpec as P

NS_ITERS = 5
LANES = 128
F32 = jnp.float32
BF16 = jnp.bfloat16


def vmem():
    return pl.BlockSpec(memory_space=pltpu.VMEM)


def smem():
    return pl.BlockSpec(memory_space=pltpu.SMEM)


def nt(a, b):
    return lax.dot_general(a, b, (((1,), (1,)), ((), ())), preferred_element_type=F32)


def split_2(x):
    high = x.astype(BF16)
    return high, (x - high.astype(F32)).astype(BF16)


def split_3(x):
    high = x.astype(BF16)
    rest = x - high.astype(F32)
    middle = rest.astype(BF16)
    return high, middle, (rest - middle.astype(F32)).astype(BF16)


def pair_swap(partner, sizes):
    grp, nx, ny = sizes
    pairs = []
    for g in range(grp):
        for x in range(nx):
            for y in range(ny):
                there = partner(g, x, y)
                if there is not None:
                    tg, tx, ty = there
                    pairs.append(((g * nx + x) * ny + y, (tg * nx + tx) * ny + ty))
    return lambda value: lax.ppermute(value, ("grp", "gx", "gy"), pairs)


def along(place, count, phase):
    first = place - (place - phase) % 2
    if first < 0 or first + 1 >= count:
        return None
    return first + 1 if place == first else first


def x_swap(phase, sizes):
    def partner(g, x, y):
        there = along(x, sizes[1], phase)
        if there is not None:
            return g, there, y
        return (g ^ 1, x, y) if sizes[0] % 2 == 0 else None

    return pair_swap(partner, sizes)


def y_swap(phase, sizes):
    def partner(g, x, y):
        there = along(y, sizes[2], phase)
        if there is not None:
            return g, x, there
        return (g, x ^ 1, y) if sizes[1] % 2 == 0 else None

    return pair_swap(partner, sizes)


def all_sum(value, sizes):
    grp, nx, ny = sizes
    if nx & (nx - 1) or ny & (ny - 1) or nx < 2:
        return lax.psum(value, ("gx", "gy"))

    def chip_swap(mask_0, mask_1):
        def partner(g, x, y):
            chip = ((x >> 1) * ny + y) ^ (mask_1 if x & 1 else mask_0)
            return g, ((chip // ny) << 1) | (x & 1), chip % ny

        return pair_swap(partner, sizes)

    core_swap = pair_swap(lambda g, x, y: (g, x ^ 1, y), sizes)
    chips = nx // 2 * ny
    value = value + core_swap(value)
    if chips == 8:
        parts = [chip_swap(a, b)(value) for a, b in ((2, 6), (1, 5), (4, 4), (3, 7))]
        value = parts[0] + parts[1] + 0.5 * (value + parts[2]) + parts[3]
        return value + core_swap(value)
    step = 1
    while step < chips:
        value = value + chip_swap(step, step)(value)
        step *= 2
    return value


def send_rows(dims, state, kappa, ref, near_top):
    k, nv, cx, cy = dims
    block = nv * k
    gx = lax.axis_index("gx")
    has = jnp.where(near_top, gx > 0, gx < lax.axis_size("gx") - 1)
    near = jnp.where(near_top, 2, cx + 1) * block
    second = jnp.where(near_top, 3, cx) * block
    for j in range(0, block, 64):
        ref[pl.ds(j, 64), :] = jnp.where(has, state[pl.ds(pl.multiple_of(near + j, 64), 64), :], 0.0)
        ref[pl.ds(block + j, 64), :] = jnp.where(has, state[pl.ds(pl.multiple_of(second + j, 64), 64), :], 0.0)
    for v in range(nv):
        edge = jnp.where(near_top, kappa[v, 0:1, :], kappa[v, cx - 1 : cx, :])
        ref[pl.ds(2 * block + v, 1), :] = jnp.where(has, edge, 0.0)
    ref[pl.ds(2 * block + nv, 8 - nv), :] = jnp.zeros((8 - nv, cy), F32)


def load_kernel(dims, ens, *refs):
    small_in, (state, send_a, send_b, sides, side_a, side_b) = refs[:6], refs[6:12]
    small, (buf, sems, small_sems) = refs[12:18], refs[18:]
    kappa = small[0]
    k, nv, cx, cy = dims
    rows = nv * cx
    chunks = 4
    part = k // chunks
    copies = []
    half = cy // LANES
    for c in range(chunks):
        span = pl.ds(c * part * rows, part * rows)
        for h in range(half):
            lanes = slice(h * LANES, (h + 1) * LANES)
            copies.append(pltpu.make_async_copy(ens.at[span, lanes], buf.at[h, span], sems.at[c, h]))
            copies[-1].start()
    small_copies = [pltpu.make_async_copy(a, b, small_sems.at[i]) for i, (a, b) in enumerate(zip(small_in, small))]
    for copy in small_copies:
        copy.start()
    lane = lax.broadcasted_iota(jnp.int32, (1, LANES), 1)

    def add(acc, place, right, left):
        low = (lane >= place) & (lane < place + 2)
        high = (lane >= 64 + place) & (lane < 64 + place + 2)
        acc = jnp.where(low, pltpu.roll(right, (place + 2) % LANES, 1), acc)
        return jnp.where(high, pltpu.roll(left, 64 + place, 1), acc)

    gy = lax.axis_index("gy")
    even_y = gy % 2 == 0
    has_left = gy > 0
    has_right = gy < lax.axis_size("gy") - 1
    wanted = []
    for to_right in (even_y, jnp.logical_not(even_y)):
        start = jnp.where(jnp.where(to_right, has_right, has_left), jnp.where(to_right, 0, 64), LANES)
        wanted.append((lane >= start) & (lane < start + 64))

    def put_sides(at, total):
        sides[at, :] = total
        side_a[at, :] = jnp.where(wanted[0], total, 0.0)
        side_b[at, :] = jnp.where(wanted[1], total, 0.0)

    for c in range(chunks):
        for h in range(half):
            copies[c * half + h].wait()
        total = jnp.zeros((part, LANES), F32)
        for r in range(cx):
            for v in range(nv):
                at = pl.ds(((r + 2) * nv + v) * k + c * part, part)
                values = [buf[h, pl.ds(c * part * rows + v * cx + r, part, stride=rows), :] for h in range(half)]
                for h in range(half):
                    state[at, h * LANES : (h + 1) * LANES] = values[h]
                total = add(total, 2 * (nv * (r + 1) + v), values[-1], values[0])
        put_sides(pl.ds(c * part, part), total)
    for copy in small_copies:
        copy.wait()
    even_x = lax.axis_index("gx") % 2 == 0
    send_rows(dims, state, kappa, send_a, jnp.logical_not(even_x))
    send_rows(dims, state, kappa, send_b, even_x)
    total = jnp.zeros((8, LANES), F32)
    for r in range(cx):
        for v in range(nv):
            row = kappa[v, r : r + 1, :]
            total = add(
                total,
                2 * (nv * (r + 1) + v),
                jnp.broadcast_to(row[:, cy - LANES :], (8, LANES)),
                jnp.broadcast_to(row[:, :LANES], (8, LANES)),
            )
    put_sides(pl.ds(k, 8), total)


def scatter_kernel(dims, cell, var, value, weight, out):
    k, nv, cx, cy = dims
    count = cell.shape[1]
    row = cell[...] // cy * nv + var[...]
    column = cell[...] % cy
    square = weight[...] * weight[...]
    rows = 32
    hit = lax.broadcasted_iota(jnp.int32, (rows, count), 0) == row
    parts = split_3(square) + split_3(square * value[...])
    left = [jnp.where(hit, p.astype(F32), 0.0).astype(BF16) for p in parts]
    one = (lax.broadcasted_iota(jnp.int32, (cy, count), 0) == column).astype(F32).astype(BF16)
    got = nt(jnp.concatenate(left, axis=0), one)
    piece = [got[i * rows : (i + 1) * rows] for i in range(6)]
    out[0:rows, :] = piece[0] + piece[1] + piece[2]
    out[rows : 2 * rows, :] = piece[3] + piece[4] + piece[5]


def mixed_columns(dims, mixing, columns, lane):
    k, nv, cx, cy = dims
    which = lane % 64 // 2 % nv
    mixed = jnp.zeros((k, LANES), F32)
    for shift in range(1 - nv, nv):
        coef = jnp.zeros((1, LANES), F32)
        for v in range(nv):
            if 0 <= v + shift < nv:
                coef = jnp.where(which == v, mixing[v, v + shift], coef)
        source = pltpu.roll(columns, (-2 * shift) % LANES, 1) if shift else columns
        mixed = mixed + coef * source
    return mixed


def first_columns_of(dims, mixing, columns, kcol, own, lane):
    k, nv, cx, cy = dims
    slot = lane % 64
    inside = (slot >= 2 * nv) & (slot < 2 * nv * (cx + 1))
    beside = jnp.where(
        lane < 64,
        pltpu.roll(columns, 1, 1) + pltpu.roll(own, 65, 1),
        pltpu.roll(columns, LANES - 1, 1) + pltpu.roll(own, 63, 1),
    )
    step = 2 * nv
    beside = beside + pltpu.roll(columns, step, 1) + pltpu.roll(columns, LANES - step, 1)
    mixed = mixed_columns(dims, mixing, columns, lane)
    return jnp.where(inside, columns + kcol * (beside - 4.0 * columns) + mixed, 0.0)


def late_columns_of(dims, mixing, columns, first_columns, kown, lane):
    k, nv, cx, cy = dims
    slot = lane % 64
    inside = (slot >= 2 * nv) & (slot < 2 * nv * (cx + 1))
    parity = jnp.where(lane < 64, 1, 0)
    outermost = inside & (lane % 2 == parity)

    def moved(x):
        return jnp.where(lane < 64, pltpu.roll(x, 65, 1), pltpu.roll(x, 63, 1))

    added = jnp.where(outermost, kown * moved(columns), 0.0)
    step = 2 * nv
    beside = pltpu.roll(added, step, 1) + pltpu.roll(added, LANES - step, 1) + moved(first_columns)
    outer = added + kown * (beside - 4.0 * added) + mixed_columns(dims, mixing, added, lane)
    inner = kown * jnp.where(lane < 64, pltpu.roll(added, LANES - 1, 1), pltpu.roll(added, 1, 1))
    return jnp.where(outermost, outer, jnp.where(inside, inner, 0.0))


def advance(dims, mixing, kext, load, side, e, lane, store):
    k, nv, cx, cy = dims
    half = cy // LANES
    eight = pl.ds(e * 8, 8)
    kappas = [kext[eight, h * LANES : (h + 1) * LANES] for h in range(half)]
    first_lane = lane == 0
    last_lane = lane == LANES - 1
    kap = [[jnp.broadcast_to(kappas[h][v : v + 1], (8, LANES)) for h in range(half)] for v in range(nv)]
    own = [[1.0 - 4.0 * kap[v][h] + mixing[v, v] for h in range(half)] for v in range(nv)]
    for j in range(0, k, 8):
        centers = [[load(0, v, j, h) for h in range(half)] for v in range(nv)]
        for v in range(nv):
            center = centers[v]
            shift = (LANES - 1 - 2 * (nv * e + v)) & (LANES - 1)
            edge = 0.0 if side is None else pltpu.roll(side[pl.ds(j, 8), :], shift, 1)
            ahead = [pltpu.roll(c, 1, 1) for c in center]
            behind = [pltpu.roll(c, LANES - 1, 1) for c in center]
            for h in range(half):
                left = jnp.where(first_lane, edge if h == 0 else ahead[h - 1], ahead[h])
                right = jnp.where(last_lane, edge if h == half - 1 else behind[h + 1], behind[h])
                around = (load(-1, v, j, h) + load(1, v, j, h)) + (left + right)
                out = own[v][h] * center[h] + kap[v][h] * around
                for w in range(nv):
                    if w != v:
                        out = out + mixing[v, w] * centers[w][h]
                store(v, j, h, out)


def edges_of(columns, lane):
    return jnp.where(lane % 2 == 0, pltpu.roll(columns, 64, 1), columns)


def loader(ref, base, k, row_size):
    def load(row, w, j, h):
        at = base + row * row_size + w * k + j
        return ref[pl.ds(at, 8), h * LANES : (h + 1) * LANES]

    return load


def first_step(dims, mixing, kext, state, first, side, rows, lane, inside=False):
    k, nv, cx, cy = dims
    block = nv * k
    for e in rows:

        def store(v, j, h, out):
            first[pl.ds(e * block + v * k + j, 8), h * LANES : (h + 1) * LANES] = out

        plain = loader(state, (e + 1) * block, k, block)

        def load(row, w, j, h):
            return 0.0 if inside and not 1 <= e + row <= cx else plain(row, w, j, h)

        advance(dims, mixing, kext, load, side, e, lane, store)


def add_sides(dims, kext, first, side, rows, lane):
    k, nv, cx, cy = dims
    block = nv * k
    ends = ((0, lane == 0), (cy - LANES, lane == LANES - 1))
    for e in rows:
        for v in range(nv):
            shift = (LANES - 1 - 2 * (nv * e + v)) & (LANES - 1)
            kap = []
            for at, here in ends:
                row = jnp.where(here, kext[e * 8 + v : e * 8 + v + 1, at : at + LANES], 0.0)
                kap.append(jnp.broadcast_to(row, (8, LANES)))
            for j in range(0, k, 8):
                edge = pltpu.roll(side[pl.ds(j, 8), :], shift, 1)
                place = pl.ds(e * block + v * k + j, 8)
                for (at, here), factor in zip(ends, kap):
                    first[place, at : at + LANES] += factor * edge


def second_step(dims, mixing, kext, first, first_side, e, ref, slot, lane):
    k, nv, cx, cy = dims
    block = nv * k
    sums = {}

    def store(v, j, h, out):
        ref[pl.ds(slot * block + v * k + j, 8), h * LANES : (h + 1) * LANES] = out
        sums[v, h] = out if j == 0 else sums[v, h] + out

    advance(dims, mixing, kext, loader(first, e * block, k, block), first_side, e, lane, store)
    return sums


def anomalies_of(dims, factor, spread, e, i, sums, kept, outs):
    k, nv, cx, cy = dims
    block = nv * k
    half = cy // LANES
    anomalies, means, moved = outs
    sub = lax.broadcasted_iota(jnp.int32, (8, 1), 0)
    for h in range(half):
        lanes = slice(h * LANES, (h + 1) * LANES)
        spreads = spread[pl.ds((e - 1) * 8, 8), lanes]
        found = jnp.zeros((8, LANES), F32)
        for v in range(nv):
            mean = jnp.sum(sums[v, h], axis=0, keepdims=True) * (1.0 / k)
            found = jnp.where(sub == v, mean, found)
            s2 = spreads[v : v + 1]
            s1 = spreads[nv + v : nv + v + 1]
            at = pl.ds((i * nv + v) * cy + h * LANES, LANES)
            scale = s2 * (factor * factor)
            for j in range(0, k, 16):
                part = kept[pl.ds(i * block + v * k + j, 16), lanes] - mean
                high, low = split_2(part)
                anomalies[j : j + 16, at] = high
                anomalies[k + j : k + j + 16, at] = low
                high, low = split_2(part * scale)
                moved[j : j + 16, at] = high
                moved[k + j : k + j + 16, at] = low
            pull = jnp.broadcast_to((s1 - mean * s2) * factor, (16, LANES))
            high, low = split_2(pull)
            moved[2 * k : 2 * k + 16, at] = high
            moved[2 * k + 16 : 2 * k + 32, at] = low
        means[i * 8 : i * 8 + 8, lanes] = found


def set_kappa(dims, kappa, kext):
    k, nv, cx, cy = dims
    for v in range(nv):
        for r in range(cx):
            kext[pl.ds((r + 1) * 8 + v, 1), :] = kappa[v, r : r + 1, :]


def middle_kernel(dims, mixing, state, kappa, cell, var, value, weight, first, kext, spread, early, cells):
    k, nv, cx, cy = dims
    scatter_kernel(dims, cell, var, value, weight, cells)
    for v in range(nv):
        for r in range(cx):
            spread[pl.ds(r * 8 + v, 1), :] = cells[pl.ds(r * nv + v, 1), :]
            spread[pl.ds(r * 8 + nv + v, 1), :] = cells[pl.ds(32 + r * nv + v, 1), :]
    set_kappa(dims, kappa, kext)
    lane = lax.broadcasted_iota(jnp.int32, (1, LANES), 1)
    first_step(dims, mixing, kext, state, first, None, range(1, cx + 1), lane, inside=True)
    for e in range(2, cx):
        second_step(dims, mixing, kext, first, None, e, early, e - 2, lane)


def inner_kernel(
    dims, factor, mixing, first_in, early, sides, halo, kext, spread,
    first, anomalies, means, partial, late, side, late_side, moved, kept,
):
    k, nv, cx, cy = dims
    block = nv * k
    half = cy // LANES
    lane = lax.broadcasted_iota(jnp.int32, (1, LANES), 1)
    columns = halo[0:k, :]
    first_columns = first_columns_of(dims, mixing, columns, halo[k : k + 1, :], sides[0:k, :], lane)
    side[...] = edges_of(columns, lane)
    late_side[...] = late_columns_of(dims, mixing, columns, first_columns, sides[k : k + 1, :], lane)

    def with_sides(e, ref, slot):
        sums = {}
        for v in range(nv):
            at = 2 * (nv * e + v)
            for j in range(0, k, 8):
                extra = late_side[pl.ds(j, 8), :]
                for h in range(half):
                    lanes = slice(h * LANES, (h + 1) * LANES)
                    out = early[pl.ds((e - 2) * block + v * k + j, 8), lanes]
                    if h == 0:
                        out = out + jnp.where(lane < 2, pltpu.roll(extra, 64 - at, 1), 0.0)
                    if h == half - 1:
                        out = out + jnp.where(lane >= LANES - 2, pltpu.roll(extra, LANES - 2 - at, 1), 0.0)
                    ref[pl.ds(slot * block + v * k + j, 8), lanes] = out
                    sums[v, h] = out if j == 0 else sums[v, h] + out
        return sums

    outs = (anomalies, means, moved)
    for i, e in enumerate(range(3, cx - 1)):
        sums = with_sides(e, kept, i)
        anomalies_of(dims, factor, spread, e, i, sums, kept, outs)
    partial[...] = nt(moved[...], anomalies[...])
    with_sides(2, late, 0)
    with_sides(cx - 1, late, 1)
    add_sides(dims, kext, first, side, (1, 2, cx - 1, cx), lane)


def rows_kernel(
    dims, factor, mixing, state_in, first_in, partial, late_in, recv_a, recv_b, sides, halo, kext_in, spread,
    state, first, anomalies, means, more, outer, kext, side, first_side, moved, kept,
):
    k, nv, cx, cy = dims
    block = nv * k
    half = cy // LANES
    down_is_a = lax.axis_index("gx") % 2 == 0

    def both(a, b):
        return jnp.where(down_is_a, b, a), jnp.where(down_is_a, a, b)

    for j in range(0, 2 * block, 32):
        up, down = both(recv_a[pl.ds(j, 32), :], recv_b[pl.ds(j, 32), :])
        state[pl.ds((block if j < block else -block) + j, 32), :] = up
        state[pl.ds((cx + 2) * block + j, 32), :] = down
    up, down = both(recv_a[2 * block : 2 * block + 8, :], recv_b[2 * block : 2 * block + 8, :])
    kext[8 : 8 * (cx + 1), :] = kext_in[8 : 8 * (cx + 1), :]
    kext[0:8, :] = up
    kext[8 * (cx + 1) : 8 * (cx + 2), :] = down

    lane = lax.broadcasted_iota(jnp.int32, (1, LANES), 1)
    columns = halo[0:k, :]
    side[...] = edges_of(columns, lane)
    columns = first_columns_of(dims, mixing, columns, halo[k : k + 1, :], sides[0:k, :], lane)
    first_side[...] = edges_of(columns, lane)
    first_step(dims, mixing, kext, state, first, side, (0, cx + 1), lane)

    def late(e, beyond, near, read, write):
        sums = {}
        for v in range(nv):
            for h in range(half):
                lanes = slice(h * LANES, (h + 1) * LANES)
                row = kext[e * 8 + v : e * 8 + v + 1, lanes]
                if near != e:
                    row = row * kext[near * 8 + v : near * 8 + v + 1, lanes]
                row = jnp.broadcast_to(row, (8, LANES))
                for j in range(0, k, 8):
                    out = read[0][pl.ds(read[1] + v * k + j, 8), lanes]
                    out = out + row * state[pl.ds(beyond * block + v * k + j, 8), lanes]
                    write[0][pl.ds(write[1] + v * k + j, 8), lanes] = out
                    sums[v, h] = out if j == 0 else sums[v, h] + out
        return sums

    for i, (e, beyond) in enumerate(((1, 1), (cx, cx + 2))):
        late(e, beyond, e, (first, e * block), (first, e * block))
        second_step(dims, mixing, kext, first, first_side, e, outer, i, lane)
    for i, (e, beyond, near) in enumerate(((2, 1, 1), (cx - 1, cx + 2, cx))):
        sums = late(e, beyond, near, (late_in, i * block), (kept, i * block))
        anomalies_of(dims, factor, spread, e, i, sums, kept, (anomalies, means, moved))
    more[...] = partial[...] + nt(moved[...], anomalies[...])


def corner_kernel(
    dims, factor, outer, partial, halo, corner_a, corner_b, kext, spread,
    anomalies, means, gram, side_up, side_down, moved, kept,
):
    k, nv, cx, cy = dims
    block = nv * k
    half = cy // LANES
    gx = lax.axis_index("gx")
    down_is_a = gx % 2 == 0
    lane = lax.broadcasted_iota(jnp.int32, (1, LANES), 1)
    a = corner_a[0:k, :]
    b = corner_b[0:k, :]
    side_up[...] = edges_of(jnp.where(gx > 0, jnp.where(down_is_a, b, a), 0.0), lane)
    side_down[...] = edges_of(jnp.where(gx < lax.axis_size("gx") - 1, jnp.where(down_is_a, a, b), 0.0), lane)
    kside = edges_of(halo[k : k + 8, :], lane)

    def to_ends(x, e, v):
        return pltpu.roll(x, (LANES - 1 - 2 * (nv * e + v)) & (LANES - 1), 1)

    for i, (e, beyond, source, there) in enumerate(((1, 0, side_up, cx), (cx, cx + 1, side_down, 1))):
        sums = {}
        for v in range(nv):
            kend = to_ends(kside, e, v)[0:1]
            factors = {}
            for h in (0, half - 1):
                lanes = slice(h * LANES, (h + 1) * LANES)
                here = (lane == 0) if h == 0 else (lane == LANES - 1)
                row = kext[e * 8 + v : e * 8 + v + 1, lanes] * (kext[beyond * 8 + v : beyond * 8 + v + 1, lanes] + kend)
                factors[h] = jnp.broadcast_to(jnp.where(here, row, 0.0), (8, LANES))
            for j in range(0, k, 8):
                corner = to_ends(source[pl.ds(j, 8), :], there, v)
                for h in range(half):
                    lanes = slice(h * LANES, (h + 1) * LANES)
                    place = pl.ds(i * block + v * k + j, 8)
                    out = outer[place, lanes]
                    if h in factors:
                        out = out + factors[h] * corner
                    kept[place, lanes] = out
                    sums[v, h] = out if j == 0 else sums[v, h] + out
        anomalies_of(dims, factor, spread, e, i, sums, kept, (anomalies, means, moved))
    got = partial[...] + nt(moved[...], anomalies[...])
    whole = got[:, 0:k] + got[:, k : 2 * k]
    matrix = whole[0:k] + whole[k : 2 * k]
    pull = whole[2 * k : 2 * k + 8] + whole[2 * k + 16 : 2 * k + 24]
    gram[0 : k // 2, :] = jnp.concatenate([matrix[0 : k // 2], matrix[k // 2 :]], axis=1)
    gram[k // 2 : k // 2 + 8, :] = jnp.concatenate([pull, pull], axis=1)


def apply_kernel(dims, gram, inner, inner_means, near, near_means, edge, edge_means, out, buf, sems):
    k, nv, cx, cy = dims
    half = cy // LANES
    row = lax.broadcasted_iota(jnp.int32, (k, k), 0)
    col = lax.broadcasted_iota(jnp.int32, (k, k), 1)
    eye = (row == col).astype(F32)
    both = gram[...]
    matrix = jnp.concatenate([both[0 : k // 2, 0:k], both[0 : k // 2, k : 2 * k]], axis=0) + eye
    pull = both[k // 2 : k // 2 + 8, 0:k]
    pull = jnp.concatenate([pull, pull], axis=0)
    norm = jnp.sqrt(jnp.sum(jnp.sum(matrix * matrix, axis=1, keepdims=True), axis=0, keepdims=True))

    def one(x, y):
        return jnp.dot(x, y, preferred_element_type=F32)

    def dot(a, b):
        a_high, a_low = split_2(a)
        b_high, b_low = split_2(b)
        rows = a.shape[0]
        both = one(jnp.concatenate([a_high, a_low], axis=0), b_high)
        return both[0:rows] + (both[rows:] + one(a_high, b_low))

    root = matrix / norm
    correction = 1.5 * eye - 0.5 * root
    stacked = dot(jnp.concatenate([root, pull], axis=0), correction)
    root = dot(stacked[0:k], correction)
    carried = jnp.concatenate([correction, stacked[k:]], axis=0)
    for i in range(1, NS_ITERS):
        correction = 1.5 * eye - 0.5 * root
        if i < NS_ITERS - 1:
            root = dot(dot(root, correction), correction)
        carried = dot(carried, correction)
    shift = dot(carried[k:], carried[0:k]) / norm
    weights = carried[0:k] / jnp.sqrt(norm) + shift[0:1, :]
    high, low = split_2(weights)
    high_2 = jnp.concatenate([high, high], axis=1)
    copies = []
    for v in range(nv):
        for r in range(cx):
            if 2 <= r < cx - 2:
                anomalies, means, i = inner, inner_means, r - 2
            elif r in (1, cx - 2):
                anomalies, means, i = near, near_means, int(r > 1)
            else:
                anomalies, means, i = edge, edge_means, int(r > 0)
            at = slice((i * nv + v) * cy, (i * nv + v + 1) * cy)
            value = jnp.dot(high_2, anomalies[:, at], preferred_element_type=F32)
            value = value + jnp.dot(low, anomalies[0:k, at], preferred_element_type=F32)
            value = value + means[i * 8 + v : i * 8 + v + 1, :]
            for h in range(half):
                buf[v * half + h, pl.ds(r, k, stride=cx), :] = value[:, h * LANES : (h + 1) * LANES]
        for h in range(half):
            source = buf.at[v * half + h].reshape(k, cx, LANES)
            target = out.at[:, v, :, h * LANES : (h + 1) * LANES]
            copies.append(pltpu.make_async_copy(source, target, sems.at[v, h]))
            copies[-1].start()
    for copy in copies:
        copy.wait()


def local(sizes, ensemble, diffusivity, mixing, obs_cell, obs_var, obs_value, obs_weight):
    k, nv, cx, cy = ensemble.shape
    dims = (k, nv, cx, cy)
    assert k == 64 and nv == 3 and cx == 8 and cy % LANES == 0
    block = nv * k
    rows = nv * cx
    grp, nx, ny = sizes
    count = obs_cell.shape[2]
    factor = 1.0 / math.sqrt((k - 1) * count * nx * ny)
    limits = pltpu.CompilerParams(vmem_limit_bytes=16 << 20)

    def shape(*dims, dtype=F32):
        return jax.ShapeDtypeStruct(dims, dtype)

    small = (diffusivity, mixing) + tuple(a.reshape(1, count) for a in (obs_cell, obs_var, obs_value, obs_weight))
    state, send_a, send_b, sides, side_a, side_b, kappa, mixing, *obs = pl.pallas_call(
        functools.partial(load_kernel, dims),
        name="load",
        in_specs=[pl.BlockSpec(memory_space=pltpu.HBM)] * 7,
        out_specs=[vmem()] * 12,
        out_shape=[
            shape((cx + 4) * block, cy),
            shape(2 * block + 8, cy),
            shape(2 * block + 8, cy),
            shape(k + 8, LANES),
            shape(k + 8, LANES),
            shape(k + 8, LANES),
        ]
        + [shape(*a.shape, dtype=a.dtype) for a in small],
        scratch_shapes=[pltpu.VMEM((cy // LANES, k * rows, LANES), F32), pltpu.SemaphoreType.DMA((4, cy // LANES)), pltpu.SemaphoreType.DMA((6,))],
        compiler_params=limits,
    )(
        *(pltpu.with_memory_space_constraint(a, pltpu.HBM) for a in (ensemble.reshape(k * rows, cy),) + small)
    )

    recv_b = x_swap(1, sizes)(send_b)
    side_a = y_swap(0, sizes)(side_a)
    side_b = y_swap(1, sizes)(side_b)
    recv_a = x_swap(0, sizes)(send_a)

    first, kext, spread, early = pl.pallas_call(
        functools.partial(middle_kernel, dims),
        name="middle",
        in_specs=[smem()] + [vmem()] * 6,
        out_specs=[vmem()] * 4,
        out_shape=[
            shape((cx + 2) * block, cy),
            shape((cx + 2) * 8, cy),
            shape(cx * 8, cy),
            shape((cx - 2) * block, cy),
        ],
        scratch_shapes=[pltpu.VMEM((64, cy), F32)],
        compiler_params=limits,
    )(mixing, state, kappa, *obs)
    side_a, side_b, first = lax.optimization_barrier((side_a, side_b, first))
    halo = side_a + side_b
    corner_b = x_swap(1, sizes)(halo)
    corner_a = x_swap(0, sizes)(halo)

    inner_rows = cx - 4
    first, inner_anomalies, inner_means, partial, late = pl.pallas_call(
        functools.partial(inner_kernel, dims, factor),
        name="inner",
        in_specs=[smem()] + [vmem()] * 6,
        out_specs=[vmem()] * 5,
        input_output_aliases={1: 0},
        out_shape=[
            shape((cx + 2) * block, cy),
            shape(2 * k, inner_rows * nv * cy, dtype=BF16),
            shape(inner_rows * 8, cy),
            shape(2 * k + 32, 2 * k),
            shape(2 * block, cy),
        ],
        scratch_shapes=[
            pltpu.VMEM((k, LANES), F32),
            pltpu.VMEM((k, LANES), F32),
            pltpu.VMEM((2 * k + 32, inner_rows * nv * cy), BF16),
            pltpu.VMEM((4 * block, cy), F32),
        ],
        compiler_params=limits,
    )(mixing, first, early, sides, halo, kext, spread)

    _, _, near_anomalies, near_means, partial, outer, kext = pl.pallas_call(
        functools.partial(rows_kernel, dims, factor),
        name="rows",
        in_specs=[smem()] + [vmem()] * 10,
        out_specs=[vmem()] * 7,
        out_shape=[
            shape((cx + 4) * block, cy),
            shape((cx + 2) * block, cy),
            shape(2 * k, 2 * nv * cy, dtype=BF16),
            shape(2 * 8, cy),
            shape(2 * k + 32, 2 * k),
            shape(2 * block, cy),
            shape((cx + 2) * 8, cy),
        ],
        scratch_shapes=[
            pltpu.VMEM((k, LANES), F32),
            pltpu.VMEM((k, LANES), F32),
            pltpu.VMEM((2 * k + 32, 2 * nv * cy), BF16),
            pltpu.VMEM((2 * block, cy), F32),
        ],
        input_output_aliases={1: 0, 2: 1},
        compiler_params=limits,
    )(mixing, state, first, partial, late, recv_a, recv_b, sides, halo, kext, spread)

    edge_anomalies, edge_means, gram = pl.pallas_call(
        functools.partial(corner_kernel, dims, factor),
        name="corner",
        in_specs=[vmem()] * 7,
        out_specs=[vmem()] * 3,
        out_shape=[
            shape(2 * k, 2 * nv * cy, dtype=BF16),
            shape(2 * 8, cy),
            shape(k // 2 + 8, 2 * k),
        ],
        scratch_shapes=[
            pltpu.VMEM((k, LANES), F32),
            pltpu.VMEM((k, LANES), F32),
            pltpu.VMEM((2 * k + 32, 2 * nv * cy), BF16),
            pltpu.VMEM((2 * block, cy), F32),
        ],
        compiler_params=limits,
    )(outer, partial, halo, corner_a, corner_b, kext, spread)

    gram = all_sum(gram, sizes)

    return pl.pallas_call(
        functools.partial(apply_kernel, dims),
        name="apply",
        in_specs=[vmem()] * 7,
        out_specs=pl.BlockSpec(memory_space=pltpu.HBM),
        out_shape=shape(k, nv, cx, cy),
        scratch_shapes=[
            pltpu.VMEM((nv * (cy // LANES), k * cx, LANES), F32),
            pltpu.SemaphoreType.DMA((nv, cy // LANES)),
        ],
        compiler_params=limits,
    )(gram, inner_anomalies, inner_means, near_anomalies, near_means, edge_anomalies, edge_means)


def solution(mesh):
    sizes = tuple(mesh.shape[a] for a in ("grp", "gx", "gy"))
    return jax.shard_map(
        functools.partial(local, sizes),
        mesh=mesh,
        in_specs=(
            P("grp", None, "gx", "gy"),
            P("grp", "gx", "gy"),
            P(),
            P("gx", "gy", "grp"),
            P("gx", "gy", "grp"),
            P("gx", "gy", "grp"),
            P("gx", "gy", "grp"),
        ),
        out_specs=P("grp", None, "gx", "gy"),
        check_vma=False,
    )
```

```python
import functools
import math

import jax
import jax.numpy as jnp
from jax import lax
from jax.experimental import pallas as pl
from jax.experimental.pallas import tpu as pltpu
from jax.sharding import PartitionSpec as P

NS_ITERS = 5
LANES = 128
F32 = jnp.float32
BF16 = jnp.bfloat16


def vmem():
    return pl.BlockSpec(memory_space=pltpu.VMEM)


def smem():
    return pl.BlockSpec(memory_space=pltpu.SMEM)


def nt(a, b):
    return lax.dot_general(a, b, (((1,), (1,)), ((), ())), preferred_element_type=F32)


def split_2(x):
    high = x.astype(BF16)
    return high, (x - high.astype(F32)).astype(BF16)


def split_3(x):
    high = x.astype(BF16)
    rest = x - high.astype(F32)
    middle = rest.astype(BF16)
    return high, middle, (rest - middle.astype(F32)).astype(BF16)


def pair_swap(partner, sizes):
    grp, nx, ny = sizes
    pairs = []
    for g in range(grp):
        for x in range(nx):
            for y in range(ny):
                there = partner(g, x, y)
                if there is not None:
                    tg, tx, ty = there
                    pairs.append(((g * nx + x) * ny + y, (tg * nx + tx) * ny + ty))
    return lambda value: lax.ppermute(value, ("grp", "gx", "gy"), pairs)


def along(place, count, phase):
    first = place - (place - phase) % 2
    if first < 0 or first + 1 >= count:
        return None
    return first + 1 if place == first else first


def x_swap(phase, sizes):
    def partner(g, x, y):
        there = along(x, sizes[1], phase)
        if there is not None:
            return g, there, y
        return (g ^ 1, x, y) if sizes[0] % 2 == 0 else None

    return pair_swap(partner, sizes)


def y_swap(phase, sizes):
    def partner(g, x, y):
        there = along(y, sizes[2], phase)
        if there is not None:
            return g, x, there
        return (g, x ^ 1, y) if sizes[1] % 2 == 0 else None

    return pair_swap(partner, sizes)


def all_sum(value, sizes):
    grp, nx, ny = sizes
    if nx & (nx - 1) or ny & (ny - 1) or nx < 2:
        return lax.psum(value, ("gx", "gy"))

    def chip_swap(mask_0, mask_1):
        def partner(g, x, y):
            chip = ((x >> 1) * ny + y) ^ (mask_1 if x & 1 else mask_0)
            return g, ((chip // ny) << 1) | (x & 1), chip % ny

        return pair_swap(partner, sizes)

    core_swap = pair_swap(lambda g, x, y: (g, x ^ 1, y), sizes)
    chips = nx // 2 * ny
    value = value + core_swap(value)
    if chips == 8:
        parts = [chip_swap(a, b)(value) for a, b in ((2, 6), (1, 5), (4, 4), (3, 7))]
        value = parts[0] + parts[1] + 0.5 * (value + parts[2]) + parts[3]
        return value + core_swap(value)
    step = 1
    while step < chips:
        value = value + chip_swap(step, step)(value)
        step *= 2
    return value


def send_rows(dims, state, kappa, ref, near_top):
    k, nv, cx, cy = dims
    block = nv * k
    gx = lax.axis_index("gx")
    has = jnp.where(near_top, gx > 0, gx < lax.axis_size("gx") - 1)
    near = jnp.where(near_top, 2, cx + 1) * block
    second = jnp.where(near_top, 3, cx) * block
    for j in range(0, block, 64):
        ref[pl.ds(j, 64), :] = jnp.where(has, state[pl.ds(pl.multiple_of(near + j, 64), 64), :], 0.0)
        ref[pl.ds(block + j, 64), :] = jnp.where(has, state[pl.ds(pl.multiple_of(second + j, 64), 64), :], 0.0)
    for v in range(nv):
        edge = jnp.where(near_top, kappa[v, 0:1, :], kappa[v, cx - 1 : cx, :])
        ref[pl.ds(2 * block + v, 1), :] = jnp.where(has, edge, 0.0)
    ref[pl.ds(2 * block + nv, 8 - nv), :] = jnp.zeros((8 - nv, cy), F32)


def load_kernel(dims, ens, *refs):
    small_in, (state, send_a, send_b, sides, side_a, side_b) = refs[:6], refs[6:12]
    small, (buf, sems, small_sems) = refs[12:18], refs[18:]
    kappa = small[0]
    k, nv, cx, cy = dims
    rows = nv * cx
    chunks = 2
    part = k // chunks
    copies = []
    half = cy // LANES
    for c in range(chunks):
        span = pl.ds(c * part * rows, part * rows)
        for h in range(half):
            lanes = slice(h * LANES, (h + 1) * LANES)
            copies.append(pltpu.make_async_copy(ens.at[span, lanes], buf.at[h, span], sems.at[c, h]))
            copies[-1].start()
    small_copies = [pltpu.make_async_copy(a, b, small_sems.at[i]) for i, (a, b) in enumerate(zip(small_in, small))]
    for copy in small_copies:
        copy.start()
    lane = lax.broadcasted_iota(jnp.int32, (1, LANES), 1)

    def add(acc, place, right, left):
        low = (lane >= place) & (lane < place + 2)
        high = (lane >= 64 + place) & (lane < 64 + place + 2)
        acc = jnp.where(low, pltpu.roll(right, (place + 2) % LANES, 1), acc)
        return jnp.where(high, pltpu.roll(left, 64 + place, 1), acc)

    gy = lax.axis_index("gy")
    even_y = gy % 2 == 0
    has_left = gy > 0
    has_right = gy < lax.axis_size("gy") - 1
    wanted = []
    for to_right in (even_y, jnp.logical_not(even_y)):
        start = jnp.where(jnp.where(to_right, has_right, has_left), jnp.where(to_right, 0, 64), LANES)
        wanted.append((lane >= start) & (lane < start + 64))

    def put_sides(at, total):
        sides[at, :] = total
        side_a[at, :] = jnp.where(wanted[0], total, 0.0)
        side_b[at, :] = jnp.where(wanted[1], total, 0.0)

    for c in range(chunks):
        for h in range(half):
            copies[c * half + h].wait()
        total = jnp.zeros((part, LANES), F32)
        for r in range(cx):
            for v in range(nv):
                at = pl.ds(((r + 2) * nv + v) * k + c * part, part)
                values = [buf[h, pl.ds(c * part * rows + v * cx + r, part, stride=rows), :] for h in range(half)]
                for h in range(half):
                    state[at, h * LANES : (h + 1) * LANES] = values[h]
                total = add(total, 2 * (nv * (r + 1) + v), values[-1], values[0])
        put_sides(pl.ds(c * part, part), total)
    for copy in small_copies:
        copy.wait()
    even_x = lax.axis_index("gx") % 2 == 0
    send_rows(dims, state, kappa, send_a, jnp.logical_not(even_x))
    send_rows(dims, state, kappa, send_b, even_x)
    total = jnp.zeros((8, LANES), F32)
    for r in range(cx):
        for v in range(nv):
            row = kappa[v, r : r + 1, :]
            total = add(
                total,
                2 * (nv * (r + 1) + v),
                jnp.broadcast_to(row[:, cy - LANES :], (8, LANES)),
                jnp.broadcast_to(row[:, :LANES], (8, LANES)),
            )
    put_sides(pl.ds(k, 8), total)


def scatter_kernel(dims, cell, var, value, weight, out):
    k, nv, cx, cy = dims
    count = cell.shape[1]
    row = cell[...] // cy * nv + var[...]
    column = cell[...] % cy
    square = weight[...] * weight[...]
    rows = 32
    hit = lax.broadcasted_iota(jnp.int32, (rows, count), 0) == row
    parts = split_3(square) + split_3(square * value[...])
    left = [jnp.where(hit, p.astype(F32), 0.0).astype(BF16) for p in parts]
    one = (lax.broadcasted_iota(jnp.int32, (cy, count), 0) == column).astype(F32).astype(BF16)
    got = nt(jnp.concatenate(left, axis=0), one)
    piece = [got[i * rows : (i + 1) * rows] for i in range(6)]
    out[0:rows, :] = piece[0] + piece[1] + piece[2]
    out[rows : 2 * rows, :] = piece[3] + piece[4] + piece[5]


def mixed_columns(dims, mixing, columns, lane):
    k, nv, cx, cy = dims
    which = lane % 64 // 2 % nv
    mixed = jnp.zeros((k, LANES), F32)
    for shift in range(1 - nv, nv):
        coef = jnp.zeros((1, LANES), F32)
        for v in range(nv):
            if 0 <= v + shift < nv:
                coef = jnp.where(which == v, mixing[v, v + shift], coef)
        source = pltpu.roll(columns, (-2 * shift) % LANES, 1) if shift else columns
        mixed = mixed + coef * source
    return mixed


def first_columns_of(dims, mixing, columns, kcol, own, lane):
    k, nv, cx, cy = dims
    slot = lane % 64
    inside = (slot >= 2 * nv) & (slot < 2 * nv * (cx + 1))
    beside = jnp.where(
        lane < 64,
        pltpu.roll(columns, 1, 1) + pltpu.roll(own, 65, 1),
        pltpu.roll(columns, LANES - 1, 1) + pltpu.roll(own, 63, 1),
    )
    step = 2 * nv
    beside = beside + pltpu.roll(columns, step, 1) + pltpu.roll(columns, LANES - step, 1)
    mixed = mixed_columns(dims, mixing, columns, lane)
    return jnp.where(inside, columns + kcol * (beside - 4.0 * columns) + mixed, 0.0)


def late_columns_of(dims, mixing, columns, first_columns, kown, lane):
    k, nv, cx, cy = dims
    slot = lane % 64
    inside = (slot >= 2 * nv) & (slot < 2 * nv * (cx + 1))
    parity = jnp.where(lane < 64, 1, 0)
    outermost = inside & (lane % 2 == parity)

    def moved(x):
        return jnp.where(lane < 64, pltpu.roll(x, 65, 1), pltpu.roll(x, 63, 1))

    added = jnp.where(outermost, kown * moved(columns), 0.0)
    step = 2 * nv
    beside = pltpu.roll(added, step, 1) + pltpu.roll(added, LANES - step, 1) + moved(first_columns)
    outer = added + kown * (beside - 4.0 * added) + mixed_columns(dims, mixing, added, lane)
    inner = kown * jnp.where(lane < 64, pltpu.roll(added, LANES - 1, 1), pltpu.roll(added, 1, 1))
    return jnp.where(outermost, outer, jnp.where(inside, inner, 0.0))


def advance(dims, mixing, kext, load, side, e, lane, store):
    k, nv, cx, cy = dims
    half = cy // LANES
    eight = pl.ds(e * 8, 8)
    kappas = [kext[eight, h * LANES : (h + 1) * LANES] for h in range(half)]
    first_lane = lane == 0
    last_lane = lane == LANES - 1
    kap = [[jnp.broadcast_to(kappas[h][v : v + 1], (8, LANES)) for h in range(half)] for v in range(nv)]
    own = [[1.0 - 4.0 * kap[v][h] + mixing[v, v] for h in range(half)] for v in range(nv)]
    for j in range(0, k, 8):
        centers = [[load(0, v, j, h) for h in range(half)] for v in range(nv)]
        for v in range(nv):
            center = centers[v]
            shift = (LANES - 1 - 2 * (nv * e + v)) & (LANES - 1)
            edge = 0.0 if side is None else pltpu.roll(side[pl.ds(j, 8), :], shift, 1)
            ahead = [pltpu.roll(c, 1, 1) for c in center]
            behind = [pltpu.roll(c, LANES - 1, 1) for c in center]
            for h in range(half):
                left = jnp.where(first_lane, edge if h == 0 else ahead[h - 1], ahead[h])
                right = jnp.where(last_lane, edge if h == half - 1 else behind[h + 1], behind[h])
                around = (load(-1, v, j, h) + load(1, v, j, h)) + (left + right)
                out = own[v][h] * center[h] + kap[v][h] * around
                for w in range(nv):
                    if w != v:
                        out = out + mixing[v, w] * centers[w][h]
                store(v, j, h, out)


def edges_of(columns, lane):
    return jnp.where(lane % 2 == 0, pltpu.roll(columns, 64, 1), columns)


def loader(ref, base, k, row_size):
    def load(row, w, j, h):
        at = base + row * row_size + w * k + j
        return ref[pl.ds(at, 8), h * LANES : (h + 1) * LANES]

    return load


def first_step(dims, mixing, kext, state, first, side, rows, lane, inside=False):
    k, nv, cx, cy = dims
    block = nv * k
    for e in rows:

        def store(v, j, h, out):
            first[pl.ds(e * block + v * k + j, 8), h * LANES : (h + 1) * LANES] = out

        plain = loader(state, (e + 1) * block, k, block)

        def load(row, w, j, h):
            return 0.0 if inside and not 1 <= e + row <= cx else plain(row, w, j, h)

        advance(dims, mixing, kext, load, side, e, lane, store)


def add_sides(dims, kext, first, side, rows, lane):
    k, nv, cx, cy = dims
    block = nv * k
    ends = ((0, lane == 0), (cy - LANES, lane == LANES - 1))
    for e in rows:
        for v in range(nv):
            shift = (LANES - 1 - 2 * (nv * e + v)) & (LANES - 1)
            kap = []
            for at, here in ends:
                row = jnp.where(here, kext[e * 8 + v : e * 8 + v + 1, at : at + LANES], 0.0)
                kap.append(jnp.broadcast_to(row, (8, LANES)))
            for j in range(0, k, 8):
                edge = pltpu.roll(side[pl.ds(j, 8), :], shift, 1)
                place = pl.ds(e * block + v * k + j, 8)
                for (at, here), factor in zip(ends, kap):
                    first[place, at : at + LANES] += factor * edge


def second_step(dims, mixing, kext, first, first_side, e, ref, slot, lane):
    k, nv, cx, cy = dims
    block = nv * k
    sums = {}

    def store(v, j, h, out):
        ref[pl.ds(slot * block + v * k + j, 8), h * LANES : (h + 1) * LANES] = out
        sums[v, h] = out if j == 0 else sums[v, h] + out

    advance(dims, mixing, kext, loader(first, e * block, k, block), first_side, e, lane, store)
    return sums


def anomalies_of(dims, factor, spread, e, i, sums, kept, outs):
    k, nv, cx, cy = dims
    block = nv * k
    half = cy // LANES
    anomalies, means, moved = outs
    sub = lax.broadcasted_iota(jnp.int32, (8, 1), 0)
    for h in range(half):
        lanes = slice(h * LANES, (h + 1) * LANES)
        spreads = spread[pl.ds((e - 1) * 8, 8), lanes]
        found = jnp.zeros((8, LANES), F32)
        for v in range(nv):
            mean = jnp.sum(sums[v, h], axis=0, keepdims=True) * (1.0 / k)
            found = jnp.where(sub == v, mean, found)
            s2 = spreads[v : v + 1]
            s1 = spreads[nv + v : nv + v + 1]
            at = pl.ds((i * nv + v) * cy + h * LANES, LANES)
            scale = s2 * (factor * factor)
            for j in range(0, k, 16):
                part = kept[pl.ds(i * block + v * k + j, 16), lanes] - mean
                high, low = split_2(part)
                anomalies[j : j + 16, at] = high
                anomalies[k + j : k + j + 16, at] = low
                high, low = split_2(part * scale)
                moved[j : j + 16, at] = high
                moved[k + j : k + j + 16, at] = low
            pull = jnp.broadcast_to((s1 - mean * s2) * factor, (16, LANES))
            high, low = split_2(pull)
            moved[2 * k : 2 * k + 16, at] = high
            moved[2 * k + 16 : 2 * k + 32, at] = low
        means[i * 8 : i * 8 + 8, lanes] = found


def set_kappa(dims, kappa, kext):
    k, nv, cx, cy = dims
    for v in range(nv):
        for r in range(cx):
            kext[pl.ds((r + 1) * 8 + v, 1), :] = kappa[v, r : r + 1, :]


def middle_kernel(dims, mixing, state, kappa, cell, var, value, weight, first, kext, spread, early, cells):
    k, nv, cx, cy = dims
    scatter_kernel(dims, cell, var, value, weight, cells)
    for v in range(nv):
        for r in range(cx):
            spread[pl.ds(r * 8 + v, 1), :] = cells[pl.ds(r * nv + v, 1), :]
            spread[pl.ds(r * 8 + nv + v, 1), :] = cells[pl.ds(32 + r * nv + v, 1), :]
    set_kappa(dims, kappa, kext)
    lane = lax.broadcasted_iota(jnp.int32, (1, LANES), 1)
    first_step(dims, mixing, kext, state, first, None, range(1, cx + 1), lane, inside=True)
    for e in range(2, cx):
        second_step(dims, mixing, kext, first, None, e, early, e - 2, lane)


def inner_kernel(
    dims, factor, mixing, first_in, early, sides, halo, kext, spread,
    first, anomalies, means, partial, late, side, late_side, moved, kept,
):
    k, nv, cx, cy = dims
    block = nv * k
    half = cy // LANES
    lane = lax.broadcasted_iota(jnp.int32, (1, LANES), 1)
    columns = halo[0:k, :]
    first_columns = first_columns_of(dims, mixing, columns, halo[k : k + 1, :], sides[0:k, :], lane)
    side[...] = edges_of(columns, lane)
    late_side[...] = late_columns_of(dims, mixing, columns, first_columns, sides[k : k + 1, :], lane)

    def with_sides(e, ref, slot):
        sums = {}
        for v in range(nv):
            at = 2 * (nv * e + v)
            for j in range(0, k, 8):
                extra = late_side[pl.ds(j, 8), :]
                for h in range(half):
                    lanes = slice(h * LANES, (h + 1) * LANES)
                    out = early[pl.ds((e - 2) * block + v * k + j, 8), lanes]
                    if h == 0:
                        out = out + jnp.where(lane < 2, pltpu.roll(extra, 64 - at, 1), 0.0)
                    if h == half - 1:
                        out = out + jnp.where(lane >= LANES - 2, pltpu.roll(extra, LANES - 2 - at, 1), 0.0)
                    ref[pl.ds(slot * block + v * k + j, 8), lanes] = out
                    sums[v, h] = out if j == 0 else sums[v, h] + out
        return sums

    outs = (anomalies, means, moved)
    for i, e in enumerate(range(3, cx - 1)):
        sums = with_sides(e, kept, i)
        anomalies_of(dims, factor, spread, e, i, sums, kept, outs)
    partial[...] = nt(moved[...], anomalies[...])
    with_sides(2, late, 0)
    with_sides(cx - 1, late, 1)
    add_sides(dims, kext, first, side, (1, 2, cx - 1, cx), lane)


def rows_kernel(
    dims, factor, mixing, state_in, first_in, partial, late_in, recv_a, recv_b, sides, halo, kext_in, spread,
    state, first, anomalies, means, more, outer, kext, side, first_side, moved, kept,
):
    k, nv, cx, cy = dims
    block = nv * k
    half = cy // LANES
    down_is_a = lax.axis_index("gx") % 2 == 0

    def both(a, b):
        return jnp.where(down_is_a, b, a), jnp.where(down_is_a, a, b)

    for j in range(0, 2 * block, 32):
        up, down = both(recv_a[pl.ds(j, 32), :], recv_b[pl.ds(j, 32), :])
        state[pl.ds((block if j < block else -block) + j, 32), :] = up
        state[pl.ds((cx + 2) * block + j, 32), :] = down
    up, down = both(recv_a[2 * block : 2 * block + 8, :], recv_b[2 * block : 2 * block + 8, :])
    kext[8 : 8 * (cx + 1), :] = kext_in[8 : 8 * (cx + 1), :]
    kext[0:8, :] = up
    kext[8 * (cx + 1) : 8 * (cx + 2), :] = down

    lane = lax.broadcasted_iota(jnp.int32, (1, LANES), 1)
    columns = halo[0:k, :]
    side[...] = edges_of(columns, lane)
    columns = first_columns_of(dims, mixing, columns, halo[k : k + 1, :], sides[0:k, :], lane)
    first_side[...] = edges_of(columns, lane)
    first_step(dims, mixing, kext, state, first, side, (0, cx + 1), lane)

    def late(e, beyond, near, read, write):
        sums = {}
        for v in range(nv):
            for h in range(half):
                lanes = slice(h * LANES, (h + 1) * LANES)
                row = kext[e * 8 + v : e * 8 + v + 1, lanes]
                if near != e:
                    row = row * kext[near * 8 + v : near * 8 + v + 1, lanes]
                row = jnp.broadcast_to(row, (8, LANES))
                for j in range(0, k, 8):
                    out = read[0][pl.ds(read[1] + v * k + j, 8), lanes]
                    out = out + row * state[pl.ds(beyond * block + v * k + j, 8), lanes]
                    write[0][pl.ds(write[1] + v * k + j, 8), lanes] = out
                    sums[v, h] = out if j == 0 else sums[v, h] + out
        return sums

    for i, (e, beyond) in enumerate(((1, 1), (cx, cx + 2))):
        late(e, beyond, e, (first, e * block), (first, e * block))
        second_step(dims, mixing, kext, first, first_side, e, outer, i, lane)
    for i, (e, beyond, near) in enumerate(((2, 1, 1), (cx - 1, cx + 2, cx))):
        sums = late(e, beyond, near, (late_in, i * block), (kept, i * block))
        anomalies_of(dims, factor, spread, e, i, sums, kept, (anomalies, means, moved))
    more[...] = partial[...] + nt(moved[...], anomalies[...])


def corner_kernel(
    dims, factor, outer, partial, halo, corner_a, corner_b, kext, spread,
    anomalies, means, gram, side_up, side_down, moved, kept,
):
    k, nv, cx, cy = dims
    block = nv * k
    half = cy // LANES
    gx = lax.axis_index("gx")
    down_is_a = gx % 2 == 0
    lane = lax.broadcasted_iota(jnp.int32, (1, LANES), 1)
    a = corner_a[0:k, :]
    b = corner_b[0:k, :]
    side_up[...] = edges_of(jnp.where(gx > 0, jnp.where(down_is_a, b, a), 0.0), lane)
    side_down[...] = edges_of(jnp.where(gx < lax.axis_size("gx") - 1, jnp.where(down_is_a, a, b), 0.0), lane)
    kside = edges_of(halo[k : k + 8, :], lane)

    def to_ends(x, e, v):
        return pltpu.roll(x, (LANES - 1 - 2 * (nv * e + v)) & (LANES - 1), 1)

    for i, (e, beyond, source, there) in enumerate(((1, 0, side_up, cx), (cx, cx + 1, side_down, 1))):
        sums = {}
        for v in range(nv):
            kend = to_ends(kside, e, v)[0:1]
            factors = {}
            for h in (0, half - 1):
                lanes = slice(h * LANES, (h + 1) * LANES)
                here = (lane == 0) if h == 0 else (lane == LANES - 1)
                row = kext[e * 8 + v : e * 8 + v + 1, lanes] * (kext[beyond * 8 + v : beyond * 8 + v + 1, lanes] + kend)
                factors[h] = jnp.broadcast_to(jnp.where(here, row, 0.0), (8, LANES))
            for j in range(0, k, 8):
                corner = to_ends(source[pl.ds(j, 8), :], there, v)
                for h in range(half):
                    lanes = slice(h * LANES, (h + 1) * LANES)
                    place = pl.ds(i * block + v * k + j, 8)
                    out = outer[place, lanes]
                    if h in factors:
                        out = out + factors[h] * corner
                    kept[place, lanes] = out
                    sums[v, h] = out if j == 0 else sums[v, h] + out
        anomalies_of(dims, factor, spread, e, i, sums, kept, (anomalies, means, moved))
    got = partial[...] + nt(moved[...], anomalies[...])
    whole = got[:, 0:k] + got[:, k : 2 * k]
    matrix = whole[0:k] + whole[k : 2 * k]
    pull = whole[2 * k : 2 * k + 8] + whole[2 * k + 16 : 2 * k + 24]
    gram[0 : k // 2, :] = jnp.concatenate([matrix[0 : k // 2], matrix[k // 2 :]], axis=1)
    gram[k // 2 : k // 2 + 8, :] = jnp.concatenate([pull, pull], axis=1)


def apply_kernel(dims, gram, inner, inner_means, near, near_means, edge, edge_means, out, buf, sems):
    k, nv, cx, cy = dims
    half = cy // LANES
    row = lax.broadcasted_iota(jnp.int32, (k, k), 0)
    col = lax.broadcasted_iota(jnp.int32, (k, k), 1)
    eye = (row == col).astype(F32)
    both = gram[...]
    matrix = jnp.concatenate([both[0 : k // 2, 0:k], both[0 : k // 2, k : 2 * k]], axis=0) + eye
    pull = both[k // 2 : k // 2 + 8, 0:k]
    pull = jnp.concatenate([pull, pull], axis=0)
    norm = jnp.sqrt(jnp.sum(jnp.sum(matrix * matrix, axis=0, keepdims=True), axis=1, keepdims=True))

    def one(x, y):
        return jnp.dot(x, y, preferred_element_type=F32)

    def dot(a, b):
        a_high, a_low = split_2(a)
        b_high, b_low = split_2(b)
        rows = a.shape[0]
        both = one(jnp.concatenate([a_high, a_low], axis=0), b_high)
        return both[0:rows] + (both[rows:] + one(a_high, b_low))

    scale = 1.0 / norm
    root = matrix * scale
    correction = 1.5 * eye - 0.5 * root
    stacked = dot(jnp.concatenate([root, pull], axis=0), correction)
    root = dot(stacked[0:k], correction)
    carried = jnp.concatenate([correction, stacked[k:]], axis=0)
    for i in range(1, NS_ITERS):
        correction = 1.5 * eye - 0.5 * root
        if i < NS_ITERS - 1:
            root = dot(dot(root, correction), correction)
        carried = dot(carried, correction)
    shift = dot(carried[k:], carried[0:k]) * scale
    weights = carried[0:k] * jnp.sqrt(scale) + shift[0:1, :]
    high, low = split_2(weights)
    high_2 = jnp.concatenate([high, high], axis=1)
    copies = []
    for v in range(nv):
        for r in range(cx):
            if 2 <= r < cx - 2:
                anomalies, means, i = inner, inner_means, r - 2
            elif r in (1, cx - 2):
                anomalies, means, i = near, near_means, int(r > 1)
            else:
                anomalies, means, i = edge, edge_means, int(r > 0)
            at = slice((i * nv + v) * cy, (i * nv + v + 1) * cy)
            value = jnp.dot(high_2, anomalies[:, at], preferred_element_type=F32)
            value = value + jnp.dot(low, anomalies[0:k, at], preferred_element_type=F32)
            value = value + means[i * 8 + v : i * 8 + v + 1, :]
            for h in range(half):
                buf[v * half + h, pl.ds(r, k, stride=cx), :] = value[:, h * LANES : (h + 1) * LANES]
        for h in range(half):
            source = buf.at[v * half + h].reshape(k, cx, LANES)
            target = out.at[:, v, :, h * LANES : (h + 1) * LANES]
            copies.append(pltpu.make_async_copy(source, target, sems.at[v, h]))
            copies[-1].start()
    for copy in copies:
        copy.wait()


def local(sizes, ensemble, diffusivity, mixing, obs_cell, obs_var, obs_value, obs_weight):
    k, nv, cx, cy = ensemble.shape
    dims = (k, nv, cx, cy)
    assert k == 64 and nv == 3 and cx == 8 and cy % LANES == 0
    block = nv * k
    rows = nv * cx
    grp, nx, ny = sizes
    count = obs_cell.shape[2]
    factor = 1.0 / math.sqrt((k - 1) * count * nx * ny)
    limits = pltpu.CompilerParams(vmem_limit_bytes=16 << 20)

    def shape(*dims, dtype=F32):
        return jax.ShapeDtypeStruct(dims, dtype)

    small = (diffusivity, mixing) + tuple(a.reshape(1, count) for a in (obs_cell, obs_var, obs_value, obs_weight))
    state, send_a, send_b, sides, side_a, side_b, kappa, mixing, *obs = pl.pallas_call(
        functools.partial(load_kernel, dims),
        name="load",
        in_specs=[pl.BlockSpec(memory_space=pltpu.HBM)] * 7,
        out_specs=[vmem()] * 12,
        out_shape=[
            shape((cx + 4) * block, cy),
            shape(2 * block + 8, cy),
            shape(2 * block + 8, cy),
            shape(k + 8, LANES),
            shape(k + 8, LANES),
            shape(k + 8, LANES),
        ]
        + [shape(*a.shape, dtype=a.dtype) for a in small],
        scratch_shapes=[pltpu.VMEM((cy // LANES, k * rows, LANES), F32), pltpu.SemaphoreType.DMA((2, cy // LANES)), pltpu.SemaphoreType.DMA((6,))],
        compiler_params=limits,
    )(
        *(pltpu.with_memory_space_constraint(a, pltpu.HBM) for a in (ensemble.reshape(k * rows, cy),) + small)
    )

    recv_b = x_swap(1, sizes)(send_b)
    side_a = y_swap(0, sizes)(side_a)
    side_b = y_swap(1, sizes)(side_b)
    recv_a = x_swap(0, sizes)(send_a)

    first, kext, spread, early = pl.pallas_call(
        functools.partial(middle_kernel, dims),
        name="middle",
        in_specs=[smem()] + [vmem()] * 6,
        out_specs=[vmem()] * 4,
        out_shape=[
            shape((cx + 2) * block, cy),
            shape((cx + 2) * 8, cy),
            shape(cx * 8, cy),
            shape((cx - 2) * block, cy),
        ],
        scratch_shapes=[pltpu.VMEM((64, cy), F32)],
        compiler_params=limits,
    )(mixing, state, kappa, *obs)
    side_a, side_b, first = lax.optimization_barrier((side_a, side_b, first))
    halo = side_a + side_b
    corner_b = x_swap(1, sizes)(halo)
    corner_a = x_swap(0, sizes)(halo)

    inner_rows = cx - 4
    first, inner_anomalies, inner_means, partial, late = pl.pallas_call(
        functools.partial(inner_kernel, dims, factor),
        name="inner",
        in_specs=[smem()] + [vmem()] * 6,
        out_specs=[vmem()] * 5,
        input_output_aliases={1: 0},
        out_shape=[
            shape((cx + 2) * block, cy),
            shape(2 * k, inner_rows * nv * cy, dtype=BF16),
            shape(inner_rows * 8, cy),
            shape(2 * k + 32, 2 * k),
            shape(2 * block, cy),
        ],
        scratch_shapes=[
            pltpu.VMEM((k, LANES), F32),
            pltpu.VMEM((k, LANES), F32),
            pltpu.VMEM((2 * k + 32, inner_rows * nv * cy), BF16),
            pltpu.VMEM((4 * block, cy), F32),
        ],
        compiler_params=limits,
    )(mixing, first, early, sides, halo, kext, spread)

    _, _, near_anomalies, near_means, partial, outer, kext = pl.pallas_call(
        functools.partial(rows_kernel, dims, factor),
        name="rows",
        in_specs=[smem()] + [vmem()] * 10,
        out_specs=[vmem()] * 7,
        out_shape=[
            shape((cx + 4) * block, cy),
            shape((cx + 2) * block, cy),
            shape(2 * k, 2 * nv * cy, dtype=BF16),
            shape(2 * 8, cy),
            shape(2 * k + 32, 2 * k),
            shape(2 * block, cy),
            shape((cx + 2) * 8, cy),
        ],
        scratch_shapes=[
            pltpu.VMEM((k, LANES), F32),
            pltpu.VMEM((k, LANES), F32),
            pltpu.VMEM((2 * k + 32, 2 * nv * cy), BF16),
            pltpu.VMEM((2 * block, cy), F32),
        ],
        input_output_aliases={1: 0, 2: 1},
        compiler_params=limits,
    )(mixing, state, first, partial, late, recv_a, recv_b, sides, halo, kext, spread)

    edge_anomalies, edge_means, gram = pl.pallas_call(
        functools.partial(corner_kernel, dims, factor),
        name="corner",
        in_specs=[vmem()] * 7,
        out_specs=[vmem()] * 3,
        out_shape=[
            shape(2 * k, 2 * nv * cy, dtype=BF16),
            shape(2 * 8, cy),
            shape(k // 2 + 8, 2 * k),
        ],
        scratch_shapes=[
            pltpu.VMEM((k, LANES), F32),
            pltpu.VMEM((k, LANES), F32),
            pltpu.VMEM((2 * k + 32, 2 * nv * cy), BF16),
            pltpu.VMEM((2 * block, cy), F32),
        ],
        compiler_params=limits,
    )(outer, partial, halo, corner_a, corner_b, kext, spread)

    gram = all_sum(gram, sizes)

    return pl.pallas_call(
        functools.partial(apply_kernel, dims),
        name="apply",
        in_specs=[vmem()] * 7,
        out_specs=pl.BlockSpec(memory_space=pltpu.HBM),
        out_shape=shape(k, nv, cx, cy),
        scratch_shapes=[
            pltpu.VMEM((nv * (cy // LANES), k * cx, LANES), F32),
            pltpu.SemaphoreType.DMA((nv, cy // LANES)),
        ],
        compiler_params=limits,
    )(gram, inner_anomalies, inner_means, near_anomalies, near_means, edge_anomalies, edge_means)


def solution(mesh):
    sizes = tuple(mesh.shape[a] for a in ("grp", "gx", "gy"))
    return jax.shard_map(
        functools.partial(local, sizes),
        mesh=mesh,
        in_specs=(
            P("grp", None, "gx", "gy"),
            P("grp", "gx", "gy"),
            P(),
            P("gx", "gy", "grp"),
            P("gx", "gy", "grp"),
            P("gx", "gy", "grp"),
            P("gx", "gy", "grp"),
        ),
        out_specs=P("grp", None, "gx", "gy"),
        check_vma=False,
    )
```

```python
import functools
import math

import jax
import jax.numpy as jnp
from jax import lax
from jax.experimental import pallas as pl
from jax.experimental.pallas import tpu as pltpu
from jax.sharding import PartitionSpec as P

NS_ITERS = 5
LANES = 128
F32 = jnp.float32
BF16 = jnp.bfloat16


def vmem():
    return pl.BlockSpec(memory_space=pltpu.VMEM)


def smem():
    return pl.BlockSpec(memory_space=pltpu.SMEM)


def nt(a, b):
    return lax.dot_general(a, b, (((1,), (1,)), ((), ())), preferred_element_type=F32)


def split_2(x):
    high = x.astype(BF16)
    return high, (x - high.astype(F32)).astype(BF16)


def split_3(x):
    high = x.astype(BF16)
    rest = x - high.astype(F32)
    middle = rest.astype(BF16)
    return high, middle, (rest - middle.astype(F32)).astype(BF16)


def pair_swap(partner, sizes):
    grp, nx, ny = sizes
    pairs = []
    for g in range(grp):
        for x in range(nx):
            for y in range(ny):
                there = partner(g, x, y)
                if there is not None:
                    tg, tx, ty = there
                    pairs.append(((g * nx + x) * ny + y, (tg * nx + tx) * ny + ty))
    return lambda value: lax.ppermute(value, ("grp", "gx", "gy"), pairs)


def along(place, count, phase):
    first = place - (place - phase) % 2
    if first < 0 or first + 1 >= count:
        return None
    return first + 1 if place == first else first


def x_swap(phase, sizes):
    def partner(g, x, y):
        there = along(x, sizes[1], phase)
        if there is not None:
            return g, there, y
        return (g ^ 1, x, y) if sizes[0] % 2 == 0 else None

    return pair_swap(partner, sizes)


def y_swap(phase, sizes):
    def partner(g, x, y):
        there = along(y, sizes[2], phase)
        if there is not None:
            return g, x, there
        return (g, x ^ 1, y) if sizes[1] % 2 == 0 else None

    return pair_swap(partner, sizes)


def all_sum(value, sizes):
    grp, nx, ny = sizes
    if nx & (nx - 1) or ny & (ny - 1) or nx < 2:
        return lax.psum(value, ("gx", "gy"))

    def chip_swap(mask_0, mask_1):
        def partner(g, x, y):
            chip = ((x >> 1) * ny + y) ^ (mask_1 if x & 1 else mask_0)
            return g, ((chip // ny) << 1) | (x & 1), chip % ny

        return pair_swap(partner, sizes)

    core_swap = pair_swap(lambda g, x, y: (g, x ^ 1, y), sizes)
    chips = nx // 2 * ny
    value = value + core_swap(value)
    if chips == 8:
        parts = [chip_swap(a, b)(value) for a, b in ((2, 6), (1, 5), (4, 4), (3, 7))]
        value = parts[0] + parts[1] + 0.5 * (value + parts[2]) + parts[3]
        return value + core_swap(value)
    step = 1
    while step < chips:
        value = value + chip_swap(step, step)(value)
        step *= 2
    return value


def send_rows(dims, state, kappa, ref, near_top):
    k, nv, cx, cy = dims
    block = nv * k
    gx = lax.axis_index("gx")
    has = jnp.where(near_top, gx > 0, gx < lax.axis_size("gx") - 1)
    near = jnp.where(near_top, 2, cx + 1) * block
    second = jnp.where(near_top, 3, cx) * block
    for j in range(0, block, 64):
        ref[pl.ds(j, 64), :] = jnp.where(has, state[pl.ds(pl.multiple_of(near + j, 64), 64), :], 0.0)
        ref[pl.ds(block + j, 64), :] = jnp.where(has, state[pl.ds(pl.multiple_of(second + j, 64), 64), :], 0.0)
    for v in range(nv):
        edge = jnp.where(near_top, kappa[v, 0:1, :], kappa[v, cx - 1 : cx, :])
        ref[pl.ds(2 * block + v, 1), :] = jnp.where(has, edge, 0.0)
    ref[pl.ds(2 * block + nv, 8 - nv), :] = jnp.zeros((8 - nv, cy), F32)


def load_kernel(dims, ens, *refs):
    small_in, (state, send_a, send_b, sides, side_a, side_b) = refs[:6], refs[6:12]
    small, (buf, sems, small_sems) = refs[12:18], refs[18:]
    kappa = small[0]
    k, nv, cx, cy = dims
    rows = nv * cx
    chunks = 4
    part = k // chunks
    copies = []
    half = cy // LANES
    for c in range(chunks):
        span = pl.ds(c * part * rows, part * rows)
        for h in range(half):
            lanes = slice(h * LANES, (h + 1) * LANES)
            copies.append(pltpu.make_async_copy(ens.at[span, lanes], buf.at[h, span], sems.at[c, h]))
            copies[-1].start()
    small_copies = [pltpu.make_async_copy(a, b, small_sems.at[i]) for i, (a, b) in enumerate(zip(small_in, small))]
    for copy in small_copies:
        copy.start()
    lane = lax.broadcasted_iota(jnp.int32, (1, LANES), 1)

    def add(acc, place, right, left):
        low = (lane >= place) & (lane < place + 2)
        high = (lane >= 64 + place) & (lane < 64 + place + 2)
        acc = jnp.where(low, pltpu.roll(right, (place + 2) % LANES, 1), acc)
        return jnp.where(high, pltpu.roll(left, 64 + place, 1), acc)

    gy = lax.axis_index("gy")
    even_y = gy % 2 == 0
    has_left = gy > 0
    has_right = gy < lax.axis_size("gy") - 1
    wanted = []
    for to_right in (even_y, jnp.logical_not(even_y)):
        start = jnp.where(jnp.where(to_right, has_right, has_left), jnp.where(to_right, 0, 64), LANES)
        wanted.append((lane >= start) & (lane < start + 64))

    def put_sides(at, total):
        sides[at, :] = total
        side_a[at, :] = jnp.where(wanted[0], total, 0.0)
        side_b[at, :] = jnp.where(wanted[1], total, 0.0)

    for c in range(chunks):
        for h in range(half):
            copies[c * half + h].wait()
        total = jnp.zeros((part, LANES), F32)
        for r in range(cx):
            for v in range(nv):
                at = pl.ds(((r + 2) * nv + v) * k + c * part, part)
                values = [buf[h, pl.ds(c * part * rows + v * cx + r, part, stride=rows), :] for h in range(half)]
                for h in range(half):
                    state[at, h * LANES : (h + 1) * LANES] = values[h]
                total = add(total, 2 * (nv * (r + 1) + v), values[-1], values[0])
        put_sides(pl.ds(c * part, part), total)
    for copy in small_copies:
        copy.wait()
    even_x = lax.axis_index("gx") % 2 == 0
    send_rows(dims, state, kappa, send_a, jnp.logical_not(even_x))
    send_rows(dims, state, kappa, send_b, even_x)
    total = jnp.zeros((8, LANES), F32)
    for r in range(cx):
        for v in range(nv):
            row = kappa[v, r : r + 1, :]
            total = add(
                total,
                2 * (nv * (r + 1) + v),
                jnp.broadcast_to(row[:, cy - LANES :], (8, LANES)),
                jnp.broadcast_to(row[:, :LANES], (8, LANES)),
            )
    put_sides(pl.ds(k, 8), total)


def scatter_kernel(dims, cell, var, value, weight, out):
    k, nv, cx, cy = dims
    count = cell.shape[1]
    row = cell[...] // cy * nv + var[...]
    column = cell[...] % cy
    square = weight[...] * weight[...]
    rows = 32
    hit = lax.broadcasted_iota(jnp.int32, (rows, count), 0) == row
    parts = split_3(square) + split_3(square * value[...])
    left = [jnp.where(hit, p.astype(F32), 0.0).astype(BF16) for p in parts]
    one = (lax.broadcasted_iota(jnp.int32, (cy, count), 0) == column).astype(F32).astype(BF16)
    got = nt(jnp.concatenate(left, axis=0), one)
    piece = [got[i * rows : (i + 1) * rows] for i in range(6)]
    out[0:rows, :] = piece[0] + piece[1] + piece[2]
    out[rows : 2 * rows, :] = piece[3] + piece[4] + piece[5]


def mixed_columns(dims, mixing, columns, lane):
    k, nv, cx, cy = dims
    which = lane % 64 // 2 % nv
    mixed = jnp.zeros((k, LANES), F32)
    for shift in range(1 - nv, nv):
        coef = jnp.zeros((1, LANES), F32)
        for v in range(nv):
            if 0 <= v + shift < nv:
                coef = jnp.where(which == v, mixing[v, v + shift], coef)
        source = pltpu.roll(columns, (-2 * shift) % LANES, 1) if shift else columns
        mixed = mixed + coef * source
    return mixed


def first_columns_of(dims, mixing, columns, kcol, own, lane):
    k, nv, cx, cy = dims
    slot = lane % 64
    inside = (slot >= 2 * nv) & (slot < 2 * nv * (cx + 1))
    beside = jnp.where(
        lane < 64,
        pltpu.roll(columns, 1, 1) + pltpu.roll(own, 65, 1),
        pltpu.roll(columns, LANES - 1, 1) + pltpu.roll(own, 63, 1),
    )
    step = 2 * nv
    beside = beside + pltpu.roll(columns, step, 1) + pltpu.roll(columns, LANES - step, 1)
    mixed = mixed_columns(dims, mixing, columns, lane)
    return jnp.where(inside, columns + kcol * (beside - 4.0 * columns) + mixed, 0.0)


def late_columns_of(dims, mixing, columns, first_columns, kown, lane):
    k, nv, cx, cy = dims
    slot = lane % 64
    inside = (slot >= 2 * nv) & (slot < 2 * nv * (cx + 1))
    parity = jnp.where(lane < 64, 1, 0)
    outermost = inside & (lane % 2 == parity)

    def moved(x):
        return jnp.where(lane < 64, pltpu.roll(x, 65, 1), pltpu.roll(x, 63, 1))

    added = jnp.where(outermost, kown * moved(columns), 0.0)
    step = 2 * nv
    beside = pltpu.roll(added, step, 1) + pltpu.roll(added, LANES - step, 1) + moved(first_columns)
    outer = added + kown * (beside - 4.0 * added) + mixed_columns(dims, mixing, added, lane)
    inner = kown * jnp.where(lane < 64, pltpu.roll(added, LANES - 1, 1), pltpu.roll(added, 1, 1))
    return jnp.where(outermost, outer, jnp.where(inside, inner, 0.0))


def advance(dims, mixing, kext, load, side, e, lane, store):
    k, nv, cx, cy = dims
    half = cy // LANES
    eight = pl.ds(e * 8, 8)
    kappas = [kext[eight, h * LANES : (h + 1) * LANES] for h in range(half)]
    first_lane = lane == 0
    last_lane = lane == LANES - 1
    kap = [[jnp.broadcast_to(kappas[h][v : v + 1], (8, LANES)) for h in range(half)] for v in range(nv)]
    own = [[1.0 - 4.0 * kap[v][h] + mixing[v, v] for h in range(half)] for v in range(nv)]
    for j in range(0, k, 8):
        centers = [[load(0, v, j, h) for h in range(half)] for v in range(nv)]
        for v in range(nv):
            center = centers[v]
            shift = (LANES - 1 - 2 * (nv * e + v)) & (LANES - 1)
            edge = 0.0 if side is None else pltpu.roll(side[pl.ds(j, 8), :], shift, 1)
            ahead = [pltpu.roll(c, 1, 1) for c in center]
            behind = [pltpu.roll(c, LANES - 1, 1) for c in center]
            for h in range(half):
                left = jnp.where(first_lane, edge if h == 0 else ahead[h - 1], ahead[h])
                right = jnp.where(last_lane, edge if h == half - 1 else behind[h + 1], behind[h])
                around = (load(-1, v, j, h) + load(1, v, j, h)) + (left + right)
                out = own[v][h] * center[h] + kap[v][h] * around
                for w in range(nv):
                    if w != v:
                        out = out + mixing[v, w] * centers[w][h]
                store(v, j, h, out)


def edges_of(columns, lane):
    return jnp.where(lane % 2 == 0, pltpu.roll(columns, 64, 1), columns)


def loader(ref, base, k, row_size):
    def load(row, w, j, h):
        at = base + row * row_size + w * k + j
        return ref[pl.ds(at, 8), h * LANES : (h + 1) * LANES]

    return load


def first_step(dims, mixing, kext, state, first, side, rows, lane, inside=False):
    k, nv, cx, cy = dims
    block = nv * k
    for e in rows:

        def store(v, j, h, out):
            first[pl.ds(e * block + v * k + j, 8), h * LANES : (h + 1) * LANES] = out

        plain = loader(state, (e + 1) * block, k, block)

        def load(row, w, j, h):
            return 0.0 if inside and not 1 <= e + row <= cx else plain(row, w, j, h)

        advance(dims, mixing, kext, load, side, e, lane, store)


def add_sides(dims, kext, first, side, rows, lane):
    k, nv, cx, cy = dims
    block = nv * k
    ends = ((0, lane == 0), (cy - LANES, lane == LANES - 1))
    for e in rows:
        for v in range(nv):
            shift = (LANES - 1 - 2 * (nv * e + v)) & (LANES - 1)
            kap = []
            for at, here in ends:
                row = jnp.where(here, kext[e * 8 + v : e * 8 + v + 1, at : at + LANES], 0.0)
                kap.append(jnp.broadcast_to(row, (8, LANES)))
            for j in range(0, k, 8):
                edge = pltpu.roll(side[pl.ds(j, 8), :], shift, 1)
                place = pl.ds(e * block + v * k + j, 8)
                for (at, here), factor in zip(ends, kap):
                    first[place, at : at + LANES] += factor * edge


def second_step(dims, mixing, kext, first, first_side, e, ref, slot, lane):
    k, nv, cx, cy = dims
    block = nv * k
    sums = {}

    def store(v, j, h, out):
        ref[pl.ds(slot * block + v * k + j, 8), h * LANES : (h + 1) * LANES] = out
        sums[v, h] = out if j == 0 else sums[v, h] + out

    advance(dims, mixing, kext, loader(first, e * block, k, block), first_side, e, lane, store)
    return sums


def anomalies_of(dims, factor, spread, e, i, sums, kept, outs):
    k, nv, cx, cy = dims
    block = nv * k
    half = cy // LANES
    anomalies, means, moved = outs
    sub = lax.broadcasted_iota(jnp.int32, (8, 1), 0)
    for h in range(half):
        lanes = slice(h * LANES, (h + 1) * LANES)
        spreads = spread[pl.ds((e - 1) * 8, 8), lanes]
        found = jnp.zeros((8, LANES), F32)
        for v in range(nv):
            mean = jnp.sum(sums[v, h], axis=0, keepdims=True) * (1.0 / k)
            found = jnp.where(sub == v, mean, found)
            s2 = spreads[v : v + 1]
            s1 = spreads[nv + v : nv + v + 1]
            at = pl.ds((i * nv + v) * cy + h * LANES, LANES)
            scale = s2 * (factor * factor)
            for j in range(0, k, 16):
                part = kept[pl.ds(i * block + v * k + j, 16), lanes] - mean
                high, low = split_2(part)
                anomalies[j : j + 16, at] = high
                anomalies[k + j : k + j + 16, at] = low
                high, low = split_2(part * scale)
                moved[j : j + 16, at] = high
                moved[k + j : k + j + 16, at] = low
            pull = jnp.broadcast_to((s1 - mean * s2) * factor, (16, LANES))
            high, low = split_2(pull)
            upper = lax.broadcasted_iota(jnp.int32, (16, 1), 0) < 8
            moved[2 * k : 2 * k + 16, at] = jnp.where(upper, high.astype(F32), low.astype(F32)).astype(BF16)
        means[i * 8 : i * 8 + 8, lanes] = found


def set_kappa(dims, kappa, kext):
    k, nv, cx, cy = dims
    for v in range(nv):
        for r in range(cx):
            kext[pl.ds((r + 1) * 8 + v, 1), :] = kappa[v, r : r + 1, :]


def middle_kernel(dims, mixing, state, kappa, cell, var, value, weight, first, kext, spread, early, cells):
    k, nv, cx, cy = dims
    scatter_kernel(dims, cell, var, value, weight, cells)
    for v in range(nv):
        for r in range(cx):
            spread[pl.ds(r * 8 + v, 1), :] = cells[pl.ds(r * nv + v, 1), :]
            spread[pl.ds(r * 8 + nv + v, 1), :] = cells[pl.ds(32 + r * nv + v, 1), :]
    set_kappa(dims, kappa, kext)
    lane = lax.broadcasted_iota(jnp.int32, (1, LANES), 1)
    first_step(dims, mixing, kext, state, first, None, range(1, cx + 1), lane, inside=True)
    for e in range(2, cx):
        second_step(dims, mixing, kext, first, None, e, early, e - 2, lane)


def inner_kernel(
    dims, factor, mixing, first_in, early, sides, halo, kext, spread,
    first, anomalies, means, partial, late, side, late_side, moved, kept,
):
    k, nv, cx, cy = dims
    block = nv * k
    half = cy // LANES
    lane = lax.broadcasted_iota(jnp.int32, (1, LANES), 1)
    columns = halo[0:k, :]
    first_columns = first_columns_of(dims, mixing, columns, halo[k : k + 1, :], sides[0:k, :], lane)
    side[...] = edges_of(columns, lane)
    late_side[...] = late_columns_of(dims, mixing, columns, first_columns, sides[k : k + 1, :], lane)

    def with_sides(e, ref, slot):
        sums = {}
        for v in range(nv):
            at = 2 * (nv * e + v)
            for j in range(0, k, 8):
                extra = late_side[pl.ds(j, 8), :]
                for h in range(half):
                    lanes = slice(h * LANES, (h + 1) * LANES)
                    out = early[pl.ds((e - 2) * block + v * k + j, 8), lanes]
                    if h == 0:
                        out = out + jnp.where(lane < 2, pltpu.roll(extra, 64 - at, 1), 0.0)
                    if h == half - 1:
                        out = out + jnp.where(lane >= LANES - 2, pltpu.roll(extra, LANES - 2 - at, 1), 0.0)
                    ref[pl.ds(slot * block + v * k + j, 8), lanes] = out
                    sums[v, h] = out if j == 0 else sums[v, h] + out
        return sums

    outs = (anomalies, means, moved)
    for i, e in enumerate(range(3, cx - 1)):
        sums = with_sides(e, kept, i)
        anomalies_of(dims, factor, spread, e, i, sums, kept, outs)
    partial[...] = nt(moved[...], anomalies[...])
    with_sides(2, late, 0)
    with_sides(cx - 1, late, 1)
    add_sides(dims, kext, first, side, (1, 2, cx - 1, cx), lane)


def rows_kernel(
    dims, factor, mixing, state_in, first_in, partial, late_in, recv_a, recv_b, sides, halo, kext_in, spread,
    state, first, anomalies, means, more, outer, kext, side, first_side, moved, kept,
):
    k, nv, cx, cy = dims
    block = nv * k
    half = cy // LANES
    down_is_a = lax.axis_index("gx") % 2 == 0

    def both(a, b):
        return jnp.where(down_is_a, b, a), jnp.where(down_is_a, a, b)

    for j in range(0, 2 * block, 32):
        up, down = both(recv_a[pl.ds(j, 32), :], recv_b[pl.ds(j, 32), :])
        state[pl.ds((block if j < block else -block) + j, 32), :] = up
        state[pl.ds((cx + 2) * block + j, 32), :] = down
    up, down = both(recv_a[2 * block : 2 * block + 8, :], recv_b[2 * block : 2 * block + 8, :])
    kext[8 : 8 * (cx + 1), :] = kext_in[8 : 8 * (cx + 1), :]
    kext[0:8, :] = up
    kext[8 * (cx + 1) : 8 * (cx + 2), :] = down

    lane = lax.broadcasted_iota(jnp.int32, (1, LANES), 1)
    columns = halo[0:k, :]
    side[...] = edges_of(columns, lane)
    columns = first_columns_of(dims, mixing, columns, halo[k : k + 1, :], sides[0:k, :], lane)
    first_side[...] = edges_of(columns, lane)
    first_step(dims, mixing, kext, state, first, side, (0, cx + 1), lane)

    def late(e, beyond, near, read, write):
        sums = {}
        for v in range(nv):
            for h in range(half):
                lanes = slice(h * LANES, (h + 1) * LANES)
                row = kext[e * 8 + v : e * 8 + v + 1, lanes]
                if near != e:
                    row = row * kext[near * 8 + v : near * 8 + v + 1, lanes]
                row = jnp.broadcast_to(row, (8, LANES))
                for j in range(0, k, 8):
                    out = read[0][pl.ds(read[1] + v * k + j, 8), lanes]
                    out = out + row * state[pl.ds(beyond * block + v * k + j, 8), lanes]
                    write[0][pl.ds(write[1] + v * k + j, 8), lanes] = out
                    sums[v, h] = out if j == 0 else sums[v, h] + out
        return sums

    for i, (e, beyond) in enumerate(((1, 1), (cx, cx + 2))):
        late(e, beyond, e, (first, e * block), (first, e * block))
        second_step(dims, mixing, kext, first, first_side, e, outer, i, lane)
    for i, (e, beyond, near) in enumerate(((2, 1, 1), (cx - 1, cx + 2, cx))):
        sums = late(e, beyond, near, (late_in, i * block), (kept, i * block))
        anomalies_of(dims, factor, spread, e, i, sums, kept, (anomalies, means, moved))
    more[...] = partial[...] + nt(moved[...], anomalies[...])


def corner_kernel(
    dims, factor, outer, partial, halo, corner_a, corner_b, kext, spread,
    anomalies, means, gram, side_up, side_down, moved, kept,
):
    k, nv, cx, cy = dims
    block = nv * k
    half = cy // LANES
    gx = lax.axis_index("gx")
    down_is_a = gx % 2 == 0
    lane = lax.broadcasted_iota(jnp.int32, (1, LANES), 1)
    a = corner_a[0:k, :]
    b = corner_b[0:k, :]
    side_up[...] = edges_of(jnp.where(gx > 0, jnp.where(down_is_a, b, a), 0.0), lane)
    side_down[...] = edges_of(jnp.where(gx < lax.axis_size("gx") - 1, jnp.where(down_is_a, a, b), 0.0), lane)
    kside = edges_of(halo[k : k + 8, :], lane)

    def to_ends(x, e, v):
        return pltpu.roll(x, (LANES - 1 - 2 * (nv * e + v)) & (LANES - 1), 1)

    for i, (e, beyond, source, there) in enumerate(((1, 0, side_up, cx), (cx, cx + 1, side_down, 1))):
        sums = {}
        for v in range(nv):
            kend = to_ends(kside, e, v)[0:1]
            factors = {}
            for h in (0, half - 1):
                lanes = slice(h * LANES, (h + 1) * LANES)
                here = (lane == 0) if h == 0 else (lane == LANES - 1)
                row = kext[e * 8 + v : e * 8 + v + 1, lanes] * (kext[beyond * 8 + v : beyond * 8 + v + 1, lanes] + kend)
                factors[h] = jnp.broadcast_to(jnp.where(here, row, 0.0), (8, LANES))
            for j in range(0, k, 8):
                corner = to_ends(source[pl.ds(j, 8), :], there, v)
                for h in range(half):
                    lanes = slice(h * LANES, (h + 1) * LANES)
                    place = pl.ds(i * block + v * k + j, 8)
                    out = outer[place, lanes]
                    if h in factors:
                        out = out + factors[h] * corner
                    kept[place, lanes] = out
                    sums[v, h] = out if j == 0 else sums[v, h] + out
        anomalies_of(dims, factor, spread, e, i, sums, kept, (anomalies, means, moved))
    got = partial[...] + nt(moved[...], anomalies[...])
    whole = got[:, 0:k] + got[:, k : 2 * k]
    matrix = whole[0:k] + whole[k : 2 * k]
    pull = whole[2 * k : 2 * k + 8] + whole[2 * k + 8 : 2 * k + 16]
    gram[0 : k // 2, :] = jnp.concatenate([matrix[0 : k // 2], matrix[k // 2 :]], axis=1)
    gram[k // 2 : k // 2 + 8, :] = jnp.concatenate([pull, pull], axis=1)


def apply_kernel(dims, gram, inner, inner_means, near, near_means, edge, edge_means, out, buf, sems):
    k, nv, cx, cy = dims
    half = cy // LANES
    row = lax.broadcasted_iota(jnp.int32, (k, k), 0)
    col = lax.broadcasted_iota(jnp.int32, (k, k), 1)
    eye = (row == col).astype(F32)
    both = gram[...]
    matrix = jnp.concatenate([both[0 : k // 2, 0:k], both[0 : k // 2, k : 2 * k]], axis=0) + eye
    pull = both[k // 2 : k // 2 + 8, 0:k]
    pull = jnp.concatenate([pull, pull], axis=0)
    norm = jnp.sqrt(jnp.sum(jnp.sum(matrix * matrix, axis=1, keepdims=True), axis=0, keepdims=True))

    def one(x, y):
        return jnp.dot(x, y, preferred_element_type=F32)

    def dot(a, b):
        a_high, a_low = split_2(a)
        b_high, b_low = split_2(b)
        rows = a.shape[0]
        both = one(jnp.concatenate([a_high, a_low], axis=0), b_high)
        return both[0:rows] + (both[rows:] + one(a_high, b_low))

    root = matrix / norm
    correction = 1.5 * eye - 0.5 * root
    stacked = dot(jnp.concatenate([root, pull], axis=0), correction)
    root = dot(stacked[0:k], correction)
    carried = jnp.concatenate([correction, stacked[k:]], axis=0)
    for i in range(1, NS_ITERS):
        correction = 1.5 * eye - 0.5 * root
        if i < NS_ITERS - 1:
            root = dot(dot(root, correction), correction)
        carried = dot(carried, correction)
    shift = dot(carried[k:], carried[0:k]) / norm
    weights = carried[0:k] / jnp.sqrt(norm) + shift[0:1, :]
    high, low = split_2(weights)
    high_2 = jnp.concatenate([high, high], axis=1)
    copies = []
    for v in range(nv):
        for r in range(cx):
            if 2 <= r < cx - 2:
                anomalies, means, i = inner, inner_means, r - 2
            elif r in (1, cx - 2):
                anomalies, means, i = near, near_means, int(r > 1)
            else:
                anomalies, means, i = edge, edge_means, int(r > 0)
            at = slice((i * nv + v) * cy, (i * nv + v + 1) * cy)
            value = jnp.dot(high_2, anomalies[:, at], preferred_element_type=F32)
            value = value + jnp.dot(low, anomalies[0:k, at], preferred_element_type=F32)
            value = value + means[i * 8 + v : i * 8 + v + 1, :]
            for h in range(half):
                buf[v * half + h, pl.ds(r, k, stride=cx), :] = value[:, h * LANES : (h + 1) * LANES]
        for h in range(half):
            source = buf.at[v * half + h].reshape(k, cx, LANES)
            target = out.at[:, v, :, h * LANES : (h + 1) * LANES]
            copies.append(pltpu.make_async_copy(source, target, sems.at[v, h]))
            copies[-1].start()
    for copy in copies:
        copy.wait()


def local(sizes, ensemble, diffusivity, mixing, obs_cell, obs_var, obs_value, obs_weight):
    k, nv, cx, cy = ensemble.shape
    dims = (k, nv, cx, cy)
    assert k == 64 and nv == 3 and cx == 8 and cy % LANES == 0
    block = nv * k
    rows = nv * cx
    grp, nx, ny = sizes
    count = obs_cell.shape[2]
    factor = 1.0 / math.sqrt((k - 1) * count * nx * ny)
    limits = pltpu.CompilerParams(vmem_limit_bytes=16 << 20)

    def shape(*dims, dtype=F32):
        return jax.ShapeDtypeStruct(dims, dtype)

    small = (diffusivity, mixing) + tuple(a.reshape(1, count) for a in (obs_cell, obs_var, obs_value, obs_weight))
    state, send_a, send_b, sides, side_a, side_b, kappa, mixing, *obs = pl.pallas_call(
        functools.partial(load_kernel, dims),
        name="load",
        in_specs=[pl.BlockSpec(memory_space=pltpu.HBM)] * 7,
        out_specs=[vmem()] * 12,
        out_shape=[
            shape((cx + 4) * block, cy),
            shape(2 * block + 8, cy),
            shape(2 * block + 8, cy),
            shape(k + 8, LANES),
            shape(k + 8, LANES),
            shape(k + 8, LANES),
        ]
        + [shape(*a.shape, dtype=a.dtype) for a in small],
        scratch_shapes=[pltpu.VMEM((cy // LANES, k * rows, LANES), F32), pltpu.SemaphoreType.DMA((4, cy // LANES)), pltpu.SemaphoreType.DMA((6,))],
        compiler_params=limits,
    )(
        *(pltpu.with_memory_space_constraint(a, pltpu.HBM) for a in (ensemble.reshape(k * rows, cy),) + small)
    )

    recv_b = x_swap(1, sizes)(send_b)
    side_a = y_swap(0, sizes)(side_a)
    side_b = y_swap(1, sizes)(side_b)
    recv_a = x_swap(0, sizes)(send_a)

    first, kext, spread, early = pl.pallas_call(
        functools.partial(middle_kernel, dims),
        name="middle",
        in_specs=[smem()] + [vmem()] * 6,
        out_specs=[vmem()] * 4,
        out_shape=[
            shape((cx + 2) * block, cy),
            shape((cx + 2) * 8, cy),
            shape(cx * 8, cy),
            shape((cx - 2) * block, cy),
        ],
        scratch_shapes=[pltpu.VMEM((64, cy), F32)],
        compiler_params=limits,
    )(mixing, state, kappa, *obs)
    side_a, side_b, first = lax.optimization_barrier((side_a, side_b, first))
    halo = side_a + side_b
    corner_b = x_swap(1, sizes)(halo)
    corner_a = x_swap(0, sizes)(halo)

    inner_rows = cx - 4
    first, inner_anomalies, inner_means, partial, late = pl.pallas_call(
        functools.partial(inner_kernel, dims, factor),
        name="inner",
        in_specs=[smem()] + [vmem()] * 6,
        out_specs=[vmem()] * 5,
        input_output_aliases={1: 0},
        out_shape=[
            shape((cx + 2) * block, cy),
            shape(2 * k, inner_rows * nv * cy, dtype=BF16),
            shape(inner_rows * 8, cy),
            shape(2 * k + 16, 2 * k),
            shape(2 * block, cy),
        ],
        scratch_shapes=[
            pltpu.VMEM((k, LANES), F32),
            pltpu.VMEM((k, LANES), F32),
            pltpu.VMEM((2 * k + 16, inner_rows * nv * cy), BF16),
            pltpu.VMEM((4 * block, cy), F32),
        ],
        compiler_params=limits,
    )(mixing, first, early, sides, halo, kext, spread)

    _, _, near_anomalies, near_means, partial, outer, kext = pl.pallas_call(
        functools.partial(rows_kernel, dims, factor),
        name="rows",
        in_specs=[smem()] + [vmem()] * 10,
        out_specs=[vmem()] * 7,
        out_shape=[
            shape((cx + 4) * block, cy),
            shape((cx + 2) * block, cy),
            shape(2 * k, 2 * nv * cy, dtype=BF16),
            shape(2 * 8, cy),
            shape(2 * k + 16, 2 * k),
            shape(2 * block, cy),
            shape((cx + 2) * 8, cy),
        ],
        scratch_shapes=[
            pltpu.VMEM((k, LANES), F32),
            pltpu.VMEM((k, LANES), F32),
            pltpu.VMEM((2 * k + 16, 2 * nv * cy), BF16),
            pltpu.VMEM((2 * block, cy), F32),
        ],
        input_output_aliases={1: 0, 2: 1},
        compiler_params=limits,
    )(mixing, state, first, partial, late, recv_a, recv_b, sides, halo, kext, spread)

    edge_anomalies, edge_means, gram = pl.pallas_call(
        functools.partial(corner_kernel, dims, factor),
        name="corner",
        in_specs=[vmem()] * 7,
        out_specs=[vmem()] * 3,
        out_shape=[
            shape(2 * k, 2 * nv * cy, dtype=BF16),
            shape(2 * 8, cy),
            shape(k // 2 + 8, 2 * k),
        ],
        scratch_shapes=[
            pltpu.VMEM((k, LANES), F32),
            pltpu.VMEM((k, LANES), F32),
            pltpu.VMEM((2 * k + 16, 2 * nv * cy), BF16),
            pltpu.VMEM((2 * block, cy), F32),
        ],
        compiler_params=limits,
    )(outer, partial, halo, corner_a, corner_b, kext, spread)

    gram = all_sum(gram, sizes)

    return pl.pallas_call(
        functools.partial(apply_kernel, dims),
        name="apply",
        in_specs=[vmem()] * 7,
        out_specs=pl.BlockSpec(memory_space=pltpu.HBM),
        out_shape=shape(k, nv, cx, cy),
        scratch_shapes=[
            pltpu.VMEM((nv * (cy // LANES), k * cx, LANES), F32),
            pltpu.SemaphoreType.DMA((nv, cy // LANES)),
        ],
        compiler_params=limits,
    )(gram, inner_anomalies, inner_means, near_anomalies, near_means, edge_anomalies, edge_means)


def solution(mesh):
    sizes = tuple(mesh.shape[a] for a in ("grp", "gx", "gy"))
    return jax.shard_map(
        functools.partial(local, sizes),
        mesh=mesh,
        in_specs=(
            P("grp", None, "gx", "gy"),
            P("grp", "gx", "gy"),
            P(),
            P("gx", "gy", "grp"),
            P("gx", "gy", "grp"),
            P("gx", "gy", "grp"),
            P("gx", "gy", "grp"),
        ),
        out_specs=P("grp", None, "gx", "gy"),
        check_vma=False,
    )
```
